256 devices in a mesh: gx: 4 (over z_hi, core), gy: 16 (over z_lo, y), gz: 4 (over x).
Axes of the slice: x: 4, y: 4, z: 8 (z_hi: 2, z_lo: 4; z = z_hi * 4 + z_lo), core: 2. Of those that a mesh axis runs over, the one named last changes fastest.
Arguments:
- composition: float32 [12, 8, 128, 512], P(None, 'gx', 'gy', 'gz'), may hold values from -3 to 3
- cotangent: float32 [12, 8, 128, 512], P(None, 'gx', 'gy', 'gz'), may hold values from -4 to 4
- weight_one: bfloat16 [64, 12], replicated, may hold values from -1.75 to 1.75
- bias_one: float32 [64], replicated, may hold values from -0.5 to 0.5
- weight_two: bfloat16 [64, 64], replicated, may hold values from -0.75 to 0.75
- bias_two: float32 [64], replicated, may hold values from -0.5 to 0.5
- weight_three: bfloat16 [144, 64], replicated, may hold values from -0.75 to 0.75
- bias_three: float32 [144], replicated, may hold values from -1 to 1
Outputs:
- grad_composition: float32 [12, 8, 128, 512], P(None, 'gx', 'gy', 'gz')
- grad_weight_one: float32 [64, 12], replicated
- grad_bias_one: float32 [64], replicated
- grad_weight_two: float32 [64, 64], replicated
- grad_bias_two: float32 [64], replicated
- grad_weight_three: float32 [144, 64], replicated
- grad_bias_three: float32 [144], replicated
The draws below stay inside these ranges and needn't reach their ends.
All inputs are finite; a program needn't handle non-finite values.
Results may differ from the reference program's by a relative error of at most 0.0077.
Values sent between devices are 32-bit elements; how exact they have to be, the bound alone decides.
No kernel may reach another device: no remote copies, remote signals or barrier semaphores. Data moves between devices by JAX's collectives and lax.ppermute only.
A program may use at most 128 MiB of HBM per device.

```python
import math
import jax
import jax.numpy as jnp
from jax import lax

NC = 12
H1 = 64
H2 = 64
MM = 144
NX = 8
NY = 128
NZ = 512


def block_scale(stream_key, extent, pieces, least, high):
    loudness, own = 1.0, jax.random.fold_in(stream_key, 6)
    for axis_at, shards_of in pieces:
        heights = jnp.exp(jax.random.uniform(jax.random.fold_in(own, axis_at), (shards_of,), jnp.float32, least / len(pieces), high / len(pieces)))
        loudness = loudness * jnp.repeat(heights, extent[axis_at] // shards_of).reshape([-1 if axis == axis_at else 1 for axis in range(len(extent))])
    return loudness


def normal_values(stream_key, dims, width, reach, split=(), kind=jnp.bfloat16):
    entries = width * jax.random.normal(stream_key, dims, jnp.float32)
    if split:
        entries = entries * block_scale(stream_key, dims, split, -0.22, 0.18)
    return jnp.clip(entries, -reach, reach).astype(kind)


def setup_inputs(seed: int = 0) -> dict:
    streams_of = jax.random.split(jax.random.key(seed), 9)
    composition = normal_values(streams_of[0], (NC, NX, NY, NZ), 1.0, 3.0, ((1, 4), (2, 16), (3, 4)), jnp.float32)
    cotangent = normal_values(streams_of[1], (NC, NX, NY, NZ), 1.0, 4.0, ((1, 4), (2, 16), (3, 4)), jnp.float32)
    weight_one = normal_values(streams_of[2], (H1, NC), NC ** -0.5, 1.75)
    bias_one = jnp.clip(jax.random.uniform(streams_of[3], (H1,), jnp.float32, -0.5, 0.5), -0.5, 0.5)
    weight_two = normal_values(streams_of[4], (H2, H1), H1 ** -0.5, 0.75)
    bias_two = jnp.clip(jax.random.uniform(streams_of[5], (H2,), jnp.float32, -0.5, 0.5), -0.5, 0.5)
    weight_three = normal_values(streams_of[6], (MM, H2), H2 ** -0.5, 0.75)
    bias_three = jnp.clip(jax.random.uniform(streams_of[7], (MM,), jnp.float32, -1.0, 1.0), -1.0, 1.0)
    return dict(composition=composition, cotangent=cotangent, weight_one=weight_one, bias_one=bias_one, weight_two=weight_two, bias_two=bias_two, weight_three=weight_three, bias_three=bias_three)


step_size = 0.08
cubic_coef = 0.1
diag_scale = 0.5
off_scale = 0.04

def potential(values):
    return values + cubic_coef * values * values * values

def potential_slope(values):
    return 1.0 + 3.0 * cubic_coef * values * values

def mobility_tables(channels):
    position = jnp.arange(channels * channels, dtype=jnp.int32)
    on_diagonal = position // channels == position % channels
    identity = jnp.where(on_diagonal, 1.0, 0.0).astype(jnp.float32)
    scales = jnp.where(on_diagonal, diag_scale, off_scale).astype(jnp.float32)
    return (identity, scales)

def forward_net(flattened, weights):
    weight_one, bias_one, weight_two, bias_two, weight_three, bias_three = weights
    identity, scales = mobility_tables(flattened.shape[0])
    inputs = flattened.astype(jnp.bfloat16)
    hidden_one = jnp.tanh(jnp.dot(weight_one, inputs, preferred_element_type=jnp.float32) + bias_one[:, None]).astype(jnp.bfloat16)
    hidden_two = jnp.tanh(jnp.dot(weight_two, hidden_one, preferred_element_type=jnp.float32) + bias_two[:, None]).astype(jnp.bfloat16)
    active = jnp.tanh(jnp.dot(weight_three, hidden_two, preferred_element_type=jnp.float32) + bias_three[:, None])
    mobility = identity[:, None] + scales[:, None] * active
    return (mobility, (inputs, hidden_one, hidden_two, active))

def backward_net(grad_mob, stored, weights):
    weight_one, bias_one, weight_two, bias_two, weight_three, bias_three = weights
    inputs, hidden_one, hidden_two, active = stored
    _, scales = mobility_tables(inputs.shape[0])
    pre_three = (grad_mob * scales[:, None] * (1.0 - active * active)).astype(jnp.bfloat16)
    upper_two = hidden_two.astype(jnp.float32)
    pre_two = (jnp.dot(weight_three.T, pre_three, preferred_element_type=jnp.float32) * (1.0 - upper_two * upper_two)).astype(jnp.bfloat16)
    upper_one = hidden_one.astype(jnp.float32)
    pre_one = (jnp.dot(weight_two.T, pre_two, preferred_element_type=jnp.float32) * (1.0 - upper_one * upper_one)).astype(jnp.bfloat16)
    net_grad = jnp.dot(weight_one.T, pre_one, preferred_element_type=jnp.float32)
    grads = (jnp.dot(pre_one, inputs.T, preferred_element_type=jnp.float32), lax.optimization_barrier(jnp.sum(pre_one.astype(jnp.float32), axis=1)), jnp.dot(pre_two, hidden_one.T, preferred_element_type=jnp.float32), lax.optimization_barrier(jnp.sum(pre_two.astype(jnp.float32), axis=1)), jnp.dot(pre_three, hidden_two.T, preferred_element_type=jnp.float32), lax.optimization_barrier(jnp.sum(pre_three.astype(jnp.float32), axis=1)))
    return (net_grad, grads)

def apply_mobility(mobility, vector):
    channels = vector.shape[0]
    matrix = mobility.reshape((channels, channels) + vector.shape[1:])
    return lax.optimization_barrier(jnp.sum(matrix * vector[None], axis=1))

def apply_transpose(mobility, vector):
    channels = vector.shape[0]
    matrix = mobility.reshape((channels, channels) + vector.shape[1:])
    return lax.optimization_barrier(jnp.sum(matrix * vector[:, None], axis=0))

def outer_terms(adjoint, pot_jump):
    channels = adjoint.shape[0]
    return (adjoint[:, None] * pot_jump[None]).reshape((channels * channels,) + adjoint.shape[1:])

def plane_at(array, position):
    return lax.dynamic_index_in_dim(array, position, 1, keepdims=False)

def plane_network(plane, weights):
    channels = plane.shape[0]
    mobility, stored = forward_net(plane.reshape(channels, -1), weights)
    return (mobility.reshape((channels * channels,) + plane.shape[1:]), stored)

def forward_step(current, weights):
    plane_count = current.shape[1]
    potentials = potential(current)
    first_mob, _ = plane_network(current[:, plane_count - 1], weights)
    second_mob, _ = plane_network(current[:, 0], weights)

    def advance(state_carry, position):
        lower_mob, middle_mob = state_carry
        upper_index = (position + 1) % plane_count
        lower_index = (position + plane_count - 1) % plane_count
        upper_mob, _ = plane_network(plane_at(current, upper_index), weights)
        pot_low = plane_at(potentials, lower_index)
        pot_mid = plane_at(potentials, position)
        pot_high = plane_at(potentials, upper_index)
        flux_up = apply_mobility(0.5 * (middle_mob + upper_mob), pot_high - pot_mid)
        flux_down = apply_mobility(0.5 * (lower_mob + middle_mob), pot_mid - pot_low)
        change = flux_up - flux_down
        for spatial in (1, 2):
            shifted_mob = jnp.roll(middle_mob, -1, axis=spatial)
            face_flux = apply_mobility(0.5 * (middle_mob + shifted_mob), jnp.roll(pot_mid, -1, axis=spatial) - pot_mid)
            change = change + (face_flux - jnp.roll(face_flux, 1, axis=spatial))
        return ((middle_mob, upper_mob), plane_at(current, position) + step_size * change)
    _, planes = lax.scan(advance, (first_mob, second_mob), jnp.arange(plane_count, dtype=jnp.int32))
    return jnp.moveaxis(planes, 0, 1)

def backward_step(current, incoming, weights):
    plane_count = current.shape[1]
    potentials = potential(current)
    first_mob, _ = plane_network(current[:, plane_count - 1], weights)
    second_mob, second_stored = plane_network(current[:, 0], weights)
    zero_grads = tuple((jnp.zeros(member.shape, jnp.float32) for member in weights))

    def retreat(state_carry, position):
        lower_mob, middle_mob, middle_stored, totals = state_carry
        upper_index = (position + 1) % plane_count
        lower_index = (position + plane_count - 1) % plane_count
        upper_mob, upper_stored = plane_network(plane_at(current, upper_index), weights)
        pot_low = plane_at(potentials, lower_index)
        pot_mid = plane_at(potentials, position)
        pot_high = plane_at(potentials, upper_index)
        adj_low = plane_at(incoming, lower_index)
        adj_mid = plane_at(incoming, position)
        adj_high = plane_at(incoming, upper_index)
        adjoint_up = step_size * (adj_mid - adj_high)
        adjoint_down = step_size * (adj_low - adj_mid)
        mob_up = 0.5 * (middle_mob + upper_mob)
        mob_down = 0.5 * (lower_mob + middle_mob)
        grad_pot = apply_transpose(mob_down, adjoint_down) - apply_transpose(mob_up, adjoint_up)
        grad_mob = outer_terms(adjoint_down, pot_mid - pot_low) + outer_terms(adjoint_up, pot_high - pot_mid)
        for spatial in (1, 2):
            shifted_mob = jnp.roll(middle_mob, -1, axis=spatial)
            pot_jump = jnp.roll(pot_mid, -1, axis=spatial) - pot_mid
            adjoint = step_size * (adj_mid - jnp.roll(adj_mid, -1, axis=spatial))
            back_flow = apply_transpose(0.5 * (middle_mob + shifted_mob), adjoint)
            grad_pot = grad_pot + (jnp.roll(back_flow, 1, axis=spatial) - back_flow)
            outer_prod = outer_terms(adjoint, pot_jump)
            grad_mob = grad_mob + (jnp.roll(outer_prod, 1, axis=spatial) + outer_prod)
        grad_mob = 0.5 * grad_mob
        net_grad, grads = backward_net(grad_mob.reshape(grad_mob.shape[0], -1), middle_stored, weights)
        plane_state = plane_at(current, position)
        outgoing = adj_mid + grad_pot * potential_slope(plane_state) + net_grad.reshape(plane_state.shape)
        totals = tuple((running + current_grad for running, current_grad in zip(totals, grads)))
        return ((middle_mob, upper_mob, upper_stored, totals), outgoing)
    final_carry, planes = lax.scan(retreat, (first_mob, second_mob, second_stored, zero_grads), jnp.arange(plane_count, dtype=jnp.int32))
    return (jnp.moveaxis(planes, 0, 1), final_carry[3])

def reference(composition, cotangent, weight_one, bias_one, weight_two, bias_two, weight_three, bias_three):
    weights = (weight_one, bias_one, weight_two, bias_two, weight_three, bias_three)
    state_one = forward_step(composition, weights)
    cotangent_one, late_grads = backward_step(state_one, cotangent, weights)
    grad_composition, early_grads = backward_step(composition, cotangent_one, weights)
    factor = 1.0 / (step_size * math.sqrt(NX * NY * NZ))
    scaled = tuple(((late + early) * factor for late, early in zip(late_grads, early_grads)))
    return (grad_composition, scaled[0], scaled[1], scaled[2], scaled[3], scaled[4], scaled[5])
```

```python
import functools
import math

import jax
import jax.numpy as jnp
from jax import lax
from jax.experimental import pallas as pl
from jax.experimental.pallas import tpu as pltpu
from jax.sharding import PartitionSpec as P


AXES = ("gx", "gy", "gz")
GX, GY, GZ = 4, 16, 4
step_size = 0.08
cubic_coef = 0.1
diag_scale = 0.5
off_scale = 0.04

NC, HID, MM = 12, 64, 144
LX, LY, LZ = 2, 8, 128
OWN = LX * LY
GRP = 16
ROWS = NC * GRP
YM, YP, ZT = 32, 34, 36
TILES = 40
CHUNK = 1024
GROWS = 136
F32, BF16 = jnp.float32, jnp.bfloat16
VM = pl.BlockSpec(memory_space=pltpu.VMEM)


def swap(value, partner):
    pairs = []
    for a in range(GX):
        for b in range(GY):
            for c in range(GZ):
                a2, b2, c2 = partner(a, b, c)
                pairs.append(((a * GY + b) * GZ + c, (a2 * GY + b2) * GZ + c2))
    return lax.ppermute(value, AXES, pairs)


def odd_up(i, n):
    return (i + 1) % n if i % 2 else (i - 1) % n


FACE_PARTNERS = (
    lambda a, b, c: (odd_up(a, GX), b, c),
    lambda a, b, c: (a, odd_up(b, GY), c),
    lambda a, b, c: (a, b ^ 1, c),
    lambda a, b, c: (a, b, odd_up(c, GZ)),
    lambda a, b, c: (a, b, c ^ 1),
    lambda a, b, c: (a ^ 1, b, c),
)


def exchange(faces):
    return [swap(face, partner) for face, partner in zip(faces, FACE_PARTNERS)]


def parities():
    return lax.axis_index("gx") % 2, lax.axis_index("gy") % 2, lax.axis_index("gz") % 2


def lanes(shape):
    return lax.broadcasted_iota(jnp.int32, shape, len(shape) - 1)


def tile(index):
    start = index * LZ
    return pl.ds(start if isinstance(start, int) else pl.multiple_of(start, LZ), LZ)


def pack_faces(native, outs, part):
    px, py, pz = parities()
    xf, yb, ya, zb, za, xn = outs
    for ch in range(NC):
        xf[pl.ds(part * 96 + ch * 8, 8), :] = native[pl.ds(pl.multiple_of(ch * OWN + px * LY, 8), 8), :]
        xn[pl.ds(part * 96 + ch * 8, 8), :] = native[pl.ds(pl.multiple_of(ch * OWN + (1 - px) * LY, 8), 8), :]
    first = native[pl.ds(0, 24, stride=8), :]
    last = native[pl.ds(7, 24, stride=8), :]
    ya[pl.ds(part * 24, 24), :] = jnp.where(py == 0, last, first)
    yb[pl.ds(part * 24, 24), :] = jnp.where(py == 0, first, last)
    lane = lanes((NC, LZ))
    low = jnp.zeros((NC, LZ), F32)
    high = jnp.zeros((NC, LZ), F32)
    for t in range(OWN):
        block = native[pl.ds(t, NC, stride=OWN), :]
        low = jnp.where(lane == t, pltpu.roll(block, t, 1), low)
        high = jnp.where(lane == t, pltpu.roll(block, (t + 1) % LZ, 1), high)
    zero = jnp.zeros((GRP - NC, LZ), F32)
    za[pl.ds(part * GRP, NC), :] = jnp.where(pz == 0, high, low)
    zb[pl.ds(part * GRP, NC), :] = jnp.where(pz == 0, low, high)
    za[pl.ds(part * GRP + NC, GRP - NC), :] = zero
    zb[pl.ds(part * GRP + NC, GRP - NC), :] = zero


def load_extended(native, faces, sent_z, part, sent_part, dest):
    px, py, pz = parities()
    xf, yb, ya, zb, za, xn = faces
    dest[...] = jnp.zeros((GRP, TILES * LZ), F32)
    for t in range(OWN):
        dest[0:NC, tile(8 + t)] = native[pl.ds(t, NC, stride=OWN), :]
    for y in range(LY):
        dest[0:NC, tile(24 * px + y)] = xf[pl.ds(part * 96 + y, NC, stride=LY), :]
        dest[0:NC, tile(24 - 24 * px + y)] = xn[pl.ds(part * 96 + y, NC, stride=LY), :]
    for x in range(LX):
        dest[0:NC, tile(YP - 2 * py + x)] = ya[pl.ds(part * 24 + x, NC, stride=LX), :]
        dest[0:NC, tile(YM + 2 * py + x)] = yb[pl.ds(part * 24 + x, NC, stride=LX), :]
    got = slice(part * GRP, part * GRP + GRP)
    own = slice(sent_part * GRP, sent_part * GRP + GRP)
    got_a, got_b = za[got, :], zb[got, :]
    own_b, own_a = sent_z[0][own, :], sent_z[1][own, :]
    even = pz == 0
    lane = lanes((GRP, LZ))
    rim = jnp.where(lane < 16, jnp.where(even, got_b, got_a), 0.0)
    rim = jnp.where((lane >= 16) & (lane < 32), pltpu.roll(jnp.where(even, own_a, own_b), 16, 1), rim)
    rim = jnp.where((lane >= 32) & (lane < 48), pltpu.roll(jnp.where(even, own_b, own_a), 32, 1), rim)
    rim = jnp.where((lane >= 48) & (lane < 64), pltpu.roll(jnp.where(even, got_a, got_b), 48, 1), rim)
    dest[:, tile(ZT)] = rim


def row_tables(by_column):
    row = lax.broadcasted_iota(jnp.int32, (ROWS, MM), 0)
    entry = lax.broadcasted_iota(jnp.int32, (ROWS, MM), 1)
    g, j = row // GRP, row % GRP
    want = j * NC + g if by_column else g * NC + j
    pick = jnp.where((entry == want) & (j < NC), 1.0, 0.0).astype(F32)
    row1 = lax.broadcasted_iota(jnp.int32, (ROWS, 1), 0)
    g1, j1 = row1 // GRP, row1 % GRP
    identity = jnp.where(g1 == j1, 1.0, 0.0).astype(F32)
    scales = jnp.where(g1 == j1, diag_scale, jnp.where(j1 < NC, off_scale, 0.0)).astype(F32)
    return pick, identity, scales


def column(row, size):
    eye = lax.broadcasted_iota(jnp.int32, (size, size), 0) == lax.broadcasted_iota(jnp.int32, (size, size), 1)
    return jnp.sum(jnp.where(eye, row, 0.0), axis=1, keepdims=True)


def dot(a, b, ca=1, cb=0):
    return lax.dot_general(a, b, (((ca,), (cb,)), ((), ())), preferred_element_type=F32)


def network(values, weights, by_column, mob, keep=None):
    w1, b1, w2, b2, w3, b3 = weights
    pick, identity, scales = row_tables(by_column)
    w3p = dot(pick.astype(BF16), w3[...]).astype(BF16)
    bias1, bias2 = column(b1[...], HID), column(b2[...], HID)
    bias3 = jnp.sum(pick * b3[...], axis=1, keepdims=True)
    for at in range(0, TILES * LZ, CHUNK):
        cols = slice(at, at + CHUNK)
        inputs = values[0:NC, cols].astype(BF16)
        one = jnp.tanh(dot(w1[...], inputs) + bias1).astype(BF16)
        two = jnp.tanh(dot(w2[...], one) + bias2).astype(BF16)
        active = jnp.tanh(dot(w3p, two) + bias3)
        mob[:, cols] = identity + scales * active
        if keep is not None and CHUNK <= at < 3 * CHUNK:
            own = slice(at - CHUNK, at)
            rhs1, rhs2, rhs3, slope = keep
            zero = jnp.zeros((HID, CHUNK), BF16)
            rhs1[0:GRP, own] = values[:, cols].astype(BF16)
            rhs1[GRP:, own] = jnp.zeros((2 * HID - GRP, CHUNK), BF16)
            rhs2[0:HID, own] = one
            rhs2[HID:, own] = zero
            rhs3[0:HID, own] = two
            rhs3[HID:, own] = zero
            slope[:, own] = (0.5 * scales) * (1.0 - active * active)
    return w3p


def potential(v):
    return v + cubic_coef * v * v * v


def flow_of(lower, upper, weight):
    total = None
    for k in range(NC):
        term = (lower(k) + upper(k)) * weight[k : k + 1, :]
        total = term if total is None else total + term
    return total


def mob_rows(mob, index):
    return lambda k: mob[GRP * k : GRP * k + GRP, tile(index)]


def rolled_rows(mob, index, shift):
    return lambda k: pltpu.roll(mob[GRP * k : GRP * k + GRP, tile(index)], shift, 1)


def y_face(j):
    x, k = j // 9, j % 9
    low = jnp.where(k == 0, YM + x, (x + 1) * 8 + k - 1)
    high = jnp.where(k == 8, YP + x, (x + 1) * 8 + k)
    return low, high


def face_flows(mob, weight_of, weight_roll, fx, fy, fz):
    def x_body(k, carry):
        fx[:, tile(k)] = flow_of(mob_rows(mob, k), mob_rows(mob, k + 8), weight_of(k, k + 8))
        return carry

    def y_body(j, carry):
        low, high = y_face(j)
        fy[:, tile(j)] = flow_of(mob_rows(mob, low), mob_rows(mob, high), weight_of(low, high))
        return carry

    def z_body(t, carry):
        fz[:, tile(t)] = flow_of(mob_rows(mob, t + 8), rolled_rows(mob, t + 8, LZ - 1), weight_roll(t + 8, LZ - 1))
        return carry

    lax.fori_loop(0, 24, x_body, 0)
    lax.fori_loop(0, 18, y_body, 0)
    lax.fori_loop(0, OWN, z_body, 0)
    fz[:, tile(OWN)] = flow_of(mob_rows(mob, ZT), rolled_rows(mob, ZT, 96), weight_roll(ZT, 96))


def z_pair(inner, rim, t, lane):
    up = jnp.where(lane == LZ - 1, pltpu.roll(rim, LZ - 1 - 16 - t, 1), inner)
    low = jnp.where(lane == 0, pltpu.roll(rim, (LZ - t) % LZ, 1), pltpu.roll(inner, 1, 1))
    return up, low


def pack_kernel(comp, *outs):
    pack_faces(comp, outs, 0)


def forward_kernel(comp, cot, *refs):
    faces, sent_z, weights = refs[0:6], refs[6:8], refs[8:14]
    state, outs = refs[14], refs[15:21]
    values, pots, mob, fx, fy, fz = refs[21:]
    load_extended(comp, faces, sent_z, 0, 0, values)
    pots[...] = potential(values[...])
    network(values, weights, True, mob)

    def weight_of(low, high):
        return 0.5 * (pots[:, tile(high)] - pots[:, tile(low)])

    def weight_roll(index, shift):
        here = pots[:, tile(index)]
        return 0.5 * (pltpu.roll(here, shift, 1) - here)

    face_flows(mob, weight_of, weight_roll, fx, fy, fz)
    lane = lanes((GRP, LZ))
    rim = fz[:, tile(OWN)]
    for t in range(OWN):
        at, y = t + 8, t // LY * 9 + t % LY
        up, low = z_pair(fz[:, tile(t)], rim, t, lane)
        change = fx[:, tile(at)] - fx[:, tile(at - 8)] + (fy[:, tile(y + 1)] - fy[:, tile(y)]) + (up - low)
        moved = values[:, tile(at)] + step_size * change
        state[pl.ds(t, NC, stride=OWN), :] = moved[0:NC, :]
    pack_faces(state, outs, 0)
    pack_faces(cot, outs, 1)


def backward_kernel(first, refs):
    refs = list(refs)
    current, incoming = refs[0:2]
    if first:
        faces, sent_z, weights = refs[2:8], refs[8:10], refs[10:16]
        v_faces = u_faces = faces
        v_sent = u_sent = sent_z
        v_part, u_part = 0, 1
        outgoing, outs, grads = refs[16], refs[17:23], refs[23]
        scratch = refs[24:]
        late = None
    else:
        v_faces, v_sent, u_faces, u_sent, weights, late = refs[2:8], refs[8:10], refs[10:16], refs[16:18], refs[18:24], refs[24]
        v_part, u_part = 0, 0
        outgoing, grads = refs[25], refs[26]
        outs = None
        scratch = refs[27:]
    values, pots, adj, mob, fx, fy, fz, rhs1, rhs2, rhs3, slope, pre3, gpot = scratch
    load_extended(current, v_faces, v_sent, v_part, v_part, values)
    load_extended(incoming, u_faces, u_sent, u_part, u_part, adj)
    pots[...] = potential(values[...])
    w1, w2 = weights[0], weights[2]
    w3p = network(values, weights, False, mob, (rhs1, rhs2, rhs3, slope))

    def jump_of(low, high):
        return pots[:, tile(high)] - pots[:, tile(low)]

    def adj_of(low, high):
        return step_size * (adj[:, tile(low)] - adj[:, tile(high)])

    def jump_roll(index, shift):
        here = pots[:, tile(index)]
        return pltpu.roll(here, shift, 1) - here

    def adj_roll(index, shift):
        here = adj[:, tile(index)]
        return step_size * (here - pltpu.roll(here, shift, 1))

    face_flows(mob, lambda l, h: 0.5 * adj_of(l, h), lambda i, s: 0.5 * adj_roll(i, s), fx, fy, fz)
    lane = lanes((GRP, LZ))
    rim_jump, rim_adj = jump_roll(ZT, 96), adj_roll(ZT, 96)

    def cell_body(t, carry):
        at = t + 8
        x, y = t // LY, t % LY
        fy_at = x * 9 + y
        rim = fz[:, tile(OWN)]
        up, low = z_pair(fz[:, tile(t)], rim, t, lane)
        y_low, y_high = y_face(fy_at)
        y_low2, y_high2 = y_face(fy_at + 1)
        gpot[:, tile(t)] = fx[:, tile(at - 8)] - fx[:, tile(at)] + (fy[:, tile(fy_at)] - fy[:, tile(fy_at + 1)]) + (low - up)
        ju, jl = z_pair(jump_roll(at, LZ - 1), rim_jump, t, lane)
        au, al = z_pair(adj_roll(at, LZ - 1), rim_adj, t, lane)
        jumps = (jump_of(at - 8, at), jump_of(at, at + 8), jump_of(y_low, y_high), jump_of(y_low2, y_high2), jl, ju)
        adjs = (adj_of(at - 8, at), adj_of(at, at + 8), adj_of(y_low, y_high), adj_of(y_low2, y_high2), al, au)
        for k in range(NC):
            total = None
            for a, j in zip(adjs, jumps):
                term = a[k : k + 1, :] * j
                total = term if total is None else total + term
            rows = slice(GRP * k, GRP * k + GRP)
            pre3[rows, tile(t)] = (total * slope[rows, tile(t)]).astype(BF16)
        return carry

    lax.fori_loop(0, OWN, cell_body, 0)
    g1 = g2 = g3 = s2 = s3 = None
    for at in range(0, OWN * LZ, CHUNK):
        own = slice(at, at + CHUNK)
        three = pre3[:, own]
        h2 = rhs3[0:HID, own].astype(F32)
        two = (dot(w3p, three, 0, 0) * (1.0 - h2 * h2)).astype(BF16)
        h1 = rhs2[0:HID, own].astype(F32)
        one = (dot(w2[...], two, 0, 0) * (1.0 - h1 * h1)).astype(BF16)
        net = dot(w1[...], one, 0, 0)
        parts = (
            dot(one, rhs1[:, own], 1, 1),
            dot(two, rhs2[:, own], 1, 1),
            dot(three, rhs3[:, own], 1, 1),
            jnp.sum(one.astype(F32), axis=1, keepdims=True),
            jnp.sum(two.astype(F32), axis=1, keepdims=True),
            jnp.sum(three.astype(F32), axis=1, keepdims=True),
        )
        if g1 is None:
            g1, g2, g3, s1, s2, s3 = parts
        else:
            g1, g2, g3, s1, s2, s3 = (old + new for old, new in zip((g1, g2, g3, s1, s2, s3), parts))
        for k in range(CHUNK // LZ):
            t = at // LZ + k
            v = values[0:NC, tile(t + 8)]
            out = (
                adj[0:NC, tile(t + 8)]
                + gpot[0:NC, tile(t)] * (1.0 + 3.0 * cubic_coef * v * v)
                + net[:, k * LZ : (k + 1) * LZ]
            )
            outgoing[pl.ds(t, NC, stride=OWN), :] = out

    def put(rows, block):
        grads[rows, :] = block if late is None else block + late[rows, :]

    for k in range(6):
        put(pl.ds(12 * k, 12), g3[GRP * k : GRP * k + NC] + pltpu.roll(g3[GRP * (k + 6) : GRP * (k + 6) + NC], HID, 1))
    put(pl.ds(72, 32), g2[0:32] + pltpu.roll(g2[32:64], HID, 1))
    lane32 = lanes((32, LZ))
    misc = g1[0:32] + pltpu.roll(g1[32:64], 16, 1)
    for k, col in enumerate((s1[0:32], s2[0:32], s1[32:64], s2[32:64])):
        misc = jnp.where(lane32 == (12, 13, 28, 29)[k], col, misc)
    for k in range(6):
        misc = jnp.where(lane32 == 32 + k, s3[32 * k : 32 * k + 32], misc)
    put(pl.ds(104, 32), misc)
    if outs is not None:
        pack_faces(outgoing, outs, 0)


def finish_kernel(factor, grads, ow1, ob1, ow2, ob2, ow3, ob3):
    for k in range(6):
        block = grads[pl.ds(12 * k, 12), :] * factor
        ow3[pl.ds(12 * k, 12), :] = block[:, 0:HID]
        ow3[pl.ds(72 + 12 * k, 12), :] = pltpu.roll(block, HID, 1)[:, 0:HID]
    block = grads[pl.ds(72, 32), :] * factor
    ow2[0:32, :] = block[:, 0:HID]
    ow2[32:64, :] = pltpu.roll(block, HID, 1)[:, 0:HID]
    misc = grads[pl.ds(104, 32), :] * factor
    ow1[0:32, :] = misc[:, 0:NC]
    ow1[32:64, :] = pltpu.roll(misc, LZ - 16, 1)[:, 0:NC]
    row = lax.broadcasted_iota(jnp.int32, (32, HID), 0)
    lane = lanes((32, HID))

    def as_row(first, second):
        low = jnp.where(lane == row, misc[:, first : first + 1], 0.0)
        high = jnp.where(lane == row + 32, misc[:, second : second + 1], 0.0)
        return jnp.sum(low + high, axis=0, keepdims=True)

    ob1[...] = as_row(12, 28)
    ob2[...] = as_row(13, 29)
    row = lax.broadcasted_iota(jnp.int32, (32, MM), 0)
    lane = lanes((32, MM))
    total = jnp.zeros((32, MM), F32)
    for k in range(6):
        padded = row + 32 * k
        target = padded // GRP * NC + padded % GRP
        total = total + jnp.where((lane == target) & (padded % GRP < NC), misc[:, 32 + k : 33 + k], 0.0)
    ob3[...] = jnp.sum(total, axis=0, keepdims=True)


def shape(*dims):
    return jax.ShapeDtypeStruct(dims, F32)


def face_shapes(parts):
    x, y, z = shape(96 * parts, LZ), shape(24 * parts, LZ), shape(GRP * parts, LZ)
    return (x, y, y, z, z, x)


def call(kernel, outs, args, scratch=()):
    return pl.pallas_call(
        kernel,
        out_shape=outs,
        in_specs=[VM] * len(args),
        out_specs=tuple(VM for _ in outs),
        scratch_shapes=list(scratch),
        compiler_params=pltpu.CompilerParams(vmem_limit_bytes=48 << 20),
    )(*args)


def wide(tiles, rows=GRP, kind=F32):
    return pltpu.VMEM((rows, tiles * LZ), kind)


BACK_SCRATCH = (
    wide(TILES), wide(TILES), wide(TILES), wide(TILES, ROWS), wide(24), wide(18), wide(OWN + 1),
    wide(OWN, 2 * HID, BF16), wide(OWN, 2 * HID, BF16), wide(OWN, 2 * HID, BF16),
    wide(OWN, ROWS), wide(OWN, ROWS, BF16), wide(OWN),
)


def group_sum(value, partners):
    received = [swap(value, partner) for partner in partners]
    for other in received:
        value = value + other
    return value


def total_over_devices(value):
    half = value.shape[0] // 2
    core = lax.axis_index("gx") % 2
    keep = lax.dynamic_slice_in_dim(value, core * half, half, 0)
    give = lax.dynamic_slice_in_dim(value, (1 - core) * half, half, 0)
    value = keep + swap(give, lambda a, b, c: (a ^ 1, b, c))
    value = group_sum(value, [lambda a, b, c, k=k: (a, b, c ^ k) for k in (2, 1, 3)])
    value = group_sum(value, [lambda a, b, c, k=k: (a, b ^ k, c) for k in (2, 1, 3)])
    value = group_sum(value, [lambda a, b, c, k=k: (a, b ^ (4 * k), c) for k in (3, 2, 1)])
    value = value + swap(value, lambda a, b, c: (a ^ 2, b, c))
    other = swap(value, lambda a, b, c: (a ^ 1, b, c))
    return jnp.concatenate([jnp.where(core == 0, value, other), jnp.where(core == 0, other, value)], 0)


def shards(composition, cotangent, w1, b1, w2, b2, w3, b3):
    block = composition.shape
    comp = composition.reshape(NC * OWN, LZ)
    cot = cotangent.reshape(NC * OWN, LZ)
    weights = (w1, b1.reshape(1, HID), w2, b2.reshape(1, HID), w3, b3.reshape(1, MM))

    sent = call(pack_kernel, face_shapes(1), (comp,))
    comp_faces = exchange(sent)
    comp_z = sent[3:5]
    moved, *sent = call(
        forward_kernel,
        (shape(NC * OWN, LZ),) + face_shapes(2),
        (comp, cot, *comp_faces, *comp_z, *weights),
        (wide(TILES), wide(TILES), wide(TILES, ROWS), wide(24), wide(18), wide(OWN + 1)),
    )
    got = exchange(sent)
    back, *rest = call(
        lambda *refs: backward_kernel(True, refs),
        (shape(NC * OWN, LZ),) + face_shapes(1) + (shape(GROWS, LZ),),
        (moved, cot, *got, *sent[3:5], *weights),
        BACK_SCRATCH,
    )
    sent, late = rest[:6], rest[6]
    got = exchange(sent)
    final, grads = call(
        lambda *refs: backward_kernel(False, refs),
        (shape(NC * OWN, LZ), shape(GROWS, LZ)),
        (comp, back, *comp_faces, *comp_z, *got, *sent[3:5], *weights, late),
        BACK_SCRATCH,
    )
    grads = total_over_devices(grads)
    cells = OWN * LZ * GX * GY * GZ
    factor = 1.0 / (step_size * math.sqrt(cells))
    ow1, ob1, ow2, ob2, ow3, ob3 = call(
        functools.partial(finish_kernel, factor),
        (shape(HID, NC), shape(1, HID), shape(HID, HID), shape(1, HID), shape(MM, HID), shape(1, MM)),
        (grads,),
    )
    return (final.reshape(block), ow1, ob1.reshape(HID), ow2, ob2.reshape(HID), ow3, ob3.reshape(MM))


def solution(mesh):
    in_specs = (P(None, "gx", "gy", "gz"), P(None, "gx", "gy", "gz"), P(), P(), P(), P(), P(), P())
    out_specs = (P(None, "gx", "gy", "gz"), P(), P(), P(), P(), P(), P())
    return jax.shard_map(shards, mesh=mesh, in_specs=in_specs, out_specs=out_specs, check_vma=False)
```

```python
import functools
import math

import jax
import jax.numpy as jnp
from jax import lax
from jax.experimental import pallas as pl
from jax.experimental.pallas import tpu as pltpu
from jax.sharding import PartitionSpec as P


AXES = ("gx", "gy", "gz")
GX, GY, GZ = 4, 16, 4
step_size = 0.08
cubic_coef = 0.1
diag_scale = 0.5
off_scale = 0.04

NC, HID, MM = 12, 64, 144
LX, LY, LZ = 2, 8, 128
OWN = LX * LY
GRP = 16
ROWS = NC * GRP
YM, YP, ZT = 32, 34, 36
TILES = 37
CHUNK = 1024
HALO = ((0, 8), (24, 32), (32, 37))
GROWS = 128
F32, BF16 = jnp.float32, jnp.bfloat16
VM = pl.BlockSpec(memory_space=pltpu.VMEM)


def swap(value, partner):
    pairs = []
    for a in range(GX):
        for b in range(GY):
            for c in range(GZ):
                a2, b2, c2 = partner(a, b, c)
                pairs.append(((a * GY + b) * GZ + c, (a2 * GY + b2) * GZ + c2))
    return lax.ppermute(value, AXES, pairs)


def odd_up(i, n):
    return (i + 1) % n if i % 2 else (i - 1) % n


FACE_PARTNERS = (
    lambda a, b, c: (odd_up(a, GX), b, c),
    lambda a, b, c: (a, odd_up(b, GY), c),
    lambda a, b, c: (a, b ^ 1, c),
    lambda a, b, c: (a, b, odd_up(c, GZ)),
    lambda a, b, c: (a, b, c ^ 1),
    lambda a, b, c: (a ^ 1, b, c),
)


def exchange(faces):
    return [swap(face, partner) for face, partner in zip(faces, FACE_PARTNERS)]


def parities():
    return lax.axis_index("gx") % 2, lax.axis_index("gy") % 2, lax.axis_index("gz") % 2


def lanes(shape):
    return lax.broadcasted_iota(jnp.int32, shape, len(shape) - 1)


def tile(index):
    start = index * LZ
    return pl.ds(start if isinstance(start, int) else pl.multiple_of(start, LZ), LZ)


def pack_faces(native, outs, part):
    px, py, pz = parities()
    xf, yb, ya, zb, za, xn = outs
    for ch in range(NC):
        xf[pl.ds(part * 96 + ch * 8, 8), :] = native[pl.ds(pl.multiple_of(ch * OWN + px * LY, 8), 8), :]
        xn[pl.ds(part * 96 + ch * 8, 8), :] = native[pl.ds(pl.multiple_of(ch * OWN + (1 - px) * LY, 8), 8), :]
    first = native[pl.ds(0, 24, stride=8), :]
    last = native[pl.ds(7, 24, stride=8), :]
    ya[pl.ds(part * 24, 24), :] = jnp.where(py == 0, last, first)
    yb[pl.ds(part * 24, 24), :] = jnp.where(py == 0, first, last)
    lane = lanes((NC, LZ))
    low = jnp.zeros((NC, LZ), F32)
    high = jnp.zeros((NC, LZ), F32)
    for t in range(OWN):
        block = native[pl.ds(t, NC, stride=OWN), :]
        low = jnp.where(lane == t, pltpu.roll(block, t, 1), low)
        high = jnp.where(lane == t, pltpu.roll(block, (t + 1) % LZ, 1), high)
    zero = jnp.zeros((GRP - NC, LZ), F32)
    za[pl.ds(part * GRP, NC), :] = jnp.where(pz == 0, high, low)
    zb[pl.ds(part * GRP, NC), :] = jnp.where(pz == 0, low, high)
    za[pl.ds(part * GRP + NC, GRP - NC), :] = zero
    zb[pl.ds(part * GRP + NC, GRP - NC), :] = zero


def load_own(native, dest):
    dest[...] = jnp.zeros((GRP, TILES * LZ), F32)
    for t in range(OWN):
        dest[0:NC, tile(8 + t)] = native[pl.ds(t, NC, stride=OWN), :]


def load_extended(native, faces, sent_z, part, sent_part, dest):
    px, py, pz = parities()
    xf, yb, ya, zb, za, xn = faces
    load_own(native, dest)
    for y in range(LY):
        dest[0:NC, tile(24 * px + y)] = xf[pl.ds(part * 96 + y, NC, stride=LY), :]
        dest[0:NC, tile(24 - 24 * px + y)] = xn[pl.ds(part * 96 + y, NC, stride=LY), :]
    for x in range(LX):
        dest[0:NC, tile(YP - 2 * py + x)] = ya[pl.ds(part * 24 + x, NC, stride=LX), :]
        dest[0:NC, tile(YM + 2 * py + x)] = yb[pl.ds(part * 24 + x, NC, stride=LX), :]
    got = slice(part * GRP, part * GRP + GRP)
    own = slice(sent_part * GRP, sent_part * GRP + GRP)
    got_a, got_b = za[got, :], zb[got, :]
    own_b, own_a = sent_z[0][own, :], sent_z[1][own, :]
    even = pz == 0
    lane = lanes((GRP, LZ))
    rim = jnp.where(lane < 16, jnp.where(even, got_b, got_a), 0.0)
    rim = jnp.where((lane >= 16) & (lane < 32), pltpu.roll(jnp.where(even, own_a, own_b), 16, 1), rim)
    rim = jnp.where((lane >= 32) & (lane < 48), pltpu.roll(jnp.where(even, own_b, own_a), 32, 1), rim)
    rim = jnp.where((lane >= 48) & (lane < 64), pltpu.roll(jnp.where(even, got_a, got_b), 48, 1), rim)
    dest[:, tile(ZT)] = rim


def row_tables(by_column):
    row = lax.broadcasted_iota(jnp.int32, (ROWS, MM), 0)
    entry = lax.broadcasted_iota(jnp.int32, (ROWS, MM), 1)
    g, j = row // GRP, row % GRP
    want = j * NC + g if by_column else g * NC + j
    pick = jnp.where((entry == want) & (j < NC), 1.0, 0.0).astype(F32)
    row1 = lax.broadcasted_iota(jnp.int32, (ROWS, 1), 0)
    g1, j1 = row1 // GRP, row1 % GRP
    identity = jnp.where(g1 == j1, 1.0, 0.0).astype(F32)
    scales = jnp.where(g1 == j1, diag_scale, jnp.where(j1 < NC, off_scale, 0.0)).astype(F32)
    return pick, identity, scales


def eye(size, kind=F32):
    same = lax.broadcasted_iota(jnp.int32, (size, size), 0) == lax.broadcasted_iota(jnp.int32, (size, size), 1)
    return jnp.where(same, 1.0, 0.0).astype(kind)


def dot(a, b, ca=1, cb=0, precision=None):
    return lax.dot_general(a, b, (((ca,), (cb,)), ((), ())), preferred_element_type=F32, precision=precision)


def prepare(w1t, b1, w2, b2, w3t, b3, outs):
    w1p, w2t, w3c, w3r, w3rt, cols = outs
    w1p[...] = dot(w1t[...], eye(NC, BF16), 0, 0).astype(BF16)
    w2t[...] = dot(w2[...], eye(HID, BF16), 0, 0).astype(BF16)
    pick_c, _, _ = row_tables(True)
    pick_r, _, _ = row_tables(False)
    w3c[...] = dot(pick_c.astype(BF16), w3t[...], 1, 1).astype(BF16)
    w3r[...] = dot(pick_r.astype(BF16), w3t[...], 1, 1).astype(BF16)
    w3rt[...] = dot(w3t[...], pick_r.astype(BF16), 1, 1).astype(BF16)
    cols[:, 0:1] = jnp.sum(pick_c * b3[...], axis=1, keepdims=True)
    cols[:, 1:2] = jnp.sum(pick_r * b3[...], axis=1, keepdims=True)
    cols[0:HID, 2:3] = jnp.sum(eye(HID) * b1[...], axis=1, keepdims=True)
    cols[0:HID, 3:4] = jnp.sum(eye(HID) * b2[...], axis=1, keepdims=True)


def network(values, spans, prep, by_column, mob, keep=None):
    w1p, w2, w3p, cols = prep
    row1 = lax.broadcasted_iota(jnp.int32, (ROWS, 1), 0)
    g1, j1 = row1 // GRP, row1 % GRP
    identity = jnp.where(g1 == j1, 1.0, 0.0).astype(F32)
    scales = jnp.where(g1 == j1, diag_scale, jnp.where(j1 < NC, off_scale, 0.0)).astype(F32)
    bias1, bias2 = cols[0:HID, 2:3], cols[0:HID, 3:4]
    bias3 = cols[:, 0:1] if by_column else cols[:, 1:2]
    for start, stop in spans:
        cols_at = slice(start * LZ, stop * LZ)
        inputs = values[0:NC, cols_at].astype(BF16)
        one = jnp.tanh(dot(w1p[...], inputs) + bias1).astype(BF16)
        two = jnp.tanh(dot(w2[...], one) + bias2).astype(BF16)
        active = jnp.tanh(dot(w3p[...], two) + bias3)
        mob[:, cols_at] = identity + scales * active
        if keep is not None and 8 <= start < 24:
            own = slice((start - 8) * LZ, (stop - 8) * LZ)
            rhs1, rhs2, rhs3, slope = keep
            width = (stop - start) * LZ
            rhs1[0:GRP, own] = values[:, cols_at].astype(BF16)
            rhs1[GRP:, own] = jnp.zeros((2 * HID - GRP, width), BF16)
            rhs2[0:HID, own] = one
            rhs2[HID:, own] = jnp.zeros((HID, width), BF16)
            rhs3[:, own] = two
            slope[:, own] = (0.5 * scales) * (1.0 - active * active)


OWN_SPANS = ((8, 16), (16, 24))


def potential(v):
    return v + cubic_coef * v * v * v


def flow_of(lower, upper, weight):
    total = None
    for k in range(NC):
        term = (lower(k) + upper(k)) * weight[k : k + 1, :]
        total = term if total is None else total + term
    return total


def mob_rows(mob, index):
    return lambda k: mob[GRP * k : GRP * k + GRP, tile(index)]


def rolled_rows(mob, index, shift):
    return lambda k: pltpu.roll(mob[GRP * k : GRP * k + GRP, tile(index)], shift, 1)


def y_face(j):
    x, k = j // 9, j % 9
    low = jnp.where(k == 0, YM + x, (x + 1) * 8 + k - 1)
    high = jnp.where(k == 8, YP + x, (x + 1) * 8 + k)
    return low, high


def face_flows(mob, weight_of, weight_roll, fx, fy, fz):
    def x_body(plane, carry):
        for y in range(LY):
            k = plane * 8 + y
            fx[:, tile(k)] = flow_of(mob_rows(mob, k), mob_rows(mob, k + 8), weight_of(k, k + 8))
        return carry

    def y_body(x, carry):
        for k in range(LY + 1):
            low = YM + x if k == 0 else x * 8 + (7 + k)
            high = YP + x if k == LY else x * 8 + (8 + k)
            fy[:, tile(x * 9 + k)] = flow_of(mob_rows(mob, low), mob_rows(mob, high), weight_of(low, high))
        return carry

    def z_body(x, carry):
        for y in range(LY):
            t = x * 8 + y
            fz[:, tile(t)] = flow_of(mob_rows(mob, t + 8), rolled_rows(mob, t + 8, LZ - 1), weight_roll(t + 8, LZ - 1))
        return carry

    lax.fori_loop(0, 3, x_body, 0)
    lax.fori_loop(0, 2, y_body, 0)
    lax.fori_loop(0, 2, z_body, 0)
    fz[:, tile(OWN)] = flow_of(mob_rows(mob, ZT), rolled_rows(mob, ZT, 96), weight_roll(ZT, 96))


def z_pair(inner, rim, t, lane):
    up = jnp.where(lane == LZ - 1, pltpu.roll(rim, LZ - 1 - 16 - t, 1), inner)
    low = jnp.where(lane == 0, pltpu.roll(rim, (LZ - t) % LZ, 1), pltpu.roll(inner, 1, 1))
    return up, low


def pack_kernel(comp, *outs):
    pack_faces(comp, outs, 0)


def prepare_kernel(comp, cot, w1t, b1, w2, b2, w3t, b3, *refs):
    outs, mob, faces, values = refs[0:6], refs[6], refs[7:13], refs[13]
    prepare(w1t, b1, w2, b2, w3t, b3, outs)
    load_own(comp, values)
    network(values, OWN_SPANS, (outs[0], w2, outs[2], outs[5]), True, mob)
    pack_faces(cot, faces, 0)


def forward_kernel(comp, *refs):
    faces, sent_z, cot_faces, prep = refs[0:6], refs[6:8], refs[8:14], refs[14:18]
    state, outs, values, mob = refs[19], refs[20:26], refs[26], refs[27]
    pots, fx, fy, fz = refs[28:]
    load_extended(comp, faces, sent_z, 0, 0, values)
    pots[...] = potential(values[...])
    network(values, HALO, prep, True, mob)

    def weight_of(low, high):
        return 0.5 * (pots[:, tile(high)] - pots[:, tile(low)])

    def weight_roll(index, shift):
        here = pots[:, tile(index)]
        return 0.5 * (pltpu.roll(here, shift, 1) - here)

    face_flows(mob, weight_of, weight_roll, fx, fy, fz)
    lane = lanes((GRP, LZ))
    rim = fz[:, tile(OWN)]
    for t in range(OWN):
        at, y = t + 8, t // LY * 9 + t % LY
        up, low = z_pair(fz[:, tile(t)], rim, t, lane)
        change = fx[:, tile(at)] - fx[:, tile(at - 8)] + (fy[:, tile(y + 1)] - fy[:, tile(y)]) + (up - low)
        moved = values[:, tile(at)] + step_size * change
        state[pl.ds(t, NC, stride=OWN), :] = moved[0:NC, :]
    pack_faces(state, outs, 0)
    for out, face in zip(outs, cot_faces):
        out[pl.ds(face.shape[0], face.shape[0]), :] = face[...]


def own_network_kernel(state, w1p, w2, w3r, cols, mob, rhs1, rhs2, rhs3, slope, values):
    load_own(state, values)
    network(values, OWN_SPANS, (w1p, w2, w3r, cols), False, mob, (rhs1, rhs2, rhs3, slope))


def full_network_kernel(values, w1p, w2, w3r, cols, mob, rhs1, rhs2, rhs3, slope):
    network(values, OWN_SPANS + HALO, (w1p, w2, w3r, cols), False, mob, (rhs1, rhs2, rhs3, slope))


def reverse_step(values, pots, adj, mob, keep, weights, flows, gpot, outgoing, pres):
    w1t, w2t, w3rt = weights
    rhs2, rhs3, slope = keep
    one_out, two_out, pre3 = pres
    fx, fy, fz = flows

    def jump_of(low, high):
        return pots[:, tile(high)] - pots[:, tile(low)]

    def adj_of(low, high):
        return step_size * (adj[:, tile(low)] - adj[:, tile(high)])

    def jump_roll(index, shift):
        here = pots[:, tile(index)]
        return pltpu.roll(here, shift, 1) - here

    def adj_roll(index, shift):
        here = adj[:, tile(index)]
        return step_size * (here - pltpu.roll(here, shift, 1))

    face_flows(mob, lambda l, h: 0.5 * adj_of(l, h), lambda i, s: 0.5 * adj_roll(i, s), fx, fy, fz)
    lane = lanes((GRP, LZ))
    rim_jump, rim_adj = jump_roll(ZT, 96), adj_roll(ZT, 96)

    def cell_body(t, carry):
        at = t + 8
        x, y = t // LY, t % LY
        fy_at = x * 9 + y
        rim = fz[:, tile(OWN)]
        up, low = z_pair(fz[:, tile(t)], rim, t, lane)
        y_low, y_high = y_face(fy_at)
        y_low2, y_high2 = y_face(fy_at + 1)
        gpot[:, tile(t)] = fx[:, tile(at - 8)] - fx[:, tile(at)] + (fy[:, tile(fy_at)] - fy[:, tile(fy_at + 1)]) + (low - up)
        ju, jl = z_pair(jump_roll(at, LZ - 1), rim_jump, t, lane)
        au, al = z_pair(adj_roll(at, LZ - 1), rim_adj, t, lane)
        jumps = (jump_of(at - 8, at), jump_of(at, at + 8), jump_of(y_low, y_high), jump_of(y_low2, y_high2), jl, ju)
        adjs = (adj_of(at - 8, at), adj_of(at, at + 8), adj_of(y_low, y_high), adj_of(y_low2, y_high2), al, au)
        for k in range(NC):
            total = None
            for a, j in zip(adjs, jumps):
                term = a[k : k + 1, :] * j
                total = term if total is None else total + term
            rows = slice(GRP * k, GRP * k + GRP)
            pre3[rows, tile(t)] = (total * slope[rows, tile(t)]).astype(BF16)
        return carry

    lax.fori_loop(0, OWN, cell_body, 0)
    for at in range(0, OWN * LZ, CHUNK):
        own = slice(at, at + CHUNK)
        h2 = rhs3[:, own].astype(F32)
        two = (dot(w3rt[...], pre3[:, own]) * (1.0 - h2 * h2)).astype(BF16)
        h1 = rhs2[0:HID, own].astype(F32)
        one = (dot(w2t[...], two) * (1.0 - h1 * h1)).astype(BF16)
        net = dot(w1t[...], one)
        one_out[:, own] = one
        two_out[:, own] = two
        for k in range(CHUNK // LZ):
            t = at // LZ + k
            v = values[0:NC, tile(t + 8)]
            out = (
                adj[0:NC, tile(t + 8)]
                + gpot[0:NC, tile(t)] * (1.0 + 3.0 * cubic_coef * v * v)
                + net[:, k * LZ : (k + 1) * LZ]
            )
            outgoing[pl.ds(t, NC, stride=OWN), :] = out


def weight_grads(pres, rhs, grads, late):
    one, two, pre3 = pres
    rhs1, rhs2, rhs3 = rhs
    g1, g2 = dot(one[...], rhs1[...], 1, 1), dot(two[...], rhs2[...], 1, 1)
    row = lax.broadcasted_iota(jnp.int32, (ROWS, 2 * LZ), 0)
    entry = lax.broadcasted_iota(jnp.int32, (ROWS, 2 * LZ), 1)
    pick = jnp.where((entry == row // GRP * NC + row % GRP) & (row % GRP < NC), 1.0, 0.0).astype(F32)
    g3 = dot(dot(rhs3[...], pre3[...], 1, 1), pick, precision=lax.Precision.HIGHEST)
    lane = lanes((HID, LZ))
    second = g2 + pltpu.roll(g3[:, LZ:], 64, 1) + pltpu.roll(g1, 80, 1)
    s1 = jnp.sum(one[...].astype(F32), axis=1, keepdims=True)
    s2 = jnp.sum(two[...].astype(F32), axis=1, keepdims=True)
    s3 = jnp.sum(pre3[...].astype(F32), axis=1, keepdims=True)
    for k, col in enumerate((s1, s2, s3[0:64], s3[64:128], s3[128:192])):
        second = jnp.where(lane == 92 + k, col, second)
    first = g3[:, 0:LZ]
    if late is not None:
        first, second = first + late[0:HID, :], second + late[HID:, :]
    grads[0:HID, :] = first
    grads[HID:, :] = second


def late_kernel(state, cot, *refs):
    faces, sent_z, prep, weights = refs[0:6], refs[6:8], refs[8:12], refs[12:15]
    keep = refs[16:19]
    outgoing, outs, pres, mob = refs[19], refs[20:26], refs[26:29], refs[29]
    values, pots, adj, fx, fy, fz, gpot = refs[30:]
    load_extended(state, faces, sent_z, 0, 0, values)
    load_extended(cot, faces, sent_z, 1, 1, adj)
    pots[...] = potential(values[...])
    network(values, HALO, prep, False, mob)
    reverse_step(values, pots, adj, mob, keep, weights, (fx, fy, fz), gpot, outgoing, pres)
    pack_faces(outgoing, outs, 0)


def late_grads_kernel(*refs):
    weight_grads(refs[0:3], refs[3:6], refs[6], None)


def early_kernel(values, back, *refs):
    faces, sent_z, weights, mob, rhs, slope, late = refs[0:6], refs[6:8], refs[8:11], refs[11], refs[12:15], refs[15], refs[16]
    outgoing, grads = refs[17:19]
    pots, adj, fx, fy, fz, gpot, one, two, pre3 = refs[19:]
    load_extended(back, faces, sent_z, 0, 0, adj)
    pots[...] = potential(values[...])
    keep = (rhs[1], rhs[2], slope)
    reverse_step(values, pots, adj, mob, keep, weights, (fx, fy, fz), gpot, outgoing, (one, two, pre3))
    weight_grads((one, two, pre3), rhs, grads, late)


def finish_kernel(factor, grads, ow1t, ob1, ow2, ob2, ow3t, ob3):
    ow3t[:, 0:LZ] = grads[0:HID, :] * factor
    second = grads[HID:, :] * factor
    ow2[...] = second[:, 0:HID]
    ow3t[:, LZ:] = pltpu.roll(second, 64, 1)[:, 0:16]
    rest = pltpu.roll(second, LZ - 80, 1)
    turned = rest.T
    ow1t[...] = turned[0:NC, :]
    ob1[...] = turned[12:13, :]
    ob2[...] = turned[13:14, :]
    row = lax.broadcasted_iota(jnp.int32, (HID, MM), 0)
    lane = lanes((HID, MM))
    total = jnp.zeros((HID, MM), F32)
    for k in range(3):
        padded = row + HID * k
        target = padded // GRP * NC + padded % GRP
        total = total + jnp.where((lane == target) & (padded % GRP < NC), rest[:, 14 + k : 15 + k], 0.0)
    ob3[...] = jnp.sum(total, axis=0, keepdims=True)


def shape(*dims):
    return jax.ShapeDtypeStruct(dims, F32)


def face_shapes(parts):
    x, y, z = shape(96 * parts, LZ), shape(24 * parts, LZ), shape(GRP * parts, LZ)
    return (x, y, y, z, z, x)


def call(kernel, outs, args, scratch=(), aliases=None):
    return pl.pallas_call(
        kernel,
        out_shape=outs,
        in_specs=[VM] * len(args),
        out_specs=tuple(VM for _ in outs),
        scratch_shapes=list(scratch),
        input_output_aliases=aliases or {},
        compiler_params=pltpu.CompilerParams(vmem_limit_bytes=20 << 20),
    )(*args)


def wide(tiles, rows=GRP, kind=F32):
    return pltpu.VMEM((rows, tiles * LZ), kind)


def array(tiles, rows=GRP, kind=F32):
    return jax.ShapeDtypeStruct((rows, tiles * LZ), kind)


FLOWS = (wide(24), wide(18), wide(OWN + 1))
KEPT = (array(OWN, 2 * HID, BF16), array(OWN, 2 * HID, BF16), array(OWN, HID, BF16), array(OWN, ROWS))
PRES = (array(OWN, HID, BF16), array(OWN, HID, BF16), array(OWN, ROWS, BF16))


def group_sum(value, partners):
    received = [swap(value, partner) for partner in partners]
    for other in received:
        value = value + other
    return value


def total_over_devices(value):
    half = value.shape[0] // 2
    core = lax.axis_index("gx") % 2
    keep = lax.dynamic_slice_in_dim(value, core * half, half, 0)
    give = lax.dynamic_slice_in_dim(value, (1 - core) * half, half, 0)
    value = keep + swap(give, lambda a, b, c: (a ^ 1, b, c))
    value = group_sum(value, [lambda a, b, c, k=k: (a, b, c ^ k) for k in (2, 1, 3)])
    value = group_sum(value, [lambda a, b, c, k=k: (a, b ^ k, c) for k in (2, 1, 3)])
    far = (lambda a, b, c: (a ^ 2, b, c), lambda a, b, c: (a, b ^ 8, c), lambda a, b, c: (a ^ 2, b ^ 8, c))
    value = group_sum(value, far)
    value = value + swap(value, lambda a, b, c: (a, b ^ 4, c))
    other = swap(value, lambda a, b, c: (a ^ 1, b, c))
    return jnp.concatenate([jnp.where(core == 0, value, other), jnp.where(core == 0, other, value)], 0)


def shards(composition, cotangent, w1, b1, w2, b2, w3, b3):
    block = composition.shape
    comp = composition.reshape(NC * OWN, LZ)
    cot = cotangent.reshape(NC * OWN, LZ)
    w1t, w3t = w1.T, w3.T
    mob_shape = array(TILES, ROWS)

    sent = call(pack_kernel, face_shapes(1), (comp,))
    comp_faces = exchange(sent)
    comp_z = sent[3:5]
    *ready, mob, cx, cyb, cya, czb, cza, cn = call(
        prepare_kernel,
        (
            jax.ShapeDtypeStruct((HID, NC), BF16),
            jax.ShapeDtypeStruct((HID, HID), BF16),
            jax.ShapeDtypeStruct((ROWS, HID), BF16),
            jax.ShapeDtypeStruct((ROWS, HID), BF16),
            jax.ShapeDtypeStruct((HID, ROWS), BF16),
            shape(ROWS, LZ),
            mob_shape,
        )
        + face_shapes(1),
        (comp, cot, w1t, b1.reshape(1, HID), w2, b2.reshape(1, HID), w3t, b3.reshape(1, MM)),
        (wide(TILES),),
    )
    w1p, w2t, w3c, w3r, w3rt, cols = ready
    forward, reverse, back_weights = (w1p, w2, w3c, cols), (w1p, w2, w3r, cols), (w1t, w2t, w3rt)
    moved, *sent, values, _ = call(
        forward_kernel,
        (shape(NC * OWN, LZ),) + face_shapes(2) + (array(TILES), mob_shape),
        (comp, *comp_faces, *comp_z, cx, cyb, cya, czb, cza, cn, *forward, mob),
        (wide(TILES),) + FLOWS,
        {19: 8},
    )
    got = exchange(sent)
    mob, *kept = call(own_network_kernel, (mob_shape,) + KEPT, (moved, *reverse), (wide(TILES),))
    comp_mob, *comp_kept = call(full_network_kernel, (mob_shape,) + KEPT, (values, *reverse))
    back, *rest = call(
        late_kernel,
        (shape(NC * OWN, LZ),) + face_shapes(1) + PRES + (mob_shape,),
        (moved, cot, *got, *sent[3:5], *reverse, *back_weights, mob, *kept[1:]),
        (wide(TILES), wide(TILES), wide(TILES)) + FLOWS + (wide(OWN),),
        {17: 10},
    )
    sent, pres = rest[:6], rest[6:9]
    got = exchange(sent)
    (late,) = call(late_grads_kernel, (shape(GROWS, LZ),), (*pres, *kept[:3]))
    final, grads = call(
        early_kernel,
        (shape(NC * OWN, LZ), shape(GROWS, LZ)),
        (values, back, *got, *sent[3:5], *back_weights, comp_mob, *comp_kept, late),
        (wide(TILES), wide(TILES)) + FLOWS + (wide(OWN), wide(OWN, HID, BF16), wide(OWN, HID, BF16), wide(OWN, ROWS, BF16)),
    )
    grads = total_over_devices(grads)
    cells = OWN * LZ * GX * GY * GZ
    factor = 1.0 / (step_size * math.sqrt(cells))
    ow1t, ob1, ow2, ob2, ow3t, ob3 = call(
        functools.partial(finish_kernel, factor),
        (shape(NC, HID), shape(1, HID), shape(HID, HID), shape(1, HID), shape(HID, MM), shape(1, MM)),
        (grads,),
    )
    return (final.reshape(block), ow1t.T, ob1.reshape(HID), ow2, ob2.reshape(HID), ow3t.T, ob3.reshape(MM))


def solution(mesh):
    in_specs = (P(None, "gx", "gy", "gz"), P(None, "gx", "gy", "gz"), P(), P(), P(), P(), P(), P())
    out_specs = (P(None, "gx", "gy", "gz"), P(), P(), P(), P(), P(), P())
    return jax.shard_map(shards, mesh=mesh, in_specs=in_specs, out_specs=out_specs, check_vma=False)
```

```python
import functools
import math

import jax
import jax.numpy as jnp
from jax import lax
from jax.experimental import pallas as pl
from jax.experimental.pallas import tpu as pltpu
from jax.sharding import PartitionSpec as P


AXES = ("gx", "gy", "gz")
GX, GY, GZ = 4, 16, 4
step_size = 0.08
cubic_coef = 0.1
diag_scale = 0.5
off_scale = 0.04

NC, HID, MM = 12, 64, 144
LX, LY, LZ = 2, 8, 128
OWN = LX * LY
GRP = 16
ROWS = NC * GRP
YM, YP, ZT = 32, 34, 36
TILES = 37
CHUNK = 1024
RIM = 21
HALO = ((0, 8, 0), (24, 32, 8), (32, 37, 16))
RHS = HID + GRP
GROWS = 144
F32, BF16 = jnp.float32, jnp.bfloat16
VM = pl.BlockSpec(memory_space=pltpu.VMEM)


def swap(value, partner):
    pairs = []
    for a in range(GX):
        for b in range(GY):
            for c in range(GZ):
                a2, b2, c2 = partner(a, b, c)
                pairs.append(((a * GY + b) * GZ + c, (a2 * GY + b2) * GZ + c2))
    return lax.ppermute(value, AXES, pairs)


def odd_up(i, n):
    return (i + 1) % n if i % 2 else (i - 1) % n


FACE_PARTNERS = (
    lambda a, b, c: (odd_up(a, GX), b, c),
    lambda a, b, c: (a, odd_up(b, GY), c),
    lambda a, b, c: (a, b ^ 1, c),
    lambda a, b, c: (a, b, odd_up(c, GZ)),
    lambda a, b, c: (a, b, c ^ 1),
    lambda a, b, c: (a ^ 1, b, c),
)


def exchange(faces):
    return [swap(face, partner) for face, partner in zip(faces, FACE_PARTNERS)]


def parities():
    return lax.axis_index("gx") % 2, lax.axis_index("gy") % 2, lax.axis_index("gz") % 2


def lanes(shape):
    return lax.broadcasted_iota(jnp.int32, shape, len(shape) - 1)


def tile(index):
    start = index * LZ
    return pl.ds(start if isinstance(start, int) else pl.multiple_of(start, LZ), LZ)


def pack_faces(native, outs, part):
    px, py, pz = parities()
    xf, yb, ya, zb, za, xn = outs
    for ch in range(NC):
        xf[pl.ds(part * 96 + ch * 8, 8), :] = native[pl.ds(pl.multiple_of(ch * OWN + px * LY, 8), 8), :]
        xn[pl.ds(part * 96 + ch * 8, 8), :] = native[pl.ds(pl.multiple_of(ch * OWN + (1 - px) * LY, 8), 8), :]
    first = native[pl.ds(0, 24, stride=8), :]
    last = native[pl.ds(7, 24, stride=8), :]
    ya[pl.ds(part * 24, 24), :] = jnp.where(py == 0, last, first)
    yb[pl.ds(part * 24, 24), :] = jnp.where(py == 0, first, last)
    lane = lanes((NC, LZ))
    low = jnp.zeros((NC, LZ), F32)
    high = jnp.zeros((NC, LZ), F32)
    for t in range(OWN):
        block = native[pl.ds(t, NC, stride=OWN), :]
        low = jnp.where(lane == t, pltpu.roll(block, t, 1), low)
        high = jnp.where(lane == t, pltpu.roll(block, (t + 1) % LZ, 1), high)
    zero = jnp.zeros((GRP - NC, LZ), F32)
    za[pl.ds(part * GRP, NC), :] = jnp.where(pz == 0, high, low)
    zb[pl.ds(part * GRP, NC), :] = jnp.where(pz == 0, low, high)
    za[pl.ds(part * GRP + NC, GRP - NC), :] = zero
    zb[pl.ds(part * GRP + NC, GRP - NC), :] = zero


def load_own(native, dest):
    dest[...] = jnp.zeros((GRP, TILES * LZ), F32)
    for t in range(OWN):
        dest[0:NC, tile(8 + t)] = native[pl.ds(t, NC, stride=OWN), :]


def load_halo(faces, sent_z, part, sent_part, dest):
    px, py, pz = parities()
    xf, yb, ya, zb, za, xn = faces
    for y in range(LY):
        dest[0:NC, tile(24 * px + y)] = xf[pl.ds(part * 96 + y, NC, stride=LY), :]
        dest[0:NC, tile(24 - 24 * px + y)] = xn[pl.ds(part * 96 + y, NC, stride=LY), :]
    for x in range(LX):
        dest[0:NC, tile(YP - 2 * py + x)] = ya[pl.ds(part * 24 + x, NC, stride=LX), :]
        dest[0:NC, tile(YM + 2 * py + x)] = yb[pl.ds(part * 24 + x, NC, stride=LX), :]
    got = slice(part * GRP, part * GRP + GRP)
    own = slice(sent_part * GRP, sent_part * GRP + GRP)
    got_a, got_b = za[got, :], zb[got, :]
    own_b, own_a = sent_z[0][own, :], sent_z[1][own, :]
    even = pz == 0
    lane = lanes((GRP, LZ))
    rim = jnp.where(lane < 16, jnp.where(even, got_b, got_a), 0.0)
    rim = jnp.where((lane >= 16) & (lane < 32), pltpu.roll(jnp.where(even, own_a, own_b), 16, 1), rim)
    rim = jnp.where((lane >= 32) & (lane < 48), pltpu.roll(jnp.where(even, own_b, own_a), 32, 1), rim)
    rim = jnp.where((lane >= 48) & (lane < 64), pltpu.roll(jnp.where(even, got_a, got_b), 48, 1), rim)
    dest[:, tile(ZT)] = rim


def pack_tiles(source, outs, part):
    px, py, pz = parities()
    xf, yb, ya, zb, za, xn = outs
    for y in range(LY):
        xf[pl.ds(part * 96 + y, NC, stride=LY), :] = source[0:NC, tile(8 + 8 * px + y)]
        xn[pl.ds(part * 96 + y, NC, stride=LY), :] = source[0:NC, tile(16 - 8 * px + y)]
    for x in range(LX):
        ya[pl.ds(part * 24 + x, NC, stride=LX), :] = source[0:NC, tile(8 + x * 8 + 7 - 7 * py)]
        yb[pl.ds(part * 24 + x, NC, stride=LX), :] = source[0:NC, tile(8 + x * 8 + 7 * py)]
    lane = lanes((GRP, LZ))
    low = jnp.zeros((GRP, LZ), F32)
    high = jnp.zeros((GRP, LZ), F32)
    for t in range(OWN):
        block = source[:, tile(8 + t)]
        low = jnp.where(lane == t, pltpu.roll(block, t, 1), low)
        high = jnp.where(lane == t, pltpu.roll(block, (t + 1) % LZ, 1), high)
    za[pl.ds(part * GRP, GRP), :] = jnp.where(pz == 0, high, low)
    zb[pl.ds(part * GRP, GRP), :] = jnp.where(pz == 0, low, high)


def clear(dest):
    dest[...] = jnp.zeros(dest.shape, dest.dtype)


def row_tables(by_column):
    row = lax.broadcasted_iota(jnp.int32, (ROWS, MM), 0)
    entry = lax.broadcasted_iota(jnp.int32, (ROWS, MM), 1)
    g, j = row // GRP, row % GRP
    want = j * NC + g if by_column else g * NC + j
    pick = jnp.where((entry == want) & (j < NC), 1.0, 0.0).astype(F32)
    row1 = lax.broadcasted_iota(jnp.int32, (ROWS, 1), 0)
    g1, j1 = row1 // GRP, row1 % GRP
    identity = jnp.where(g1 == j1, 1.0, 0.0).astype(F32)
    scales = jnp.where(g1 == j1, diag_scale, jnp.where(j1 < NC, off_scale, 0.0)).astype(F32)
    return pick, identity, scales


def eye(size, kind=F32):
    same = lax.broadcasted_iota(jnp.int32, (size, size), 0) == lax.broadcasted_iota(jnp.int32, (size, size), 1)
    return jnp.where(same, 1.0, 0.0).astype(kind)


def dot(a, b, ca=1, cb=0, precision=None):
    return lax.dot_general(a, b, (((ca,), (cb,)), ((), ())), preferred_element_type=F32, precision=precision)


def prepare(w1t, b1, w2, b2, w3t, b3, outs):
    w1p, w1c, w2c, w2t, w3c, w3r, w3rt, cols = outs
    w1c[...] = w1t[...]
    w2c[...] = w2[...]
    w1p[...] = dot(w1t[...], eye(NC, BF16), 0, 0).astype(BF16)
    w2t[...] = dot(w2[...], eye(HID, BF16), 0, 0).astype(BF16)
    pick_c, _, _ = row_tables(True)
    pick_r, _, _ = row_tables(False)
    w3c[...] = dot(pick_c.astype(BF16), w3t[...], 1, 1).astype(BF16)
    w3r[...] = dot(pick_r.astype(BF16), w3t[...], 1, 1).astype(BF16)
    w3rt[...] = dot(w3t[...], pick_r.astype(BF16), 1, 1).astype(BF16)
    cols[:, 0:1] = jnp.sum(pick_c * b3[...], axis=1, keepdims=True)
    cols[:, 1:2] = jnp.sum(pick_r * b3[...], axis=1, keepdims=True)
    cols[0:HID, 2:3] = jnp.sum(eye(HID) * b1[...], axis=1, keepdims=True)
    cols[0:HID, 3:4] = jnp.sum(eye(HID) * b2[...], axis=1, keepdims=True)


def network(values, spans, prep, by_column, mob, keep=None):
    w1p, w2, w3p, cols = prep
    row1 = lax.broadcasted_iota(jnp.int32, (ROWS, 1), 0)
    g1, j1 = row1 // GRP, row1 % GRP
    identity = jnp.where(g1 == j1, 1.0, 0.0).astype(F32)
    scales = jnp.where(g1 == j1, diag_scale, jnp.where(j1 < NC, off_scale, 0.0)).astype(F32)
    bias1, bias2 = cols[0:HID, 2:3], cols[0:HID, 3:4]
    bias3 = cols[:, 0:1] if by_column else cols[:, 1:2]
    for start, stop, goal in spans:
        cols_at = slice(start * LZ, stop * LZ)
        inputs = values[0:NC, cols_at].astype(BF16)
        one = jnp.tanh(dot(w1p[...], inputs) + bias1).astype(BF16)
        two = jnp.tanh(dot(w2[...], one) + bias2).astype(BF16)
        active = jnp.tanh(dot(w3p[...], two) + bias3)
        mob[:, goal * LZ : (goal + stop - start) * LZ] = identity + scales * active
        if keep is not None:
            own = slice(goal * LZ, (goal + stop - start) * LZ)
            rhs12, rhs3, slope1, slope2, slope = keep
            width = (stop - start) * LZ
            row = lax.broadcasted_iota(jnp.int32, (GRP, width), 0)
            rhs12[0:HID, own] = one
            rhs12[HID:, own] = jnp.where(row == NC, 1.0, values[:, cols_at]).astype(BF16)
            rhs3[0:HID, own] = two
            rhs3[HID:, own] = jnp.ones((GRP, width), BF16)
            one32, two32 = one.astype(F32), two.astype(F32)
            slope1[:, own] = 1.0 - one32 * one32
            slope2[:, own] = 1.0 - two32 * two32
            slope[:, own] = (0.5 * scales) * (1.0 - active * active)


OWN_SPANS = ((8, 16, 0), (16, 24, 8))


def potential(v):
    return v + cubic_coef * v * v * v


def flow_of(lower, upper, weight):
    total = None
    for k in range(NC):
        term = (lower(k) + upper(k)) * weight[k : k + 1, :]
        total = term if total is None else total + term
    return total


def mob_rows(mob, index):
    return lambda k: mob[GRP * k : GRP * k + GRP, tile(index)]


def product(mob, index, weight):
    total = None
    for k in range(NC):
        term = mob[GRP * k : GRP * k + GRP, tile(index)] * weight[k : k + 1, :]
        total = term if total is None else total + term
    return total


def y_face(j):
    x, k = j // 9, j % 9
    low = jnp.where(k == 0, YM + x, (x + 1) * 8 + k - 1)
    high = jnp.where(k == 8, YP + x, (x + 1) * 8 + k)
    return low, high


def xy_flows(mobs, weight_of, fx, fy):
    own, halo = mobs
    for k in range(24):
        low = mob_rows(halo, k) if k < 8 else mob_rows(own, k - 8)
        high = mob_rows(own, k) if k < 16 else mob_rows(halo, k - 8)
        fx[:, tile(k)] = flow_of(low, high, weight_of(k, k + 8))
    for x in range(LX):
        for k in range(LY + 1):
            low, high = x * 8 + (7 + k), x * 8 + (8 + k)
            low_rows, high_rows = mob_rows(own, low - 8), mob_rows(own, high - 8)
            if k == 0:
                low, low_rows = YM + x, mob_rows(halo, 16 + x)
            if k == LY:
                high, high_rows = YP + x, mob_rows(halo, 18 + x)
            fy[:, tile(x * 9 + k)] = flow_of(low_rows, high_rows, weight_of(low, high))


def rim_step(source):
    here = source[:, tile(ZT)]
    return pltpu.roll(here, 96, 1) - here


def z_steps(source, rim, t, lane):
    here = source[:, tile(t + 8)]
    step = pltpu.roll(here, LZ - 1, 1) - here
    up = jnp.where(lane == LZ - 1, pltpu.roll(rim, LZ - 1 - 16 - t, 1), step)
    low = jnp.where(lane == 0, pltpu.roll(rim, (LZ - t) % LZ, 1), pltpu.roll(step, 1, 1))
    return up, low


def rim_product(mob, weight, lane):
    return product(mob, RIM - 1, jnp.where(lane < 32, weight, pltpu.roll(weight, 32, 1)))


def z_balance(mob, t, up, low, rim, lane):
    at_up, at_low = product(mob, t, up), product(mob, t, low)
    from_next = jnp.where(lane == LZ - 1, pltpu.roll(rim, LZ - 1 - 48 - t, 1), pltpu.roll(at_low, LZ - 1, 1))
    from_last = jnp.where(lane == 0, pltpu.roll(rim, (LZ - t) % LZ, 1), pltpu.roll(at_up, 1, 1))
    return (at_up - at_low) + (from_next - from_last)


def pack_kernel(comp, *outs):
    pack_faces(comp, outs, 0)


def prepare_kernel(comp, *refs):
    far, outs = refs[0:7], refs[7:15]
    mob, values, adj, faces = refs[15], refs[16], refs[17], refs[18:24]
    near, sems = refs[24:31], refs[31]
    copies = [pltpu.make_async_copy(a, b, sems.at[i]) for i, (a, b) in enumerate(zip(far, near))]
    for copy in copies:
        copy.start()
    clear(values)
    clear(adj)
    for t in range(OWN):
        values[0:NC, tile(8 + t)] = comp[pl.ds(t, NC, stride=OWN), :]
    for copy in copies:
        copy.wait()
    cot, w1t, b1, w2, b2, w3t, b3 = near
    prepare(w1t, b1, w2, b2, w3t, b3, outs)
    network(values, OWN_SPANS, (outs[0], w2, outs[4], outs[7]), True, mob)
    for t in range(OWN):
        adj[0:NC, tile(8 + t)] = cot[pl.ds(t, NC, stride=OWN), :]
    pack_tiles(adj, faces, 0)


def forward_kernel(*refs):
    faces, sent_z, cot_faces, prep = refs[0:6], refs[6:8], refs[8:14], refs[14:18]
    mob, state, outs, values = refs[18], refs[20], refs[21:27], refs[27]
    pots, rim_mob, fx, fy = refs[28:]
    load_halo(faces, sent_z, 0, 0, values)
    pots[...] = potential(values[...])
    network(values, HALO, prep, True, rim_mob)
    xy_flows((mob, rim_mob), lambda low, high: 0.5 * (pots[:, tile(high)] - pots[:, tile(low)]), fx, fy)
    lane = lanes((GRP, LZ))
    rim = rim_step(pots)
    rim_flow = rim_product(rim_mob, 0.5 * rim, lane)
    clear(state)

    def body(x, carry):
        for y in range(LY):
            t = x * 8 + y
            at, yf = t + 8, x * 9 + y
            up, low = z_steps(pots, rim, t, lane)
            change = z_balance(mob, t, 0.5 * up, 0.5 * low, rim_flow, lane)
            change = change + (fx[:, tile(at)] - fx[:, tile(at - 8)]) + (fy[:, tile(yf + 1)] - fy[:, tile(yf)])
            state[:, tile(at)] = values[:, tile(at)] + step_size * change
        return carry

    lax.fori_loop(0, 2, body, 0)
    pack_tiles(state, outs, 0)
    for out, face in zip(outs, cot_faces):
        out[pl.ds(face.shape[0], face.shape[0]), :] = face[...]


def own_networks_kernel(state, values, w1p, w2, w3r, cols, *outs):
    prep = (w1p, w2, w3r, cols)
    network(state, OWN_SPANS, prep, False, outs[0], outs[1:6])
    network(values, OWN_SPANS, prep, False, outs[6], outs[7:12])


def rim_network_kernel(values, w1p, w2, w3r, cols, mob):
    network(values, HALO, (w1p, w2, w3r, cols), False, mob)


def reverse_step(values, pots, adj, mobs, slopes, weights, scratch, pres, emit):
    w1t, w2t, w3rt = weights
    slope1, slope2, slope = slopes
    pres12, pre3 = pres
    fx, fy, gpot, zju, zjl, zau, zal = scratch
    mob, rim_mob = mobs

    def jump_of(low, high):
        return pots[:, tile(high)] - pots[:, tile(low)]

    def adj_of(low, high):
        return step_size * (adj[:, tile(low)] - adj[:, tile(high)])

    xy_flows(mobs, lambda low, high: 0.5 * adj_of(low, high), fx, fy)
    lane = lanes((GRP, LZ))
    rim_jump, rim_adj = rim_step(pots), -step_size * rim_step(adj)
    rim_flow = rim_product(rim_mob, 0.5 * rim_adj, lane)

    def z_body(x, carry):
        for y in range(LY):
            t = x * 8 + y
            at, yf = t + 8, x * 9 + y
            zju[:, tile(t)], zjl[:, tile(t)] = z_steps(pots, rim_jump, t, lane)
            here = adj[:, tile(at)]
            step = step_size * (here - pltpu.roll(here, LZ - 1, 1))
            up = jnp.where(lane == LZ - 1, pltpu.roll(rim_adj, LZ - 1 - 16 - t, 1), step)
            low = jnp.where(lane == 0, pltpu.roll(rim_adj, (LZ - t) % LZ, 1), pltpu.roll(step, 1, 1))
            zau[:, tile(t)], zal[:, tile(t)] = up, low
            balance = z_balance(mob, t, 0.5 * up, 0.5 * low, rim_flow, lane)
            gpot[:, tile(t)] = (
                (fx[:, tile(at - 8)] - fx[:, tile(at)]) + (fy[:, tile(yf)] - fy[:, tile(yf + 1)]) - balance
            )
        return carry

    lax.fori_loop(0, 2, z_body, 0)

    def cell_body(i, carry):
        for t in (2 * i, 2 * i + 1):
            at = t + 8
            x, y = t // LY, t % LY
            y_low = jnp.where(y == 0, YM + x, at - 1)
            y_high = jnp.where(y == LY - 1, YP + x, at + 1)
            z = tile(t)
            pairs = (
                (adj_of(at - 8, at), jump_of(at - 8, at)),
                (adj_of(at, at + 8), jump_of(at, at + 8)),
                (adj_of(y_low, at), jump_of(y_low, at)),
                (adj_of(at, y_high), jump_of(at, y_high)),
                (zal[:, z], zjl[:, z]),
                (zau[:, z], zju[:, z]),
            )
            for k in range(NC):
                total = None
                for a, j in pairs:
                    term = a[k : k + 1, :] * j
                    total = term if total is None else total + term
                rows = slice(GRP * k, GRP * k + GRP)
                pre3[rows, z] = (total * slope[rows, z]).astype(BF16)
        return carry

    lax.fori_loop(0, OWN // 2, cell_body, 0)
    for at in range(0, OWN * LZ, CHUNK):
        own = slice(at, at + CHUNK)
        two = (dot(w3rt[...], pre3[:, own]) * slope2[:, own]).astype(BF16)
        one = (dot(w2t[...], two) * slope1[:, own]).astype(BF16)
        net = dot(w1t[...], one)
        pres12[0:HID, own] = one
        pres12[HID:, own] = two
        for k in range(CHUNK // LZ):
            t = at // LZ + k
            v = values[0:NC, tile(t + 8)]
            emit(
                t,
                adj[0:NC, tile(t + 8)]
                + gpot[0:NC, tile(t)] * (1.0 + 3.0 * cubic_coef * v * v)
                + net[:, k * LZ : (k + 1) * LZ],
            )


def weight_grads(pres, rhs, grads, room, late):
    pres12, pre3 = pres
    rhs12, rhs3 = rhs
    room[...] = jnp.zeros((2 * HID, 2 * LZ), F32)
    room[:, 0:RHS] = dot(pres12[...], rhs12[...], 1, 1)
    lane = lanes((HID, LZ))
    upper, lower = room[HID:, 0:LZ], room[0:HID, 0:LZ]
    second = jnp.where(lane < HID, upper, lower)
    second = jnp.where(lane == HID + NC + 1, pltpu.roll(upper, 1, 1), second)
    room[0:RHS, 0:ROWS] = dot(rhs3[...], pre3[...], 1, 1)
    left, right = room[0:RHS, 0:LZ], room[0:RHS, LZ:]
    lane = lanes((RHS, LZ))
    third, rest = jnp.zeros((RHS, LZ), F32), jnp.zeros((RHS, LZ), F32)
    for g in range(NC):
        source, start = (left, GRP * g) if g < 8 else (right, GRP * g - LZ)
        goal = NC * g
        if goal < LZ:
            moved = pltpu.roll(source, (goal - start) % LZ, 1)
            third = jnp.where((lane >= goal) & (lane < goal + NC), moved, third)
        if goal + NC > LZ:
            moved = pltpu.roll(source, (goal - LZ - start) % LZ, 1)
            rest = jnp.where((lane >= max(goal - LZ, 0)) & (lane < goal + NC - LZ), moved, rest)
    second = second + jnp.where(lanes((HID, LZ)) >= 80, pltpu.roll(rest[0:HID, :], 80, 1), 0.0)
    row = lax.broadcasted_iota(jnp.int32, (8, LZ), 0)
    bias = jnp.where(row == 0, third[HID : HID + 8, :], jnp.where(row == 1, rest[HID : HID + 8, :], 0.0))
    blocks = ((0, third[0:HID, :]), (HID, bias), (72, second), (136, jnp.zeros((8, LZ), F32)))
    for at, block in blocks:
        where = slice(at, at + block.shape[0])
        grads[where, :] = block if late is None else block + late[where, :]


def late_kernel(*refs):
    faces, sent_z, prep, weights, slopes = refs[0:6], refs[6:8], refs[8:12], refs[12:15], refs[18:21]
    mob, back, outs, pres, values, adj = refs[15], refs[21], refs[22:28], refs[28:30], refs[30], refs[31]
    pots, rim_mob, scratch = refs[32], refs[33], refs[34:]
    load_halo(faces, sent_z, 0, 0, values)
    load_halo(faces, sent_z, 1, 1, adj)
    pots[...] = potential(values[...])
    network(values, HALO, prep, False, rim_mob)
    clear(back)

    def emit(t, block):
        back[0:NC, tile(t + 8)] = block

    reverse_step(values, pots, adj, (mob, rim_mob), slopes, weights, scratch, pres, emit)
    pack_tiles(back, outs, 0)


def late_grads_kernel(*refs):
    weight_grads(refs[0:2], refs[2:4], refs[4], refs[5], None)


def core_rows(half):
    core = lax.axis_index("gx") % 2
    mine = pl.multiple_of(core * half, 8)
    others = pl.multiple_of((1 - core) * half, 8)
    return pl.ds(mine, half), pl.ds(others, half)


def early_kernel(values, *refs):
    faces, sent_z, weights, mobs, rhs, slopes, late = refs[0:6], refs[6:8], refs[8:11], refs[11:13], refs[13:15], refs[15:18], refs[18]
    final, keep, give, adj = refs[20:24]
    pots, pres, room, grads, scratch = refs[24], refs[25:27], refs[27], refs[28], refs[29:]
    load_halo(faces, sent_z, 0, 0, adj)
    pots[...] = potential(values[...])

    def emit(t, block):
        final[pl.ds(t, NC, stride=OWN), :] = block

    reverse_step(values, pots, adj, mobs, slopes, weights, scratch, pres, emit)
    weight_grads(pres, rhs, grads, room, late)
    half = GROWS // 2
    mine, others = core_rows(half)
    keep[...] = grads[mine, :]
    give[...] = grads[others, :]


def finish_kernel(factor, own, other, ow1t, ob1, ow2, ob2, ow3t, ob3, grads):
    mine, others = core_rows(GROWS // 2)
    grads[mine, :] = own[...]
    grads[others, :] = other[...]
    second = grads[72:136, :] * factor
    ow3t[:, 0:LZ] = grads[0:HID, :] * factor
    ow3t[:, LZ:] = pltpu.roll(second, LZ - 80, 1)[:, 0:16]
    ow2[...] = second[:, 0:HID]
    turned = pltpu.roll(second, 64, 1).T
    ow1t[...] = turned[0:NC, :]
    ob1[...] = turned[NC : NC + 1, :]
    ob2[...] = turned[NC + 1 : NC + 2, :]
    ob3[:, 0:LZ] = grads[HID : HID + 1, :] * factor
    ob3[:, LZ:] = grads[HID + 1 : HID + 2, 0:16] * factor


def shape(*dims):
    return jax.ShapeDtypeStruct(dims, F32)


def face_shapes(parts):
    x, y, z = shape(96 * parts, LZ), shape(24 * parts, LZ), shape(GRP * parts, LZ)
    return (x, y, y, z, z, x)


def call(kernel, outs, args, scratch=(), aliases=None, far=()):
    return pl.pallas_call(
        kernel,
        out_shape=outs,
        in_specs=[pl.BlockSpec(memory_space=pltpu.HBM) if i in far else VM for i in range(len(args))],
        out_specs=tuple(VM for _ in outs),
        scratch_shapes=list(scratch),
        input_output_aliases=aliases or {},
        compiler_params=pltpu.CompilerParams(vmem_limit_bytes=12 << 20),
    )(*args)


def wide(tiles, rows=GRP, kind=F32):
    return pltpu.VMEM((rows, tiles * LZ), kind)


def array(tiles, rows=GRP, kind=F32):
    return jax.ShapeDtypeStruct((rows, tiles * LZ), kind)


FLOWS = (wide(24), wide(18))
BACK = FLOWS + (wide(OWN),) * 5
KEPT = (array(OWN, RHS, BF16), array(OWN, RHS, BF16), array(OWN, HID), array(OWN, HID), array(OWN, ROWS))
PRES = (array(OWN, 2 * HID, BF16), array(OWN, ROWS, BF16))
ROOM = pltpu.VMEM((2 * HID, 2 * LZ), F32)


def group_sum(value, partners):
    received = [swap(value, partner) for partner in partners]
    for other in received:
        value = value + other
    return value


def total_over_devices(keep, give):
    value = keep + swap(give, lambda a, b, c: (a ^ 1, b, c))
    value = group_sum(value, [lambda a, b, c, k=k: (a, b, c ^ k) for k in (2, 1, 3)])
    value = group_sum(value, [lambda a, b, c, k=k: (a, b ^ k, c) for k in (2, 1, 3)])
    far = (lambda a, b, c: (a ^ 2, b, c), lambda a, b, c: (a, b ^ 8, c), lambda a, b, c: (a ^ 2, b ^ 8, c))
    value = group_sum(value, far)
    value = value + swap(value, lambda a, b, c: (a, b ^ 4, c))
    return value, swap(value, lambda a, b, c: (a ^ 1, b, c))


def shards(composition, cotangent, w1, b1, w2, b2, w3, b3):
    block = composition.shape
    comp = composition.reshape(NC * OWN, LZ)
    cot = cotangent.reshape(NC * OWN, LZ)
    w1t, w3t = w1.T, w3.T
    mob_shape = array(OWN, ROWS)

    sent = call(pack_kernel, face_shapes(1), (comp,))
    comp_faces = exchange(sent)
    comp_z = sent[3:5]
    inputs = (cot, w1t, b1.reshape(1, HID), w2, b2.reshape(1, HID), w3t, b3.reshape(1, MM))
    w1p, w1c, w2c, w2t, w3c, w3r, w3rt, cols, mob, values, adj, *cot_faces = call(
        prepare_kernel,
        (
            jax.ShapeDtypeStruct((HID, NC), BF16),
            jax.ShapeDtypeStruct((NC, HID), BF16),
            jax.ShapeDtypeStruct((HID, HID), BF16),
            jax.ShapeDtypeStruct((HID, HID), BF16),
            jax.ShapeDtypeStruct((ROWS, HID), BF16),
            jax.ShapeDtypeStruct((ROWS, HID), BF16),
            jax.ShapeDtypeStruct((HID, ROWS), BF16),
            shape(ROWS, LZ),
            mob_shape,
            array(TILES),
            array(TILES),
        )
        + face_shapes(1),
        (comp, *inputs),
        tuple(pltpu.VMEM(a.shape, a.dtype) for a in inputs) + (pltpu.SemaphoreType.DMA((len(inputs),)),),
        far=range(1, 1 + len(inputs)),
    )
    forward, reverse, back_weights = (w1p, w2c, w3c, cols), (w1p, w2c, w3r, cols), (w1c, w2t, w3rt)
    state, *sent, values = call(
        forward_kernel,
        (array(TILES),) + face_shapes(2) + (array(TILES),),
        (*comp_faces, *comp_z, *cot_faces, *forward, mob, values),
        (wide(TILES), wide(RIM, ROWS)) + FLOWS,
        {19: 7},
    )
    got = exchange(sent)
    mob, *kept = call(own_networks_kernel, ((mob_shape,) + KEPT) * 2, (state, values, *reverse))
    kept, comp_mob, comp_kept = kept[:5], kept[5], kept[6:]
    back, *rest = call(
        late_kernel,
        (array(TILES),) + face_shapes(1) + PRES + (array(TILES), array(TILES)),
        (*got, *sent[3:5], *reverse, *back_weights, mob, state, adj, *kept[2:]),
        (wide(TILES), wide(RIM, ROWS)) + BACK,
        {16: 9, 17: 10},
    )
    sent, pres = rest[:6], rest[6:8]
    got = exchange(sent)
    (late,) = call(late_grads_kernel, (shape(GROWS, LZ),), (*pres, *kept[:2]), (ROOM,))
    (comp_rim,) = call(rim_network_kernel, (array(RIM, ROWS),), (values, *reverse))
    final, keep, give, _ = call(
        early_kernel,
        (shape(NC * OWN, LZ), shape(GROWS // 2, LZ), shape(GROWS // 2, LZ), array(TILES)),
        (values, *got, *sent[3:5], *back_weights, comp_mob, comp_rim, *comp_kept, late, back),
        (wide(TILES), wide(OWN, 2 * HID, BF16), wide(OWN, ROWS, BF16), ROOM, pltpu.VMEM((GROWS, LZ), F32)) + BACK,
        {20: 3},
    )
    totals = total_over_devices(keep, give)
    cells = OWN * LZ * GX * GY * GZ
    factor = 1.0 / (step_size * math.sqrt(cells))
    ow1t, ob1, ow2, ob2, ow3t, ob3 = call(
        functools.partial(finish_kernel, factor),
        (shape(NC, HID), shape(1, HID), shape(HID, HID), shape(1, HID), shape(HID, MM), shape(1, MM)),
        totals,
        (pltpu.VMEM((GROWS, LZ), F32),),
    )
    return (final.reshape(block), ow1t.T, ob1.reshape(HID), ow2, ob2.reshape(HID), ow3t.T, ob3.reshape(MM))


def solution(mesh):
    in_specs = (P(None, "gx", "gy", "gz"), P(None, "gx", "gy", "gz"), P(), P(), P(), P(), P(), P())
    out_specs = (P(None, "gx", "gy", "gz"), P(), P(), P(), P(), P(), P())
    return jax.shard_map(shards, mesh=mesh, in_specs=in_specs, out_specs=out_specs, check_vma=False)
```

```python
import functools
import math

import jax
import jax.numpy as jnp
from jax import lax
from jax.experimental import pallas as pl
from jax.experimental.pallas import tpu as pltpu
from jax.sharding import PartitionSpec as P


AXES = ("gx", "gy", "gz")
GX, GY, GZ = 4, 16, 4
step_size = 0.08
cubic_coef = 0.1
diag_scale = 0.5
off_scale = 0.04

NC, HID, MM = 12, 64, 144
LX, LY, LZ = 2, 8, 128
OWN = LX * LY
GRP = 16
ROWS = NC * GRP
YM, YP, ZT = 32, 34, 36
TILES = 37
CHUNK = 1024
RIM = 21
HALO = ((0, 8, 0), (24, 32, 8), (32, 37, 16))
RHS = HID + GRP
GROWS = 128
F32, BF16 = jnp.float32, jnp.bfloat16
VM = pl.BlockSpec(memory_space=pltpu.VMEM)


def swap(value, partner):
    pairs = []
    for a in range(GX):
        for b in range(GY):
            for c in range(GZ):
                a2, b2, c2 = partner(a, b, c)
                pairs.append(((a * GY + b) * GZ + c, (a2 * GY + b2) * GZ + c2))
    return lax.ppermute(value, AXES, pairs)


def odd_up(i, n):
    return (i + 1) % n if i % 2 else (i - 1) % n


FACE_PARTNERS = (
    lambda a, b, c: (odd_up(a, GX), b, c),
    lambda a, b, c: (a, odd_up(b, GY), c),
    lambda a, b, c: (a, b ^ 1, c),
    lambda a, b, c: (a, b, odd_up(c, GZ)),
    lambda a, b, c: (a, b, c ^ 1),
    lambda a, b, c: (a ^ 1, b, c),
)


def exchange(faces):
    return [swap(face, partner) for face, partner in zip(faces, FACE_PARTNERS)]


def parities():
    return lax.axis_index("gx") % 2, lax.axis_index("gy") % 2, lax.axis_index("gz") % 2


def lanes(shape):
    return lax.broadcasted_iota(jnp.int32, shape, len(shape) - 1)


def tile(index):
    start = index * LZ
    return pl.ds(start if isinstance(start, int) else pl.multiple_of(start, LZ), LZ)


def pack_faces(native, outs, part):
    px, py, pz = parities()
    xf, yb, ya, zb, za, xn = outs
    for ch in range(NC):
        xf[pl.ds(part * 96 + ch * 8, 8), :] = native[pl.ds(pl.multiple_of(ch * OWN + px * LY, 8), 8), :]
        xn[pl.ds(part * 96 + ch * 8, 8), :] = native[pl.ds(pl.multiple_of(ch * OWN + (1 - px) * LY, 8), 8), :]
    first = native[pl.ds(0, 24, stride=8), :]
    last = native[pl.ds(7, 24, stride=8), :]
    ya[pl.ds(part * 24, 24), :] = jnp.where(py == 0, last, first)
    yb[pl.ds(part * 24, 24), :] = jnp.where(py == 0, first, last)
    lane = lanes((NC, LZ))
    low = jnp.zeros((NC, LZ), F32)
    high = jnp.zeros((NC, LZ), F32)
    for t in range(OWN):
        block = native[pl.ds(t, NC, stride=OWN), :]
        low = jnp.where(lane == t, pltpu.roll(block, t, 1), low)
        high = jnp.where(lane == t, pltpu.roll(block, (t + 1) % LZ, 1), high)
    zero = jnp.zeros((GRP - NC, LZ), F32)
    za[pl.ds(part * GRP, NC), :] = jnp.where(pz == 0, high, low)
    zb[pl.ds(part * GRP, NC), :] = jnp.where(pz == 0, low, high)
    za[pl.ds(part * GRP + NC, GRP - NC), :] = zero
    zb[pl.ds(part * GRP + NC, GRP - NC), :] = zero


def load_own(native, dest):
    dest[...] = jnp.zeros((GRP, TILES * LZ), F32)
    for t in range(OWN):
        dest[0:NC, tile(8 + t)] = native[pl.ds(t, NC, stride=OWN), :]


def load_halo(faces, sent_z, part, sent_part, dest):
    px, py, pz = parities()
    xf, yb, ya, zb, za, xn = faces
    for y in range(LY):
        dest[0:NC, tile(24 * px + y)] = xf[pl.ds(part * 96 + y, NC, stride=LY), :]
        dest[0:NC, tile(24 - 24 * px + y)] = xn[pl.ds(part * 96 + y, NC, stride=LY), :]
    for x in range(LX):
        dest[0:NC, tile(YP - 2 * py + x)] = ya[pl.ds(part * 24 + x, NC, stride=LX), :]
        dest[0:NC, tile(YM + 2 * py + x)] = yb[pl.ds(part * 24 + x, NC, stride=LX), :]
    got = slice(part * GRP, part * GRP + GRP)
    own = slice(sent_part * GRP, sent_part * GRP + GRP)
    got_a, got_b = za[got, :], zb[got, :]
    own_b, own_a = sent_z[0][own, :], sent_z[1][own, :]
    even = pz == 0
    lane = lanes((GRP, LZ))
    rim = jnp.where(lane < 16, jnp.where(even, got_b, got_a), 0.0)
    rim = jnp.where((lane >= 16) & (lane < 32), pltpu.roll(jnp.where(even, own_a, own_b), 16, 1), rim)
    rim = jnp.where((lane >= 32) & (lane < 48), pltpu.roll(jnp.where(even, own_b, own_a), 32, 1), rim)
    rim = jnp.where((lane >= 48) & (lane < 64), pltpu.roll(jnp.where(even, got_a, got_b), 48, 1), rim)
    dest[:, tile(ZT)] = rim


def pack_tiles(source, outs, part):
    px, py, pz = parities()
    xf, yb, ya, zb, za, xn = outs
    for y in range(LY):
        xf[pl.ds(part * 96 + y, NC, stride=LY), :] = source[0:NC, tile(8 + 8 * px + y)]
        xn[pl.ds(part * 96 + y, NC, stride=LY), :] = source[0:NC, tile(16 - 8 * px + y)]
    for x in range(LX):
        ya[pl.ds(part * 24 + x, NC, stride=LX), :] = source[0:NC, tile(8 + x * 8 + 7 - 7 * py)]
        yb[pl.ds(part * 24 + x, NC, stride=LX), :] = source[0:NC, tile(8 + x * 8 + 7 * py)]
    lane = lanes((GRP, LZ))
    low = jnp.zeros((GRP, LZ), F32)
    high = jnp.zeros((GRP, LZ), F32)
    for t in range(OWN):
        block = source[:, tile(8 + t)]
        low = jnp.where(lane == t, pltpu.roll(block, t, 1), low)
        high = jnp.where(lane == t, pltpu.roll(block, (t + 1) % LZ, 1), high)
    za[pl.ds(part * GRP, GRP), :] = jnp.where(pz == 0, high, low)
    zb[pl.ds(part * GRP, GRP), :] = jnp.where(pz == 0, low, high)


def clear(dest):
    dest[...] = jnp.zeros(dest.shape, dest.dtype)


def row_tables(by_column):
    row = lax.broadcasted_iota(jnp.int32, (ROWS, MM), 0)
    entry = lax.broadcasted_iota(jnp.int32, (ROWS, MM), 1)
    g, j = row // GRP, row % GRP
    want = j * NC + g if by_column else g * NC + j
    pick = jnp.where((entry == want) & (j < NC), 1.0, 0.0).astype(F32)
    row1 = lax.broadcasted_iota(jnp.int32, (ROWS, 1), 0)
    g1, j1 = row1 // GRP, row1 % GRP
    identity = jnp.where(g1 == j1, 1.0, 0.0).astype(F32)
    scales = jnp.where(g1 == j1, diag_scale, jnp.where(j1 < NC, off_scale, 0.0)).astype(F32)
    return pick, identity, scales


def eye(size, kind=F32):
    same = lax.broadcasted_iota(jnp.int32, (size, size), 0) == lax.broadcasted_iota(jnp.int32, (size, size), 1)
    return jnp.where(same, 1.0, 0.0).astype(kind)


def dot(a, b, ca=1, cb=0, precision=None):
    return lax.dot_general(a, b, (((ca,), (cb,)), ((), ())), preferred_element_type=F32, precision=precision)


def prepare(w1t, b1, w2, b2, w3t, b3, outs):
    w1p, w1c, w2c, w2t, w3c, w3r, w3rt, cols = outs
    w1c[...] = w1t[...]
    w2c[...] = w2[...]
    w1p[...] = dot(w1t[...], eye(NC, BF16), 0, 0).astype(BF16)
    w2t[...] = dot(w2[...], eye(HID, BF16), 0, 0).astype(BF16)
    pick_c, _, _ = row_tables(True)
    pick_r, _, _ = row_tables(False)
    w3c[...] = dot(pick_c.astype(BF16), w3t[...], 1, 1).astype(BF16)
    w3r[...] = dot(pick_r.astype(BF16), w3t[...], 1, 1).astype(BF16)
    w3rt[...] = dot(w3t[...], pick_r.astype(BF16), 1, 1).astype(BF16)
    cols[:, 0:1] = jnp.sum(pick_c * b3[...], axis=1, keepdims=True)
    cols[:, 1:2] = jnp.sum(pick_r * b3[...], axis=1, keepdims=True)
    cols[0:HID, 2:3] = jnp.sum(eye(HID) * b1[...], axis=1, keepdims=True)
    cols[0:HID, 3:4] = jnp.sum(eye(HID) * b2[...], axis=1, keepdims=True)


def network(values, spans, prep, by_column, mob, keep=None):
    w1p, w2, w3p, cols = prep
    row1 = lax.broadcasted_iota(jnp.int32, (ROWS, 1), 0)
    g1, j1 = row1 // GRP, row1 % GRP
    identity = jnp.where(g1 == j1, 1.0, 0.0).astype(F32)
    scales = jnp.where(g1 == j1, diag_scale, jnp.where(j1 < NC, off_scale, 0.0)).astype(F32)
    bias1, bias2 = cols[0:HID, 2:3], cols[0:HID, 3:4]
    bias3 = cols[:, 0:1] if by_column else cols[:, 1:2]
    for start, stop, goal in spans:
        cols_at = slice(start * LZ, stop * LZ)
        inputs = values[0:NC, cols_at].astype(BF16)
        one = jnp.tanh(dot(w1p[...], inputs) + bias1).astype(BF16)
        two = jnp.tanh(dot(w2[...], one) + bias2).astype(BF16)
        active = jnp.tanh(dot(w3p[...], two) + bias3)
        mob[:, goal * LZ : (goal + stop - start) * LZ] = identity + scales * active
        if keep is not None:
            own = slice(goal * LZ, (goal + stop - start) * LZ)
            rhs12, rhs3, slope1, slope2, slope = keep
            width = (stop - start) * LZ
            row = lax.broadcasted_iota(jnp.int32, (GRP, width), 0)
            rhs12[0:HID, own] = one
            rhs12[HID:, own] = jnp.where(row == NC, 1.0, values[:, cols_at]).astype(BF16)
            rhs3[0:HID, own] = two
            rhs3[HID:, own] = jnp.ones((GRP, width), BF16)
            one32, two32 = one.astype(F32), two.astype(F32)
            slope1[:, own] = 1.0 - one32 * one32
            slope2[:, own] = 1.0 - two32 * two32
            slope[:, own] = (0.5 * scales) * (1.0 - active * active)


OWN_SPANS = ((8, 16, 0), (16, 24, 8))


def potential(v):
    return v + cubic_coef * v * v * v


def flow_of(lower, upper, weight):
    total = None
    for k in range(NC):
        term = (lower(k) + upper(k)) * weight[k : k + 1, :]
        total = term if total is None else total + term
    return total


def mob_rows(mob, index):
    return lambda k: mob[GRP * k : GRP * k + GRP, tile(index)]


def product(mob, index, weight):
    total = None
    for k in range(NC):
        term = mob[GRP * k : GRP * k + GRP, tile(index)] * weight[k : k + 1, :]
        total = term if total is None else total + term
    return total


def y_face(j):
    x, k = j // 9, j % 9
    low = jnp.where(k == 0, YM + x, (x + 1) * 8 + k - 1)
    high = jnp.where(k == 8, YP + x, (x + 1) * 8 + k)
    return low, high


def xy_flows(mobs, weight_of, fx, fy):
    own, halo = mobs
    for k in range(24):
        low = mob_rows(halo, k) if k < 8 else mob_rows(own, k - 8)
        high = mob_rows(own, k) if k < 16 else mob_rows(halo, k - 8)
        fx[:, tile(k)] = flow_of(low, high, weight_of(k, k + 8))
    for x in range(LX):
        for k in range(LY + 1):
            low, high = x * 8 + (7 + k), x * 8 + (8 + k)
            low_rows, high_rows = mob_rows(own, low - 8), mob_rows(own, high - 8)
            if k == 0:
                low, low_rows = YM + x, mob_rows(halo, 16 + x)
            if k == LY:
                high, high_rows = YP + x, mob_rows(halo, 18 + x)
            fy[:, tile(x * 9 + k)] = flow_of(low_rows, high_rows, weight_of(low, high))


def rim_step(source):
    here = source[:, tile(ZT)]
    return pltpu.roll(here, 96, 1) - here


def z_steps(source, rim, t, lane):
    here = source[:, tile(t + 8)]
    step = pltpu.roll(here, LZ - 1, 1) - here
    up = jnp.where(lane == LZ - 1, pltpu.roll(rim, LZ - 1 - 16 - t, 1), step)
    low = jnp.where(lane == 0, pltpu.roll(rim, (LZ - t) % LZ, 1), pltpu.roll(step, 1, 1))
    return up, low


def rim_product(mob, weight, lane):
    return product(mob, RIM - 1, jnp.where(lane < 32, weight, pltpu.roll(weight, 32, 1)))


def z_balance(mob, t, up, low, rim, lane):
    at_up, at_low = product(mob, t, up), product(mob, t, low)
    from_next = jnp.where(lane == LZ - 1, pltpu.roll(rim, LZ - 1 - 48 - t, 1), pltpu.roll(at_low, LZ - 1, 1))
    from_last = jnp.where(lane == 0, pltpu.roll(rim, (LZ - t) % LZ, 1), pltpu.roll(at_up, 1, 1))
    return (at_up - at_low) + (from_next - from_last)


def pack_kernel(comp, *outs):
    pack_faces(comp, outs, 0)


def prepare_kernel(comp, *refs):
    far, outs = refs[0:7], refs[7:15]
    mob, values, adj, faces = refs[15], refs[16], refs[17], refs[18:24]
    near, sems = refs[24:31], refs[31]
    copies = [pltpu.make_async_copy(a, b, sems.at[i]) for i, (a, b) in enumerate(zip(far, near))]
    for copy in copies:
        copy.start()
    clear(values)
    clear(adj)
    for t in range(OWN):
        values[0:NC, tile(8 + t)] = comp[pl.ds(t, NC, stride=OWN), :]
    for copy in copies:
        copy.wait()
    cot, w1t, b1, w2, b2, w3t, b3 = near
    prepare(w1t, b1, w2, b2, w3t, b3, outs)
    network(values, OWN_SPANS, (outs[0], w2, outs[4], outs[7]), True, mob)
    for t in range(OWN):
        adj[0:NC, tile(8 + t)] = cot[pl.ds(t, NC, stride=OWN), :]
    pack_tiles(adj, faces, 0)


def forward_kernel(*refs):
    faces, sent_z, cot_faces, prep = refs[0:6], refs[6:8], refs[8:14], refs[14:18]
    mob, state, outs, values = refs[18], refs[20], refs[21:27], refs[27]
    pots, rim_mob, fx, fy = refs[28:]
    load_halo(faces, sent_z, 0, 0, values)
    pots[...] = potential(values[...])
    network(values, HALO, prep, True, rim_mob)
    xy_flows((mob, rim_mob), lambda low, high: 0.5 * (pots[:, tile(high)] - pots[:, tile(low)]), fx, fy)
    lane = lanes((GRP, LZ))
    rim = rim_step(pots)
    rim_flow = rim_product(rim_mob, 0.5 * rim, lane)
    clear(state)

    def body(x, carry):
        for y in range(LY):
            t = x * 8 + y
            at, yf = t + 8, x * 9 + y
            up, low = z_steps(pots, rim, t, lane)
            change = z_balance(mob, t, 0.5 * up, 0.5 * low, rim_flow, lane)
            change = change + (fx[:, tile(at)] - fx[:, tile(at - 8)]) + (fy[:, tile(yf + 1)] - fy[:, tile(yf)])
            state[:, tile(at)] = values[:, tile(at)] + step_size * change
        return carry

    lax.fori_loop(0, 2, body, 0)
    pack_tiles(state, outs, 0)
    for out, face in zip(outs, cot_faces):
        out[pl.ds(face.shape[0], face.shape[0]), :] = face[...]


def own_networks_kernel(state, values, w1p, w2, w3r, cols, *outs):
    prep = (w1p, w2, w3r, cols)
    network(state, OWN_SPANS, prep, False, outs[0], outs[1:6])
    network(values, OWN_SPANS, prep, False, outs[6], outs[7:12])


def rim_network_kernel(values, w1p, w2, w3r, cols, mob):
    network(values, HALO, (w1p, w2, w3r, cols), False, mob)


def reverse_step(values, pots, adj, mobs, slopes, weights, scratch, pres, emit):
    w1t, w2t, w3rt = weights
    slope1, slope2, slope = slopes
    pres12, pre3 = pres
    fx, fy, gpot, zju, zjl, zau, zal = scratch
    mob, rim_mob = mobs

    def jump_of(low, high):
        return pots[:, tile(high)] - pots[:, tile(low)]

    def adj_of(low, high):
        return step_size * (adj[:, tile(low)] - adj[:, tile(high)])

    xy_flows(mobs, lambda low, high: 0.5 * adj_of(low, high), fx, fy)
    lane = lanes((GRP, LZ))
    rim_jump, rim_adj = rim_step(pots), -step_size * rim_step(adj)
    rim_flow = rim_product(rim_mob, 0.5 * rim_adj, lane)

    def z_body(x, carry):
        for y in range(LY):
            t = x * 8 + y
            at, yf = t + 8, x * 9 + y
            zju[:, tile(t)], zjl[:, tile(t)] = z_steps(pots, rim_jump, t, lane)
            here = adj[:, tile(at)]
            step = step_size * (here - pltpu.roll(here, LZ - 1, 1))
            up = jnp.where(lane == LZ - 1, pltpu.roll(rim_adj, LZ - 1 - 16 - t, 1), step)
            low = jnp.where(lane == 0, pltpu.roll(rim_adj, (LZ - t) % LZ, 1), pltpu.roll(step, 1, 1))
            zau[:, tile(t)], zal[:, tile(t)] = up, low
            balance = z_balance(mob, t, 0.5 * up, 0.5 * low, rim_flow, lane)
            gpot[:, tile(t)] = (
                (fx[:, tile(at - 8)] - fx[:, tile(at)]) + (fy[:, tile(yf)] - fy[:, tile(yf + 1)]) - balance
            )
        return carry

    lax.fori_loop(0, 2, z_body, 0)

    def cell_body(i, carry):
        for t in (2 * i, 2 * i + 1):
            at = t + 8
            x, y = t // LY, t % LY
            y_low = jnp.where(y == 0, YM + x, at - 1)
            y_high = jnp.where(y == LY - 1, YP + x, at + 1)
            z = tile(t)
            pairs = (
                (adj_of(at - 8, at), jump_of(at - 8, at)),
                (adj_of(at, at + 8), jump_of(at, at + 8)),
                (adj_of(y_low, at), jump_of(y_low, at)),
                (adj_of(at, y_high), jump_of(at, y_high)),
                (zal[:, z], zjl[:, z]),
                (zau[:, z], zju[:, z]),
            )
            for k in range(NC):
                total = None
                for a, j in pairs:
                    term = a[k : k + 1, :] * j
                    total = term if total is None else total + term
                rows = slice(GRP * k, GRP * k + GRP)
                pre3[rows, z] = (total * slope[rows, z]).astype(BF16)
        return carry

    lax.fori_loop(0, OWN // 2, cell_body, 0)
    for at in range(0, OWN * LZ, CHUNK):
        own = slice(at, at + CHUNK)
        two = (dot(w3rt[...], pre3[:, own]) * slope2[:, own]).astype(BF16)
        one = (dot(w2t[...], two) * slope1[:, own]).astype(BF16)
        net = dot(w1t[...], one)
        pres12[0:HID, own] = one
        pres12[HID:, own] = two
        for k in range(CHUNK // LZ):
            t = at // LZ + k
            v = values[0:NC, tile(t + 8)]
            emit(
                t,
                adj[0:NC, tile(t + 8)]
                + gpot[0:NC, tile(t)] * (1.0 + 3.0 * cubic_coef * v * v)
                + net[:, k * LZ : (k + 1) * LZ],
            )


def weight_grads(pres, rhs, grads, room, late):
    pres12, pre3 = pres
    rhs12, rhs3 = rhs
    room[...] = jnp.zeros((2 * HID, 2 * LZ), F32)
    room[:, 0:RHS] = dot(pres12[...], rhs12[...], 1, 1)
    lane = lanes((HID, LZ))
    upper, lower = room[HID:, 0:LZ], room[0:HID, 0:LZ]
    second = jnp.where(lane < HID, upper, lower)
    second = jnp.where(lane == HID + NC + 1, pltpu.roll(upper, 1, 1), second)
    room[0:RHS, 0:ROWS] = dot(rhs3[...], pre3[...], 1, 1)
    left, right = room[0:RHS, 0:LZ], room[0:RHS, LZ:]
    lane = lanes((RHS, LZ))
    third, rest = jnp.zeros((RHS, LZ), F32), jnp.zeros((RHS, LZ), F32)
    for g in range(NC):
        source, start = (left, GRP * g) if g < 8 else (right, GRP * g - LZ)
        goal = NC * g
        if goal < LZ:
            moved = pltpu.roll(source, (goal - start) % LZ, 1)
            third = jnp.where((lane >= goal) & (lane < goal + NC), moved, third)
        if goal + NC > LZ:
            moved = pltpu.roll(source, (goal - LZ - start) % LZ, 1)
            rest = jnp.where((lane >= max(goal - LZ, 0)) & (lane < goal + NC - LZ), moved, rest)
    second = second + jnp.where(lanes((HID, LZ)) >= 80, pltpu.roll(rest[0:HID, :], 80, 1), 0.0)
    row, lane = lax.broadcasted_iota(jnp.int32, (8, LZ), 0), lanes((8, LZ))
    bias = jnp.zeros((8, LZ), F32)
    for r in range(5):
        line = pltpu.roll(third[HID : HID + 8, :] if r < 4 else rest[HID : HID + 8, :], (96 - 32 * r) % LZ, 1)
        bias = jnp.where((row == r) & (lane >= 96), line, bias)
    blocks = ((0, third[0:HID, :]), (HID, second[0:8, :] + bias), (HID + 8, second[8:, :]))
    for at, block in blocks:
        where = slice(at, at + block.shape[0])
        grads[where, :] = block if late is None else block + late[where, :]


def late_kernel(*refs):
    faces, sent_z, prep, weights, slopes = refs[0:6], refs[6:8], refs[8:12], refs[12:15], refs[18:21]
    mob, back, outs, pres, values, adj = refs[15], refs[21], refs[22:28], refs[28:30], refs[30], refs[31]
    pots, rim_mob, scratch = refs[32], refs[33], refs[34:]
    load_halo(faces, sent_z, 0, 0, values)
    load_halo(faces, sent_z, 1, 1, adj)
    pots[...] = potential(values[...])
    network(values, HALO, prep, False, rim_mob)
    clear(back)

    def emit(t, block):
        back[0:NC, tile(t + 8)] = block

    reverse_step(values, pots, adj, (mob, rim_mob), slopes, weights, scratch, pres, emit)
    pack_tiles(back, outs, 0)


def late_grads_kernel(*refs):
    weight_grads(refs[0:2], refs[2:4], refs[4], refs[5], None)


def core_rows(half):
    core = lax.axis_index("gx") % 2
    mine = pl.multiple_of(core * half, 8)
    others = pl.multiple_of((1 - core) * half, 8)
    return pl.ds(mine, half), pl.ds(others, half)


def early_kernel(values, *refs):
    faces, sent_z, weights, mobs, rhs, slopes, late = refs[0:6], refs[6:8], refs[8:11], refs[11:13], refs[13:15], refs[15:18], refs[18]
    final, keep, give, adj = refs[20:24]
    pots, pres, room, grads, scratch = refs[24], refs[25:27], refs[27], refs[28], refs[29:]
    load_halo(faces, sent_z, 0, 0, adj)
    pots[...] = potential(values[...])

    def emit(t, block):
        final[pl.ds(t, NC, stride=OWN), :] = block

    reverse_step(values, pots, adj, mobs, slopes, weights, scratch, pres, emit)
    weight_grads(pres, rhs, grads, room, late)
    half = GROWS // 2
    mine, others = core_rows(half)
    keep[...] = grads[mine, :]
    give[...] = grads[others, :]


def finish_kernel(factor, own, other, ow1t, ob1, ow2, ob2, ow3t, ob3, grads):
    mine, others = core_rows(GROWS // 2)
    grads[mine, :] = own[...]
    grads[others, :] = other[...]
    second = grads[HID:, :] * factor
    ow3t[:, 0:LZ] = grads[0:HID, :] * factor
    ow3t[:, LZ:] = pltpu.roll(second, LZ - 80, 1)[:, 0:16]
    ow2[...] = second[:, 0:HID]
    turned = pltpu.roll(second, 64, 1).T
    ow1t[...] = turned[0:NC, :]
    ob1[...] = turned[NC : NC + 1, :]
    ob2[...] = turned[NC + 1 : NC + 2, :]
    row, lane = lax.broadcasted_iota(jnp.int32, (8, LZ), 0), lanes((8, LZ))
    bias = jnp.zeros((8, LZ), F32)
    for r in range(4):
        line = pltpu.roll(second[0:8, :], (32 + 32 * r) % LZ, 1)
        bias = jnp.where((row == r) & (lane >= 32 * r) & (lane < 32 * r + 32), line, bias)
    ob3[:, 0:LZ] = jnp.sum(bias, axis=0, keepdims=True)
    ob3[:, LZ:] = pltpu.roll(second[0:8, :], 32, 1)[4:5, 0:16]


def shape(*dims):
    return jax.ShapeDtypeStruct(dims, F32)


def face_shapes(parts):
    x, y, z = shape(96 * parts, LZ), shape(24 * parts, LZ), shape(GRP * parts, LZ)
    return (x, y, y, z, z, x)


def call(kernel, outs, args, scratch=(), aliases=None, far=()):
    return pl.pallas_call(
        kernel,
        out_shape=outs,
        in_specs=[pl.BlockSpec(memory_space=pltpu.HBM) if i in far else VM for i in range(len(args))],
        out_specs=tuple(VM for _ in outs),
        scratch_shapes=list(scratch),
        input_output_aliases=aliases or {},
        compiler_params=pltpu.CompilerParams(vmem_limit_bytes=12 << 20),
    )(*args)


def wide(tiles, rows=GRP, kind=F32):
    return pltpu.VMEM((rows, tiles * LZ), kind)


def array(tiles, rows=GRP, kind=F32):
    return jax.ShapeDtypeStruct((rows, tiles * LZ), kind)


FLOWS = (wide(24), wide(18))
BACK = FLOWS + (wide(OWN),) * 5
KEPT = (array(OWN, RHS, BF16), array(OWN, RHS, BF16), array(OWN, HID), array(OWN, HID), array(OWN, ROWS))
PRES = (array(OWN, 2 * HID, BF16), array(OWN, ROWS, BF16))
ROOM = pltpu.VMEM((2 * HID, 2 * LZ), F32)


def group_sum(value, partners):
    received = [swap(value, partner) for partner in partners]
    for other in received:
        value = value + other
    return value


def along_z(goal):
    def partner(a, b, c):
        z = goal[(a // 2) * 4 + b // 4]
        return (z // 4) * 2 + a % 2, (z % 4) * 4 + b % 4, c

    return partner


def total_over_devices(keep, give):
    value = keep + swap(give, lambda a, b, c: (a ^ 1, b, c))
    value = group_sum(value, [lambda a, b, c, k=k: (a, b, c ^ k) for k in (2, 1, 3)])
    value = group_sum(value, [lambda a, b, c, k=k: (a, b ^ k, c) for k in (2, 1, 3)])
    value = value + swap(value, lambda a, b, c: (a, b ^ 4, c))
    value = group_sum(value, (along_z((5, 4, 7, 6, 1, 0, 3, 2)), along_z((6, 3, 0, 5, 2, 7, 4, 1)), along_z((7, 2, 1, 4, 3, 6, 5, 0))))
    return value, swap(value, lambda a, b, c: (a ^ 1, b, c))


def shards(composition, cotangent, w1, b1, w2, b2, w3, b3):
    block = composition.shape
    comp = composition.reshape(NC * OWN, LZ)
    cot = cotangent.reshape(NC * OWN, LZ)
    w1t, w3t = w1.T, w3.T
    mob_shape = array(OWN, ROWS)

    sent = call(pack_kernel, face_shapes(1), (comp,))
    comp_faces = exchange(sent)
    comp_z = sent[3:5]
    inputs = (cot, w1t, b1.reshape(1, HID), w2, b2.reshape(1, HID), w3t, b3.reshape(1, MM))
    inputs = tuple(pltpu.with_memory_space_constraint(a, pltpu.HBM) for a in inputs)
    w1p, w1c, w2c, w2t, w3c, w3r, w3rt, cols, mob, values, adj, *cot_faces = call(
        prepare_kernel,
        (
            jax.ShapeDtypeStruct((HID, NC), BF16),
            jax.ShapeDtypeStruct((NC, HID), BF16),
            jax.ShapeDtypeStruct((HID, HID), BF16),
            jax.ShapeDtypeStruct((HID, HID), BF16),
            jax.ShapeDtypeStruct((ROWS, HID), BF16),
            jax.ShapeDtypeStruct((ROWS, HID), BF16),
            jax.ShapeDtypeStruct((HID, ROWS), BF16),
            shape(ROWS, LZ),
            mob_shape,
            array(TILES),
            array(TILES),
        )
        + face_shapes(1),
        (comp, *inputs),
        tuple(pltpu.VMEM(a.shape, a.dtype) for a in inputs) + (pltpu.SemaphoreType.DMA((len(inputs),)),),
        far=range(1, 1 + len(inputs)),
    )
    forward, reverse, back_weights = (w1p, w2c, w3c, cols), (w1p, w2c, w3r, cols), (w1c, w2t, w3rt)
    state, *sent, values = call(
        forward_kernel,
        (array(TILES),) + face_shapes(2) + (array(TILES),),
        (*comp_faces, *comp_z, *cot_faces, *forward, mob, values),
        (wide(TILES), wide(RIM, ROWS)) + FLOWS,
        {19: 7},
    )
    got = exchange(sent)
    mob, *kept = call(own_networks_kernel, ((mob_shape,) + KEPT) * 2, (state, values, *reverse))
    kept, comp_mob, comp_kept = kept[:5], kept[5], kept[6:]
    back, *rest = call(
        late_kernel,
        (array(TILES),) + face_shapes(1) + PRES + (array(TILES), array(TILES)),
        (*got, *sent[3:5], *reverse, *back_weights, mob, state, adj, *kept[2:]),
        (wide(TILES), wide(RIM, ROWS)) + BACK,
        {16: 9, 17: 10},
    )
    sent, pres = rest[:6], rest[6:8]
    got = exchange(sent)
    (late,) = call(late_grads_kernel, (shape(GROWS, LZ),), (*pres, *kept[:2]), (ROOM,))
    (comp_rim,) = call(rim_network_kernel, (array(RIM, ROWS),), (values, *reverse))
    final, keep, give, _ = call(
        early_kernel,
        (shape(NC * OWN, LZ), shape(GROWS // 2, LZ), shape(GROWS // 2, LZ), array(TILES)),
        (values, *got, *sent[3:5], *back_weights, comp_mob, comp_rim, *comp_kept, late, back),
        (wide(TILES), wide(OWN, 2 * HID, BF16), wide(OWN, ROWS, BF16), ROOM, pltpu.VMEM((GROWS, LZ), F32)) + BACK,
        {20: 3},
    )
    totals = total_over_devices(keep, give)
    cells = OWN * LZ * GX * GY * GZ
    factor = 1.0 / (step_size * math.sqrt(cells))
    ow1t, ob1, ow2, ob2, ow3t, ob3 = call(
        functools.partial(finish_kernel, factor),
        (shape(NC, HID), shape(1, HID), shape(HID, HID), shape(1, HID), shape(HID, MM), shape(1, MM)),
        totals,
        (pltpu.VMEM((GROWS, LZ), F32),),
    )
    return (final.reshape(block), ow1t.T, ob1.reshape(HID), ow2, ob2.reshape(HID), ow3t.T, ob3.reshape(MM))


def solution(mesh):
    in_specs = (P(None, "gx", "gy", "gz"), P(None, "gx", "gy", "gz"), P(), P(), P(), P(), P(), P())
    out_specs = (P(None, "gx", "gy", "gz"), P(), P(), P(), P(), P(), P())
    return jax.shard_map(shards, mesh=mesh, in_specs=in_specs, out_specs=out_specs, check_vma=False)
```

```python
import functools
import math

import jax
import jax.numpy as jnp
from jax import lax
from jax.experimental import pallas as pl
from jax.experimental.pallas import tpu as pltpu
from jax.sharding import PartitionSpec as P


AXES = ("gx", "gy", "gz")
GX, GY, GZ = 4, 16, 4
step_size = 0.08
cubic_coef = 0.1
diag_scale = 0.5
off_scale = 0.04

NC, HID, MM = 12, 64, 144
LX, LY, LZ = 2, 8, 128
OWN = LX * LY
GRP = 16
ROWS = NC * GRP
YM, YP, ZT = 32, 34, 36
TILES = 37
CHUNK = 1024
RIM = 21
HALO = ((0, 8, 0), (24, 32, 8), (32, 37, 16))
RHS = HID + GRP
GROWS = 128
UNROLL = 4
F32, BF16 = jnp.float32, jnp.bfloat16
VM = pl.BlockSpec(memory_space=pltpu.VMEM)


def swap(value, partner):
    pairs = []
    for a in range(GX):
        for b in range(GY):
            for c in range(GZ):
                a2, b2, c2 = partner(a, b, c)
                pairs.append(((a * GY + b) * GZ + c, (a2 * GY + b2) * GZ + c2))
    return lax.ppermute(value, AXES, pairs)


def odd_up(i, n):
    return (i + 1) % n if i % 2 else (i - 1) % n


FACE_PARTNERS = (
    lambda a, b, c: (odd_up(a, GX), b, c),
    lambda a, b, c: (a, odd_up(b, GY), c),
    lambda a, b, c: (a, b ^ 1, c),
    lambda a, b, c: (a, b, odd_up(c, GZ)),
    lambda a, b, c: (a, b, c ^ 1),
    lambda a, b, c: (a ^ 1, b, c),
)


def exchange(faces):
    return [swap(face, partner) for face, partner in zip(faces, FACE_PARTNERS)]


def parities():
    return lax.axis_index("gx") % 2, lax.axis_index("gy") % 2, lax.axis_index("gz") % 2


def lanes(shape):
    return lax.broadcasted_iota(jnp.int32, shape, len(shape) - 1)


def tile(index):
    start = index * LZ
    return pl.ds(start if isinstance(start, int) else pl.multiple_of(start, LZ), LZ)


def pack_faces(native, outs, part):
    px, py, pz = parities()
    xf, yb, ya, zb, za, xn = outs
    for ch in range(NC):
        xf[pl.ds(part * 96 + ch * 8, 8), :] = native[pl.ds(pl.multiple_of(ch * OWN + px * LY, 8), 8), :]
        xn[pl.ds(part * 96 + ch * 8, 8), :] = native[pl.ds(pl.multiple_of(ch * OWN + (1 - px) * LY, 8), 8), :]
    first = native[pl.ds(0, 24, stride=8), :]
    last = native[pl.ds(7, 24, stride=8), :]
    ya[pl.ds(part * 24, 24), :] = jnp.where(py == 0, last, first)
    yb[pl.ds(part * 24, 24), :] = jnp.where(py == 0, first, last)
    lane = lanes((NC, LZ))
    low = jnp.zeros((NC, LZ), F32)
    high = jnp.zeros((NC, LZ), F32)
    for t in range(OWN):
        block = native[pl.ds(t, NC, stride=OWN), :]
        low = jnp.where(lane == 2 * t, pltpu.roll(block, 2 * t, 1), low)
        high = jnp.where(lane == 2 * t, pltpu.roll(block, 2 * t + 1, 1), high)
    zero = jnp.zeros((GRP - NC, LZ), F32)
    za[pl.ds(part * GRP, NC), :] = jnp.where(pz == 0, high, low)
    zb[pl.ds(part * GRP, NC), :] = jnp.where(pz == 0, low, high)
    za[pl.ds(part * GRP + NC, GRP - NC), :] = zero
    zb[pl.ds(part * GRP + NC, GRP - NC), :] = zero


def load_own(native, dest):
    dest[...] = jnp.zeros((GRP, TILES * LZ), F32)
    for t in range(OWN):
        dest[0:NC, tile(8 + t)] = native[pl.ds(t, NC, stride=OWN), :]


def load_halo(faces, sent_z, part, sent_part, dest):
    px, py, pz = parities()
    xf, yb, ya, zb, za, xn = faces
    for y in range(LY):
        dest[0:NC, tile(24 * px + y)] = xf[pl.ds(part * 96 + y, NC, stride=LY), :]
        dest[0:NC, tile(24 - 24 * px + y)] = xn[pl.ds(part * 96 + y, NC, stride=LY), :]
    for x in range(LX):
        dest[0:NC, tile(YP - 2 * py + x)] = ya[pl.ds(part * 24 + x, NC, stride=LX), :]
        dest[0:NC, tile(YM + 2 * py + x)] = yb[pl.ds(part * 24 + x, NC, stride=LX), :]
    got = slice(part * GRP, part * GRP + GRP)
    own = slice(sent_part * GRP, sent_part * GRP + GRP)
    got_a, got_b = za[got, :], zb[got, :]
    own_b, own_a = sent_z[0][own, :], sent_z[1][own, :]
    even = pz == 0
    minus, plus = jnp.where(even, got_b, got_a), jnp.where(even, got_a, got_b)
    first, last = jnp.where(even, own_b, own_a), jnp.where(even, own_a, own_b)
    rim = (pltpu.roll(minus, 1, 1) + last) + (pltpu.roll(first, 33, 1) + pltpu.roll(plus, 32, 1))
    dest[:, tile(ZT)] = rim


def pack_tiles(source, outs, part):
    px, py, pz = parities()
    xf, yb, ya, zb, za, xn = outs
    for y in range(LY):
        xf[pl.ds(part * 96 + y, NC, stride=LY), :] = source[0:NC, tile(8 + 8 * px + y)]
        xn[pl.ds(part * 96 + y, NC, stride=LY), :] = source[0:NC, tile(16 - 8 * px + y)]
    for x in range(LX):
        ya[pl.ds(part * 24 + x, NC, stride=LX), :] = source[0:NC, tile(8 + x * 8 + 7 - 7 * py)]
        yb[pl.ds(part * 24 + x, NC, stride=LX), :] = source[0:NC, tile(8 + x * 8 + 7 * py)]
    lane = lanes((GRP, LZ))
    low = jnp.zeros((GRP, LZ), F32)
    high = jnp.zeros((GRP, LZ), F32)
    for t in range(OWN):
        block = source[:, tile(8 + t)]
        low = jnp.where(lane == 2 * t, pltpu.roll(block, 2 * t, 1), low)
        high = jnp.where(lane == 2 * t, pltpu.roll(block, 2 * t + 1, 1), high)
    za[pl.ds(part * GRP, GRP), :] = jnp.where(pz == 0, high, low)
    zb[pl.ds(part * GRP, GRP), :] = jnp.where(pz == 0, low, high)


def clear(dest):
    dest[...] = jnp.zeros(dest.shape, dest.dtype)


def row_tables(by_column):
    row = lax.broadcasted_iota(jnp.int32, (ROWS, MM), 0)
    entry = lax.broadcasted_iota(jnp.int32, (ROWS, MM), 1)
    g, j = row // GRP, row % GRP
    want = j * NC + g if by_column else g * NC + j
    pick = jnp.where((entry == want) & (j < NC), 1.0, 0.0).astype(F32)
    row1 = lax.broadcasted_iota(jnp.int32, (ROWS, 1), 0)
    g1, j1 = row1 // GRP, row1 % GRP
    identity = jnp.where(g1 == j1, 1.0, 0.0).astype(F32)
    scales = jnp.where(g1 == j1, diag_scale, jnp.where(j1 < NC, off_scale, 0.0)).astype(F32)
    return pick, identity, scales


def eye(size, kind=F32):
    same = lax.broadcasted_iota(jnp.int32, (size, size), 0) == lax.broadcasted_iota(jnp.int32, (size, size), 1)
    return jnp.where(same, 1.0, 0.0).astype(kind)


def dot(a, b, ca=1, cb=0, precision=None):
    return lax.dot_general(a, b, (((ca,), (cb,)), ((), ())), preferred_element_type=F32, precision=precision)


def prepare(w1t, b1, w2, b2, w3t, b3, outs):
    w1p, w1c, w2c, w2t, w3c, w3r, w3rt, cols = outs
    w1c[...] = w1t[...]
    w2c[...] = w2[...]
    w1p[...] = dot(w1t[...], eye(NC, BF16), 0, 0).astype(BF16)
    w2t[...] = dot(w2[...], eye(HID, BF16), 0, 0).astype(BF16)
    pick_c, _, _ = row_tables(True)
    pick_r, _, _ = row_tables(False)
    w3c[...] = dot(pick_c.astype(BF16), w3t[...], 1, 1).astype(BF16)
    w3r[...] = dot(pick_r.astype(BF16), w3t[...], 1, 1).astype(BF16)
    w3rt[...] = dot(w3t[...], pick_r.astype(BF16), 1, 1).astype(BF16)
    cols[:, 0:1] = jnp.sum(pick_c * b3[...], axis=1, keepdims=True)
    cols[:, 1:2] = jnp.sum(pick_r * b3[...], axis=1, keepdims=True)
    cols[0:HID, 2:3] = jnp.sum(eye(HID) * b1[...], axis=1, keepdims=True)
    cols[0:HID, 3:4] = jnp.sum(eye(HID) * b2[...], axis=1, keepdims=True)


def network(values, spans, prep, by_column, mob, keep=None):
    w1p, w2, w3p, cols = prep
    row1 = lax.broadcasted_iota(jnp.int32, (ROWS, 1), 0)
    g1, j1 = row1 // GRP, row1 % GRP
    identity = jnp.where(g1 == j1, 1.0, 0.0).astype(F32)
    scales = jnp.where(g1 == j1, diag_scale, jnp.where(j1 < NC, off_scale, 0.0)).astype(F32)
    bias1, bias2 = cols[0:HID, 2:3], cols[0:HID, 3:4]
    bias3 = cols[:, 0:1] if by_column else cols[:, 1:2]
    places = [slice(start * LZ, stop * LZ) for start, stop, _ in spans]
    ones = [jnp.tanh(dot(w1p[...], values[0:NC, at].astype(BF16)) + bias1).astype(BF16) for at in places]
    twos = [jnp.tanh(dot(w2[...], one) + bias2).astype(BF16) for one in ones]
    for (start, stop, goal), cols_at, one, two in zip(spans, places, ones, twos):
        active = jnp.tanh(dot(w3p[...], two) + bias3)
        mob[:, goal * LZ : (goal + stop - start) * LZ] = identity + scales * active
        if keep is not None:
            own = slice(goal * LZ, (goal + stop - start) * LZ)
            rhs12, rhs3, slope1, slope2, slope = keep
            width = (stop - start) * LZ
            row = lax.broadcasted_iota(jnp.int32, (GRP, width), 0)
            rhs12[0:HID, own] = one
            rhs12[HID:, own] = jnp.where(row == NC, 1.0, values[:, cols_at]).astype(BF16)
            rhs3[0:HID, own] = two
            rhs3[HID:, own] = jnp.ones((GRP, width), BF16)
            one32, two32 = one.astype(F32), two.astype(F32)
            slope1[:, own] = 1.0 - one32 * one32
            slope2[:, own] = 1.0 - two32 * two32
            slope[:, own] = (0.5 * scales) * (1.0 - active * active)


OWN_SPANS = ((8, 16, 0), (16, 24, 8))


def potential(v):
    return v + cubic_coef * v * v * v


def flow_of(lower, upper, weight):
    total = None
    for k in range(NC):
        term = (lower(k) + upper(k)) * weight[k : k + 1, :]
        total = term if total is None else total + term
    return total


def mob_rows(mob, index):
    return lambda k: mob[GRP * k : GRP * k + GRP, tile(index)]


def product(mob, index, weight):
    total = None
    for k in range(NC):
        term = mob[GRP * k : GRP * k + GRP, tile(index)] * weight[k : k + 1, :]
        total = term if total is None else total + term
    return total


def y_face(j):
    x, k = j // 9, j % 9
    low = jnp.where(k == 0, YM + x, (x + 1) * 8 + k - 1)
    high = jnp.where(k == 8, YP + x, (x + 1) * 8 + k)
    return low, high


def xy_flows(mobs, weight_of, fx, fy):
    own, halo = mobs
    for k in range(24):
        low = mob_rows(halo, k) if k < 8 else mob_rows(own, k - 8)
        high = mob_rows(own, k) if k < 16 else mob_rows(halo, k - 8)
        fx[:, tile(k)] = flow_of(low, high, weight_of(k, k + 8))
    for x in range(LX):
        for k in range(LY + 1):
            low, high = x * 8 + (7 + k), x * 8 + (8 + k)
            low_rows, high_rows = mob_rows(own, low - 8), mob_rows(own, high - 8)
            if k == 0:
                low, low_rows = YM + x, mob_rows(halo, 16 + x)
            if k == LY:
                high, high_rows = YP + x, mob_rows(halo, 18 + x)
            fy[:, tile(x * 9 + k)] = flow_of(low_rows, high_rows, weight_of(low, high))


def rim_step(source):
    here = source[:, tile(ZT)]
    return pltpu.roll(here, 96, 1) - here


def rim_ends(rim, t):
    return pltpu.roll(rim, LZ - 1 - 2 * t, 1)


def z_steps(source, rim, t, lane):
    here = source[:, tile(t + 8)]
    step = pltpu.roll(here, LZ - 1, 1) - here
    ends = rim_ends(rim, t)
    up = jnp.where(lane == LZ - 1, ends, step)
    low = jnp.where(lane == 0, ends, pltpu.roll(step, 1, 1))
    return up, low


def rim_product(mob, weight, lane):
    share = product(mob, RIM - 1, jnp.where(lane < 32, weight, pltpu.roll(weight, 32, 1)))
    return jnp.where(lane % 2 == 1, share, pltpu.roll(share, 96, 1))


def z_balance(at_up, at_low, t, rim, lane):
    ends = rim_ends(rim, t)
    from_next = jnp.where(lane == LZ - 1, ends, pltpu.roll(at_low, LZ - 1, 1))
    from_last = jnp.where(lane == 0, ends, pltpu.roll(at_up, 1, 1))
    return (at_up - at_low) + (from_next - from_last)


def pack_kernel(comp, *outs):
    pack_faces(comp, outs, 0)


def prepare_kernel(comp, *refs):
    far, outs = refs[0:7], refs[7:15]
    mob, values, adj, faces = refs[15], refs[16], refs[17], refs[18:24]
    near, sems = refs[24:31], refs[31]
    copies = [pltpu.make_async_copy(a, b, sems.at[i]) for i, (a, b) in enumerate(zip(far, near))]
    for copy in copies:
        copy.start()
    clear(values)
    clear(adj)
    for t in range(OWN):
        values[0:NC, tile(8 + t)] = comp[pl.ds(t, NC, stride=OWN), :]
    for copy in copies:
        copy.wait()
    cot, w1t, b1, w2, b2, w3t, b3 = near
    prepare(w1t, b1, w2, b2, w3t, b3, outs)
    network(values, OWN_SPANS, (outs[0], w2, outs[4], outs[7]), True, mob)
    for t in range(OWN):
        adj[0:NC, tile(8 + t)] = cot[pl.ds(t, NC, stride=OWN), :]
    pack_tiles(adj, faces, 0)


def forward_kernel(*refs):
    faces, sent_z, cot_faces, prep = refs[0:6], refs[6:8], refs[8:14], refs[14:18]
    mob, state, outs, values = refs[18], refs[20], refs[21:27], refs[27]
    pots, rim_mob, fx, fy, steps_up, steps_low, flow_up, flow_low = refs[28:]
    load_halo(faces, sent_z, 0, 0, values)
    pots[...] = potential(values[...])
    network(values, HALO, prep, True, rim_mob)
    xy_flows((mob, rim_mob), lambda low, high: 0.5 * (pots[:, tile(high)] - pots[:, tile(low)]), fx, fy)
    lane = lanes((GRP, LZ))
    rim = rim_step(pots)
    rim_flow = rim_product(rim_mob, 0.5 * rim, lane)
    clear(state)

    for t in range(OWN):
        up, low = z_steps(pots, rim, t, lane)
        steps_up[:, tile(t)], steps_low[:, tile(t)] = 0.5 * up, 0.5 * low

    def body(x, carry):
        for y in range(UNROLL):
            t = x * UNROLL + y
            flow_up[:, tile(t)] = product(mob, t, steps_up[:, tile(t)])
            flow_low[:, tile(t)] = product(mob, t, steps_low[:, tile(t)])
        return carry

    lax.fori_loop(0, OWN // UNROLL, body, 0)
    for t in range(OWN):
        at, yf = t + 8, t // LY * 9 + t % LY
        change = z_balance(flow_up[:, tile(t)], flow_low[:, tile(t)], t, rim_flow, lane)
        change = change + (fx[:, tile(at)] - fx[:, tile(at - 8)]) + (fy[:, tile(yf + 1)] - fy[:, tile(yf)])
        state[:, tile(at)] = values[:, tile(at)] + step_size * change
    pack_tiles(state, outs, 0)
    for out, face in zip(outs, cot_faces):
        out[pl.ds(face.shape[0], face.shape[0]), :] = face[...]


def own_networks_kernel(state, values, w1p, w2, w3r, cols, *outs):
    prep = (w1p, w2, w3r, cols)
    network(state, OWN_SPANS, prep, False, outs[0], outs[1:6])
    network(values, OWN_SPANS, prep, False, outs[6], outs[7:12])


def rim_network_kernel(values, w1p, w2, w3r, cols, mob, pots, zju, zjl):
    network(values, HALO, (w1p, w2, w3r, cols), False, mob)
    pots[...] = potential(values[...])
    lane = lanes((GRP, LZ))
    rim = rim_step(pots)
    for t in range(OWN):
        zju[:, tile(t)], zjl[:, tile(t)] = z_steps(pots, rim, t, lane)


def reverse_step(values, pots, adj, mobs, slopes, weights, scratch, pres, emit, jumps_ready=False):
    w1t, w2t, w3rt = weights
    slope1, slope2, slope = slopes
    pres12, pre3 = pres
    fx, fy, gpot, zju, zjl, zau, zal = scratch
    mob, rim_mob = mobs

    def jump_of(low, high):
        return pots[:, tile(high)] - pots[:, tile(low)]

    def adj_of(low, high):
        return step_size * (adj[:, tile(low)] - adj[:, tile(high)])

    xy_flows(mobs, lambda low, high: 0.5 * adj_of(low, high), fx, fy)
    lane = lanes((GRP, LZ))
    rim_jump, rim_adj = None if jumps_ready else rim_step(pots), rim_step(adj)
    rim_flow = rim_product(rim_mob, (-0.5 * step_size) * rim_adj, lane)

    def z_body(x, carry):
        for y in range(LY):
            t = x * 8 + y
            at, yf = t + 8, x * 9 + y
            if rim_jump is not None:
                zju[:, tile(t)], zjl[:, tile(t)] = z_steps(pots, rim_jump, t, lane)
            up, low = z_steps(adj, rim_adj, t, lane)
            zau[:, tile(t)], zal[:, tile(t)] = -step_size * up, -step_size * low
            at_up = product(mob, t, (-0.5 * step_size) * up)
            at_low = product(mob, t, (-0.5 * step_size) * low)
            balance = z_balance(at_up, at_low, t, rim_flow, lane)
            gpot[:, tile(t)] = (
                (fx[:, tile(at - 8)] - fx[:, tile(at)]) + (fy[:, tile(yf)] - fy[:, tile(yf + 1)]) - balance
            )
        return carry

    lax.fori_loop(0, 2, z_body, 0)

    def cell_body(i, carry):
        for t in (2 * i, 2 * i + 1):
            at = t + 8
            x, y = t // LY, t % LY
            y_low = jnp.where(y == 0, YM + x, at - 1)
            y_high = jnp.where(y == LY - 1, YP + x, at + 1)
            z = tile(t)
            pairs = (
                (adj_of(at - 8, at), jump_of(at - 8, at)),
                (adj_of(at, at + 8), jump_of(at, at + 8)),
                (adj_of(y_low, at), jump_of(y_low, at)),
                (adj_of(at, y_high), jump_of(at, y_high)),
                (zal[:, z], zjl[:, z]),
                (zau[:, z], zju[:, z]),
            )
            for k in range(NC):
                total = None
                for a, j in pairs:
                    term = a[k : k + 1, :] * j
                    total = term if total is None else total + term
                rows = slice(GRP * k, GRP * k + GRP)
                pre3[rows, z] = (total * slope[rows, z]).astype(BF16)
        return carry

    lax.fori_loop(0, OWN // 2, cell_body, 0)
    for at in range(0, OWN * LZ, CHUNK):
        own = slice(at, at + CHUNK)
        two = (dot(w3rt[...], pre3[:, own]) * slope2[:, own]).astype(BF16)
        one = (dot(w2t[...], two) * slope1[:, own]).astype(BF16)
        net = dot(w1t[...], one)
        pres12[0:HID, own] = one
        pres12[HID:, own] = two
        for k in range(CHUNK // LZ):
            t = at // LZ + k
            v = values[0:NC, tile(t + 8)]
            emit(
                t,
                adj[0:NC, tile(t + 8)]
                + gpot[0:NC, tile(t)] * (1.0 + 3.0 * cubic_coef * v * v)
                + net[:, k * LZ : (k + 1) * LZ],
            )


def weight_grads(pres, rhs, grads, room, late):
    pres12, pre3 = pres
    rhs12, rhs3 = rhs
    room[...] = jnp.zeros((2 * HID, 2 * LZ), F32)
    room[:, 0:RHS] = dot(pres12[...], rhs12[...], 1, 1)
    lane = lanes((HID, LZ))
    upper, lower = room[HID:, 0:LZ], room[0:HID, 0:LZ]
    second = jnp.where(lane < HID, upper, lower)
    second = jnp.where(lane == HID + NC + 1, pltpu.roll(upper, 1, 1), second)
    room[0:RHS, 0:ROWS] = dot(rhs3[...], pre3[...], 1, 1)
    left, right = room[0:RHS, 0:LZ], room[0:RHS, LZ:]
    lane = lanes((RHS, LZ))
    third, rest = jnp.zeros((RHS, LZ), F32), jnp.zeros((RHS, LZ), F32)
    for g in range(NC):
        source, start = (left, GRP * g) if g < 8 else (right, GRP * g - LZ)
        goal = NC * g
        if goal < LZ:
            moved = pltpu.roll(source, (goal - start) % LZ, 1)
            third = jnp.where((lane >= goal) & (lane < goal + NC), moved, third)
        if goal + NC > LZ:
            moved = pltpu.roll(source, (goal - LZ - start) % LZ, 1)
            rest = jnp.where((lane >= max(goal - LZ, 0)) & (lane < goal + NC - LZ), moved, rest)
    second = second + jnp.where(lanes((HID, LZ)) >= 80, pltpu.roll(rest[0:HID, :], 80, 1), 0.0)
    row, lane = lax.broadcasted_iota(jnp.int32, (8, LZ), 0), lanes((8, LZ))
    bias = jnp.zeros((8, LZ), F32)
    for r in range(5):
        line = pltpu.roll(third[HID : HID + 8, :] if r < 4 else rest[HID : HID + 8, :], (96 - 32 * r) % LZ, 1)
        bias = jnp.where((row == r) & (lane >= 96), line, bias)
    blocks = ((0, third[0:HID, :]), (HID, second[0:8, :] + bias), (HID + 8, second[8:, :]))
    for at, block in blocks:
        where = slice(at, at + block.shape[0])
        grads[where, :] = block if late is None else block + late[where, :]


def late_kernel(*refs):
    faces, sent_z, prep, weights, slopes = refs[0:6], refs[6:8], refs[8:12], refs[12:15], refs[18:21]
    mob, back, outs, pres, values, adj = refs[15], refs[21], refs[22:28], refs[28:30], refs[30], refs[31]
    pots, rim_mob, scratch = refs[32], refs[33], refs[34:]
    load_halo(faces, sent_z, 0, 0, values)
    load_halo(faces, sent_z, 1, 1, adj)
    pots[...] = potential(values[...])
    network(values, HALO, prep, False, rim_mob)
    clear(back)

    def emit(t, block):
        back[0:NC, tile(t + 8)] = block

    reverse_step(values, pots, adj, (mob, rim_mob), slopes, weights, scratch, pres, emit)
    pack_tiles(back, outs, 0)


def late_grads_kernel(*refs):
    weight_grads(refs[0:2], refs[2:4], refs[4], refs[5], None)


def core_rows(half):
    core = lax.axis_index("gx") % 2
    mine = pl.multiple_of(core * half, 8)
    others = pl.multiple_of((1 - core) * half, 8)
    return pl.ds(mine, half), pl.ds(others, half)


def early_kernel(values, *refs):
    faces, sent_z, weights, mobs, rhs, slopes, late = refs[0:6], refs[6:8], refs[8:11], refs[11:13], refs[13:15], refs[15:18], refs[18]
    pots, zju, zjl = refs[20:23]
    final, keep, give, adj = refs[23:27]
    near, sem, pres, room, grads, scratch = refs[27], refs[28], refs[29:31], refs[31], refs[32], refs[33:]
    load_halo(faces, sent_z, 0, 0, adj)

    def emit(t, block):
        near[pl.ds(t, NC, stride=OWN), :] = block

    fx, fy, gpot, zau, zal = scratch
    scratch = (fx, fy, gpot, zju, zjl, zau, zal)
    reverse_step(values, pots, adj, mobs, slopes, weights, scratch, pres, emit, jumps_ready=True)
    copy = pltpu.make_async_copy(near, final, sem)
    copy.start()
    weight_grads(pres, rhs, grads, room, late)
    half = GROWS // 2
    mine, others = core_rows(half)
    keep[...] = grads[mine, :]
    give[...] = grads[others, :]
    copy.wait()


def finish_kernel(factor, own, other, ow1t, ob1, ow2, ob2, ow3t, ob3, grads):
    mine, others = core_rows(GROWS // 2)
    grads[mine, :] = own[...]
    grads[others, :] = other[...]
    second = grads[HID:, :] * factor
    ow3t[:, 0:LZ] = grads[0:HID, :] * factor
    ow3t[:, LZ:] = pltpu.roll(second, LZ - 80, 1)[:, 0:16]
    ow2[...] = second[:, 0:HID]
    turned = pltpu.roll(second, 64, 1).T
    ow1t[...] = turned[0:NC, :]
    ob1[...] = turned[NC : NC + 1, :]
    ob2[...] = turned[NC + 1 : NC + 2, :]
    row, lane = lax.broadcasted_iota(jnp.int32, (8, LZ), 0), lanes((8, LZ))
    bias = jnp.zeros((8, LZ), F32)
    for r in range(4):
        line = pltpu.roll(second[0:8, :], (32 + 32 * r) % LZ, 1)
        bias = jnp.where((row == r) & (lane >= 32 * r) & (lane < 32 * r + 32), line, bias)
    ob3[:, 0:LZ] = jnp.sum(bias, axis=0, keepdims=True)
    ob3[:, LZ:] = pltpu.roll(second[0:8, :], 32, 1)[4:5, 0:16]


def shape(*dims):
    return jax.ShapeDtypeStruct(dims, F32)


def face_shapes(parts):
    x, y, z = shape(96 * parts, LZ), shape(24 * parts, LZ), shape(GRP * parts, LZ)
    return (x, y, y, z, z, x)


def call(kernel, outs, args, scratch=(), aliases=None, far=(), far_out=()):
    return pl.pallas_call(
        kernel,
        out_shape=outs,
        in_specs=[pl.BlockSpec(memory_space=pltpu.HBM) if i in far else VM for i in range(len(args))],
        out_specs=tuple(pl.BlockSpec(memory_space=pltpu.HBM) if i in far_out else VM for i in range(len(outs))),
        scratch_shapes=list(scratch),
        input_output_aliases=aliases or {},
        compiler_params=pltpu.CompilerParams(vmem_limit_bytes=12 << 20),
    )(*args)


def wide(tiles, rows=GRP, kind=F32):
    return pltpu.VMEM((rows, tiles * LZ), kind)


def array(tiles, rows=GRP, kind=F32):
    return jax.ShapeDtypeStruct((rows, tiles * LZ), kind)


FLOWS = (wide(24), wide(18))
EARLY = FLOWS + (wide(OWN),) * 3
BACK = FLOWS + (wide(OWN),) * 5
KEPT = (array(OWN, RHS, BF16), array(OWN, RHS, BF16), array(OWN, HID), array(OWN, HID), array(OWN, ROWS))
PRES = (array(OWN, 2 * HID, BF16), array(OWN, ROWS, BF16))
ROOM = pltpu.VMEM((2 * HID, 2 * LZ), F32)


def group_sum(value, partners):
    received = [swap(value, partner) for partner in partners]
    for other in received:
        value = value + other
    return value


def along_z(goal):
    def partner(a, b, c):
        z = goal[(a // 2) * 4 + b // 4]
        return (z // 4) * 2 + a % 2, (z % 4) * 4 + b % 4, c

    return partner


def total_over_devices(keep, give):
    value = keep + swap(give, lambda a, b, c: (a ^ 1, b, c))
    value = group_sum(value, [lambda a, b, c, k=k: (a, b, c ^ k) for k in (2, 1, 3)])
    value = group_sum(value, [lambda a, b, c, k=k: (a, b ^ k, c) for k in (2, 1, 3)])
    value = value + swap(value, lambda a, b, c: (a, b ^ 4, c))
    value = group_sum(value, (along_z((5, 4, 7, 6, 1, 0, 3, 2)), along_z((6, 3, 0, 5, 2, 7, 4, 1)), along_z((7, 2, 1, 4, 3, 6, 5, 0))))
    return value, swap(value, lambda a, b, c: (a ^ 1, b, c))


def shards(composition, cotangent, w1, b1, w2, b2, w3, b3):
    block = composition.shape
    comp = composition.reshape(NC * OWN, LZ)
    cot = cotangent.reshape(NC * OWN, LZ)
    w1t, w3t = w1.T, w3.T
    mob_shape = array(OWN, ROWS)

    sent = call(pack_kernel, face_shapes(1), (comp,))
    comp_faces = exchange(sent)
    comp_z = sent[3:5]
    inputs = (cot, w1t, b1.reshape(1, HID), w2, b2.reshape(1, HID), w3t, b3.reshape(1, MM))
    inputs = tuple(pltpu.with_memory_space_constraint(a, pltpu.HBM) for a in inputs)
    w1p, w1c, w2c, w2t, w3c, w3r, w3rt, cols, mob, values, adj, *cot_faces = call(
        prepare_kernel,
        (
            jax.ShapeDtypeStruct((HID, NC), BF16),
            jax.ShapeDtypeStruct((NC, HID), BF16),
            jax.ShapeDtypeStruct((HID, HID), BF16),
            jax.ShapeDtypeStruct((HID, HID), BF16),
            jax.ShapeDtypeStruct((ROWS, HID), BF16),
            jax.ShapeDtypeStruct((ROWS, HID), BF16),
            jax.ShapeDtypeStruct((HID, ROWS), BF16),
            shape(ROWS, LZ),
            mob_shape,
            array(TILES),
            array(TILES),
        )
        + face_shapes(1),
        (comp, *inputs),
        tuple(pltpu.VMEM(a.shape, a.dtype) for a in inputs) + (pltpu.SemaphoreType.DMA((len(inputs),)),),
        far=range(1, 1 + len(inputs)),
    )
    forward, reverse, back_weights = (w1p, w2c, w3c, cols), (w1p, w2c, w3r, cols), (w1c, w2t, w3rt)
    state, *sent, values = call(
        forward_kernel,
        (array(TILES),) + face_shapes(2) + (array(TILES),),
        (*comp_faces, *comp_z, *cot_faces, *forward, mob, values),
        (wide(TILES), wide(RIM, ROWS)) + FLOWS + (wide(OWN),) * 4,
        {19: 7},
    )
    got = exchange(sent)
    mob, *kept = call(own_networks_kernel, ((mob_shape,) + KEPT) * 2, (state, values, *reverse))
    kept, comp_mob, comp_kept = kept[:5], kept[5], kept[6:]
    back, *rest = call(
        late_kernel,
        (array(TILES),) + face_shapes(1) + PRES + (array(TILES), array(TILES)),
        (*got, *sent[3:5], *reverse, *back_weights, mob, state, adj, *kept[2:]),
        (wide(TILES), wide(RIM, ROWS)) + BACK,
        {16: 9, 17: 10},
    )
    sent, pres = rest[:6], rest[6:8]
    got = exchange(sent)
    (late,) = call(late_grads_kernel, (shape(GROWS, LZ),), (*pres, *kept[:2]), (ROOM,))
    comp_rim, *jumps = call(rim_network_kernel, (array(RIM, ROWS), array(TILES), array(OWN), array(OWN)), (values, *reverse))
    final, keep, give, _ = call(
        early_kernel,
        (shape(NC * OWN, LZ), shape(GROWS // 2, LZ), shape(GROWS // 2, LZ), array(TILES)),
        (values, *got, *sent[3:5], *back_weights, comp_mob, comp_rim, *comp_kept, late, back, *jumps),
        (
            pltpu.VMEM((NC * OWN, LZ), F32),
            pltpu.SemaphoreType.DMA,
            wide(OWN, 2 * HID, BF16),
            wide(OWN, ROWS, BF16),
            ROOM,
            pltpu.VMEM((GROWS, LZ), F32),
        )
        + EARLY,
        {20: 3},
        far_out=(0,),
    )
    totals = total_over_devices(keep, give)
    cells = OWN * LZ * GX * GY * GZ
    factor = 1.0 / (step_size * math.sqrt(cells))
    ow1t, ob1, ow2, ob2, ow3t, ob3 = call(
        functools.partial(finish_kernel, factor),
        (shape(NC, HID), shape(1, HID), shape(HID, HID), shape(1, HID), shape(HID, MM), shape(1, MM)),
        totals,
        (pltpu.VMEM((GROWS, LZ), F32),),
    )
    return (final.reshape(block), ow1t.T, ob1.reshape(HID), ow2, ob2.reshape(HID), ow3t.T, ob3.reshape(MM))


def solution(mesh):
    in_specs = (P(None, "gx", "gy", "gz"), P(None, "gx", "gy", "gz"), P(), P(), P(), P(), P(), P())
    out_specs = (P(None, "gx", "gy", "gz"), P(), P(), P(), P(), P(), P())
    return jax.shard_map(shards, mesh=mesh, in_specs=in_specs, out_specs=out_specs, check_vma=False)
```

```python
import functools
import math

import jax
import jax.numpy as jnp
from jax import lax
from jax.experimental import pallas as pl
from jax.experimental.pallas import tpu as pltpu
from jax.sharding import PartitionSpec as P


AXES = ("gx", "gy", "gz")
GX, GY, GZ = 4, 16, 4
step_size = 0.08
cubic_coef = 0.1
diag_scale = 0.5
off_scale = 0.04

NC, HID, MM = 12, 64, 144
LX, LY, LZ = 2, 8, 128
OWN = LX * LY
GRP = 16
ROWS = NC * GRP
YM, YP, ZT = 32, 34, 36
TILES = 37
CHUNK = 1024
RIM = 21
HALO = ((0, 8, 0), (24, 32, 8), (32, 37, 16))
RHS = HID + GRP
GROWS = 128
UNROLL = 4
F32, BF16 = jnp.float32, jnp.bfloat16
VM = pl.BlockSpec(memory_space=pltpu.VMEM)


def swap(value, partner):
    pairs = []
    for a in range(GX):
        for b in range(GY):
            for c in range(GZ):
                a2, b2, c2 = partner(a, b, c)
                pairs.append(((a * GY + b) * GZ + c, (a2 * GY + b2) * GZ + c2))
    return lax.ppermute(value, AXES, pairs)


def odd_up(i, n):
    return (i + 1) % n if i % 2 else (i - 1) % n


FACE_PARTNERS = (
    lambda a, b, c: (odd_up(a, GX), b, c),
    lambda a, b, c: (a, odd_up(b, GY), c),
    lambda a, b, c: (a, b ^ 1, c),
    lambda a, b, c: (a, b, odd_up(c, GZ)),
    lambda a, b, c: (a, b, c ^ 1),
    lambda a, b, c: (a ^ 1, b, c),
)


def exchange(faces):
    return [swap(face, partner) for face, partner in zip(faces, FACE_PARTNERS)]


def parities():
    return lax.axis_index("gx") % 2, lax.axis_index("gy") % 2, lax.axis_index("gz") % 2


def lanes(shape):
    return lax.broadcasted_iota(jnp.int32, shape, len(shape) - 1)


def tile(index):
    start = index * LZ
    return pl.ds(start if isinstance(start, int) else pl.multiple_of(start, LZ), LZ)


def pack_faces(native, outs, part):
    px, py, pz = parities()
    xf, yb, ya, zb, za, xn = outs
    for ch in range(NC):
        xf[pl.ds(part * 96 + ch * 8, 8), :] = native[pl.ds(pl.multiple_of(ch * OWN + px * LY, 8), 8), :]
        xn[pl.ds(part * 96 + ch * 8, 8), :] = native[pl.ds(pl.multiple_of(ch * OWN + (1 - px) * LY, 8), 8), :]
    first = native[pl.ds(0, 24, stride=8), :]
    last = native[pl.ds(7, 24, stride=8), :]
    ya[pl.ds(part * 24, 24), :] = jnp.where(py == 0, last, first)
    yb[pl.ds(part * 24, 24), :] = jnp.where(py == 0, first, last)
    lane = lanes((NC, LZ))
    low = jnp.zeros((NC, LZ), F32)
    high = jnp.zeros((NC, LZ), F32)
    for t in range(OWN):
        block = native[pl.ds(t, NC, stride=OWN), :]
        low = jnp.where(lane == 2 * t, pltpu.roll(block, 2 * t, 1), low)
        high = jnp.where(lane == 2 * t, pltpu.roll(block, 2 * t + 1, 1), high)
    zero = jnp.zeros((GRP - NC, LZ), F32)
    za[pl.ds(part * GRP, NC), :] = jnp.where(pz == 0, high, low)
    zb[pl.ds(part * GRP, NC), :] = jnp.where(pz == 0, low, high)
    za[pl.ds(part * GRP + NC, GRP - NC), :] = zero
    zb[pl.ds(part * GRP + NC, GRP - NC), :] = zero


def load_own(native, dest):
    dest[...] = jnp.zeros((GRP, TILES * LZ), F32)
    for t in range(OWN):
        dest[0:NC, tile(8 + t)] = native[pl.ds(t, NC, stride=OWN), :]


def load_halo(faces, sent_z, part, sent_part, dest):
    px, py, pz = parities()
    xf, yb, ya, zb, za, xn = faces
    for y in range(LY):
        dest[0:NC, tile(24 * px + y)] = xf[pl.ds(part * 96 + y, NC, stride=LY), :]
        dest[0:NC, tile(24 - 24 * px + y)] = xn[pl.ds(part * 96 + y, NC, stride=LY), :]
    for x in range(LX):
        dest[0:NC, tile(YP - 2 * py + x)] = ya[pl.ds(part * 24 + x, NC, stride=LX), :]
        dest[0:NC, tile(YM + 2 * py + x)] = yb[pl.ds(part * 24 + x, NC, stride=LX), :]
    got = slice(part * GRP, part * GRP + GRP)
    own = slice(sent_part * GRP, sent_part * GRP + GRP)
    got_a, got_b = za[got, :], zb[got, :]
    own_b, own_a = sent_z[0][own, :], sent_z[1][own, :]
    even = pz == 0
    minus, plus = jnp.where(even, got_b, got_a), jnp.where(even, got_a, got_b)
    first, last = jnp.where(even, own_b, own_a), jnp.where(even, own_a, own_b)
    rim = (pltpu.roll(minus, 1, 1) + last) + (pltpu.roll(first, 33, 1) + pltpu.roll(plus, 32, 1))
    dest[:, tile(ZT)] = rim


def pack_tiles(source, outs, part):
    px, py, pz = parities()
    xf, yb, ya, zb, za, xn = outs
    for y in range(LY):
        xf[pl.ds(part * 96 + y, NC, stride=LY), :] = source[0:NC, tile(8 + 8 * px + y)]
        xn[pl.ds(part * 96 + y, NC, stride=LY), :] = source[0:NC, tile(16 - 8 * px + y)]
    for x in range(LX):
        ya[pl.ds(part * 24 + x, NC, stride=LX), :] = source[0:NC, tile(8 + x * 8 + 7 - 7 * py)]
        yb[pl.ds(part * 24 + x, NC, stride=LX), :] = source[0:NC, tile(8 + x * 8 + 7 * py)]
    lane = lanes((GRP, LZ))
    low = jnp.zeros((GRP, LZ), F32)
    high = jnp.zeros((GRP, LZ), F32)
    for t in range(OWN):
        block = source[:, tile(8 + t)]
        low = jnp.where(lane == 2 * t, pltpu.roll(block, 2 * t, 1), low)
        high = jnp.where(lane == 2 * t, pltpu.roll(block, 2 * t + 1, 1), high)
    za[pl.ds(part * GRP, GRP), :] = jnp.where(pz == 0, high, low)
    zb[pl.ds(part * GRP, GRP), :] = jnp.where(pz == 0, low, high)


def clear(dest):
    dest[...] = jnp.zeros(dest.shape, dest.dtype)


def row_tables(by_column):
    row = lax.broadcasted_iota(jnp.int32, (ROWS, MM), 0)
    entry = lax.broadcasted_iota(jnp.int32, (ROWS, MM), 1)
    g, j = row // GRP, row % GRP
    want = j * NC + g if by_column else g * NC + j
    pick = jnp.where((entry == want) & (j < NC), 1.0, 0.0).astype(F32)
    row1 = lax.broadcasted_iota(jnp.int32, (ROWS, 1), 0)
    g1, j1 = row1 // GRP, row1 % GRP
    identity = jnp.where(g1 == j1, 1.0, 0.0).astype(F32)
    scales = jnp.where(g1 == j1, diag_scale, jnp.where(j1 < NC, off_scale, 0.0)).astype(F32)
    return pick, identity, scales


def eye(size, kind=F32):
    same = lax.broadcasted_iota(jnp.int32, (size, size), 0) == lax.broadcasted_iota(jnp.int32, (size, size), 1)
    return jnp.where(same, 1.0, 0.0).astype(kind)


def dot(a, b, ca=1, cb=0, precision=None):
    return lax.dot_general(a, b, (((ca,), (cb,)), ((), ())), preferred_element_type=F32, precision=precision)


def prepare(w1t, b1, w2, b2, w3t, b3, outs):
    w1p, w1c, w2c, w2t, w3c, w3r, w3rt, cols = outs
    w1c[...] = w1t[...]
    w2c[...] = w2[...]
    w1p[...] = dot(w1t[...], eye(NC, BF16), 0, 0).astype(BF16)
    w2t[...] = dot(w2[...], eye(HID, BF16), 0, 0).astype(BF16)
    pick_c, _, _ = row_tables(True)
    pick_r, _, _ = row_tables(False)
    w3c[...] = dot(pick_c.astype(BF16), w3t[...], 1, 1).astype(BF16)
    w3r[...] = dot(pick_r.astype(BF16), w3t[...], 1, 1).astype(BF16)
    w3rt[...] = dot(w3t[...], pick_r.astype(BF16), 1, 1).astype(BF16)
    cols[:, 0:1] = jnp.sum(pick_c * b3[...], axis=1, keepdims=True)
    cols[:, 1:2] = jnp.sum(pick_r * b3[...], axis=1, keepdims=True)
    cols[0:HID, 2:3] = jnp.sum(eye(HID) * b1[...], axis=1, keepdims=True)
    cols[0:HID, 3:4] = jnp.sum(eye(HID) * b2[...], axis=1, keepdims=True)


def network(values, spans, prep, by_column, mob, keep=None):
    w1p, w2, w3p, cols = prep
    row1 = lax.broadcasted_iota(jnp.int32, (ROWS, 1), 0)
    g1, j1 = row1 // GRP, row1 % GRP
    identity = jnp.where(g1 == j1, 1.0, 0.0).astype(F32)
    scales = jnp.where(g1 == j1, diag_scale, jnp.where(j1 < NC, off_scale, 0.0)).astype(F32)
    bias1, bias2 = cols[0:HID, 2:3], cols[0:HID, 3:4]
    bias3 = cols[:, 0:1] if by_column else cols[:, 1:2]
    places = [slice(start * LZ, stop * LZ) for start, stop, _ in spans]
    ones = [jnp.tanh(dot(w1p[...], values[0:NC, at].astype(BF16)) + bias1).astype(BF16) for at in places]
    twos = [jnp.tanh(dot(w2[...], one) + bias2).astype(BF16) for one in ones]
    for (start, stop, goal), cols_at, one, two in zip(spans, places, ones, twos):
        active = jnp.tanh(dot(w3p[...], two) + bias3)
        mob[:, goal * LZ : (goal + stop - start) * LZ] = identity + scales * active
        if keep is not None:
            own = slice(goal * LZ, (goal + stop - start) * LZ)
            rhs12, rhs3, slope1, slope2, slope = keep
            width = (stop - start) * LZ
            row = lax.broadcasted_iota(jnp.int32, (GRP, width), 0)
            rhs12[0:HID, own] = one
            rhs12[HID:, own] = jnp.where(row == NC, 1.0, values[:, cols_at]).astype(BF16)
            rhs3[0:HID, own] = two
            rhs3[HID:, own] = jnp.ones((GRP, width), BF16)
            one32, two32 = one.astype(F32), two.astype(F32)
            slope1[:, own] = 1.0 - one32 * one32
            slope2[:, own] = 1.0 - two32 * two32
            slope[:, own] = (0.5 * scales) * (1.0 - active * active)


OWN_SPANS = ((8, 16, 0), (16, 24, 8))


def potential(v):
    return v + cubic_coef * v * v * v


def flow_of(lower, upper, weight):
    total = None
    for k in range(NC):
        term = (lower(k) + upper(k)) * weight[k : k + 1, :]
        total = term if total is None else total + term
    return total


def mob_rows(mob, index):
    return lambda k: mob[GRP * k : GRP * k + GRP, tile(index)]


def product(mob, index, weight):
    total = None
    for k in range(NC):
        term = mob[GRP * k : GRP * k + GRP, tile(index)] * weight[k : k + 1, :]
        total = term if total is None else total + term
    return total


def y_face(j):
    x, k = j // 9, j % 9
    low = jnp.where(k == 0, YM + x, (x + 1) * 8 + k - 1)
    high = jnp.where(k == 8, YP + x, (x + 1) * 8 + k)
    return low, high


def step_between(source, factor):
    return lambda low, high: factor * (source[:, tile(high)] - source[:, tile(low)])


def own_flows(mob, source, factor, outs):
    fx, fy, flow_up, flow_low, step_up, step_low = outs
    weight_of = step_between(source, factor)
    for k in range(8):
        fx[:, tile(k)] = flow_of(mob_rows(mob, k), mob_rows(mob, k + 8), weight_of(k + 8, k + 16))
    for x in range(LX):
        for k in range(LY - 1):
            at = x * 8 + k
            fy[:, tile(x * 7 + k)] = flow_of(mob_rows(mob, at), mob_rows(mob, at + 1), weight_of(at + 8, at + 9))

    def z_body(i, carry):
        for k in range(8):
            t = i * 8 + k
            here = source[:, tile(t + 8)]
            up = pltpu.roll(here, LZ - 1, 1) - here
            low = pltpu.roll(up, 1, 1)
            flow = product(mob, t, factor * up) + pltpu.roll(product(mob, t, factor * low), LZ - 1, 1)
            flow_up[:, tile(t)], flow_low[:, tile(t)] = flow, pltpu.roll(flow, 1, 1)
            step_up[:, tile(t)], step_low[:, tile(t)] = up, low
        return carry

    lax.fori_loop(0, 2, z_body, 0)


def halo_flows(mobs, source, factor, fx, fy):
    own, halo = mobs
    weight_of = step_between(source, factor)
    for y in range(LY):
        fx[:, tile(y)] = flow_of(mob_rows(halo, y), mob_rows(own, y), weight_of(y, y + 8))
        fx[:, tile(y + 8)] = flow_of(mob_rows(own, y + 8), mob_rows(halo, y + 8), weight_of(y + 16, y + 24))
    for x in range(LX):
        first, last = x * 8, x * 8 + 7
        fy[:, tile(2 * x)] = flow_of(mob_rows(halo, 16 + x), mob_rows(own, first), weight_of(YM + x, first + 8))
        fy[:, tile(2 * x + 1)] = flow_of(mob_rows(own, last), mob_rows(halo, 18 + x), weight_of(last + 8, YP + x))


def rim_flow_of(mob, rim, factor, lane):
    weight = factor * rim
    share = product(mob, RIM - 1, jnp.where(lane < 32, weight, pltpu.roll(weight, 32, 1)))
    return share + pltpu.roll(share, 96, 1)


def balance(t, own, halo, rim_flow, lane):
    fx, fy, flow_up, flow_low = own
    hx, hy = halo
    x, y = t // LY, t % LY
    x_low, x_up = (hx[:, tile(y)], fx[:, tile(y)]) if x == 0 else (fx[:, tile(y)], hx[:, tile(8 + y)])
    y_low = hy[:, tile(2 * x)] if y == 0 else fy[:, tile(x * 7 + y - 1)]
    y_up = hy[:, tile(2 * x + 1)] if y == LY - 1 else fy[:, tile(x * 7 + y)]
    ends = rim_ends(rim_flow, t)
    z_up = jnp.where(lane == LZ - 1, ends, flow_up[:, tile(t)])
    z_low = jnp.where(lane == 0, ends, flow_low[:, tile(t)])
    return (x_up - x_low) + (y_up - y_low) + (z_up - z_low)


def rim_step(source):
    here = source[:, tile(ZT)]
    return pltpu.roll(here, 96, 1) - here


def rim_ends(rim, t):
    return pltpu.roll(rim, LZ - 1 - 2 * t, 1)


def z_steps(source, rim, t, lane):
    here = source[:, tile(t + 8)]
    step = pltpu.roll(here, LZ - 1, 1) - here
    ends = rim_ends(rim, t)
    up = jnp.where(lane == LZ - 1, ends, step)
    low = jnp.where(lane == 0, ends, pltpu.roll(step, 1, 1))
    return up, low


def pack_kernel(comp, *outs):
    pack_faces(comp, outs, 0)


def prepare_kernel(comp, *refs):
    far, outs = refs[0:7], refs[7:15]
    mob, values, adj, faces, flows = refs[15], refs[16], refs[17], refs[18:24], refs[24:28]
    near, sems, pots, steps = refs[28:35], refs[35], refs[36], refs[37:39]
    copies = [pltpu.make_async_copy(a, b, sems.at[i]) for i, (a, b) in enumerate(zip(far, near))]
    for copy in copies:
        copy.start()
    clear(values)
    clear(adj)
    for t in range(OWN):
        values[0:NC, tile(8 + t)] = comp[pl.ds(t, NC, stride=OWN), :]
    for copy in copies:
        copy.wait()
    cot, w1t, b1, w2, b2, w3t, b3 = near
    prepare(w1t, b1, w2, b2, w3t, b3, outs)
    network(values, OWN_SPANS, (outs[0], w2, outs[4], outs[7]), True, mob)
    for t in range(OWN):
        adj[0:NC, tile(8 + t)] = cot[pl.ds(t, NC, stride=OWN), :]
    pack_tiles(adj, faces, 0)
    own = slice(8 * LZ, 24 * LZ)
    pots[:, own] = potential(values[:, own])
    own_flows(mob, pots, 0.5, (*flows, *steps))


def forward_kernel(*refs):
    faces, sent_z, cot_faces, prep = refs[0:6], refs[6:8], refs[8:14], refs[14:18]
    mob, flows, state, outs, values = refs[18], refs[20:24], refs[24], refs[25:31], refs[31]
    pots, rim_mob, hx, hy = refs[32:]
    load_halo(faces, sent_z, 0, 0, values)
    pots[...] = potential(values[...])
    network(values, HALO, prep, True, rim_mob)
    halo_flows((mob, rim_mob), pots, 0.5, hx, hy)
    lane = lanes((GRP, LZ))
    rim_flow = rim_flow_of(rim_mob, rim_step(pots), 0.5, lane)
    clear(state)
    for t in range(OWN):
        at = t + 8
        state[:, tile(at)] = values[:, tile(at)] + step_size * balance(t, flows, (hx, hy), rim_flow, lane)
    pack_tiles(state, outs, 0)
    for out, face in zip(outs, cot_faces):
        out[pl.ds(face.shape[0], face.shape[0]), :] = face[...]


def own_networks_kernel(state, values, adj, w1p, w2, w3r, cols, *refs):
    outs, flows, jumps, pots = refs[0:12], refs[12:18], refs[18:20], refs[20]
    prep = (w1p, w2, w3r, cols)
    network(state, OWN_SPANS, prep, False, outs[0], outs[1:6])
    network(values, OWN_SPANS, prep, False, outs[6], outs[7:12])
    own_flows(outs[0], adj, -0.5 * step_size, flows)
    for t in range(OWN):
        here = potential(state[:, tile(t + 8)])
        step = pltpu.roll(here, LZ - 1, 1) - here
        jumps[0][:, tile(t)], jumps[1][:, tile(t)] = step, pltpu.roll(step, 1, 1)


def rim_network_kernel(values, back, own_mob, w1p, w2, w3r, cols, mob, pots, *refs):
    jumps, flows = refs[0:2], refs[2:8]
    network(values, HALO, (w1p, w2, w3r, cols), False, mob)
    pots[...] = potential(values[...])
    lane = lanes((GRP, LZ))
    rim = rim_step(pots)
    for t in range(OWN):
        jumps[0][:, tile(t)], jumps[1][:, tile(t)] = z_steps(pots, rim, t, lane)
    own_flows(own_mob, back, -0.5 * step_size, flows)


def reverse_step(values, pots, adj, mobs, slopes, weights, flows, jumps, scratch, pres, emit, jumps_ready):
    w1t, w2t, w3rt = weights
    slope1, slope2, slope = slopes
    pres12, pre3 = pres
    hx, hy, gpot, zau, zal, zju, zjl = scratch

    def jump_of(low, high):
        return pots[:, tile(high)] - pots[:, tile(low)]

    def adj_of(low, high):
        return step_size * (adj[:, tile(low)] - adj[:, tile(high)])

    halo_flows(mobs, adj, -0.5 * step_size, hx, hy)
    lane = lanes((GRP, LZ))
    rim_jump, rim_adj = None if jumps_ready else rim_step(pots), rim_step(adj)
    rim_flow = rim_flow_of(mobs[1], rim_adj, -0.5 * step_size, lane)
    if jumps_ready:
        zju, zjl = jumps
    for t in range(OWN):
        at = tile(t)
        gpot[:, at] = -balance(t, flows[0:4], (hx, hy), rim_flow, lane)
        ends = rim_ends(rim_adj, t)
        zau[:, at] = -step_size * jnp.where(lane == LZ - 1, ends, flows[4][:, at])
        zal[:, at] = -step_size * jnp.where(lane == 0, ends, flows[5][:, at])
        if not jumps_ready:
            ends = rim_ends(rim_jump, t)
            zju[:, at] = jnp.where(lane == LZ - 1, ends, jumps[0][:, at])
            zjl[:, at] = jnp.where(lane == 0, ends, jumps[1][:, at])

    def cell_body(i, carry):
        for t in (2 * i, 2 * i + 1):
            at = t + 8
            x, y = t // LY, t % LY
            y_low = jnp.where(y == 0, YM + x, at - 1)
            y_high = jnp.where(y == LY - 1, YP + x, at + 1)
            z = tile(t)
            pairs = (
                (adj_of(at - 8, at), jump_of(at - 8, at)),
                (adj_of(at, at + 8), jump_of(at, at + 8)),
                (adj_of(y_low, at), jump_of(y_low, at)),
                (adj_of(at, y_high), jump_of(at, y_high)),
                (zal[:, z], zjl[:, z]),
                (zau[:, z], zju[:, z]),
            )
            for k in range(NC):
                total = None
                for a, j in pairs:
                    term = a[k : k + 1, :] * j
                    total = term if total is None else total + term
                rows = slice(GRP * k, GRP * k + GRP)
                pre3[rows, z] = (total * slope[rows, z]).astype(BF16)
        return carry

    lax.fori_loop(0, OWN // 2, cell_body, 0)
    for at in range(0, OWN * LZ, CHUNK):
        own = slice(at, at + CHUNK)
        two = (dot(w3rt[...], pre3[:, own]) * slope2[:, own]).astype(BF16)
        one = (dot(w2t[...], two) * slope1[:, own]).astype(BF16)
        net = dot(w1t[...], one)
        pres12[0:HID, own] = one
        pres12[HID:, own] = two
        for k in range(CHUNK // LZ):
            t = at // LZ + k
            v = values[0:NC, tile(t + 8)]
            emit(
                t,
                adj[0:NC, tile(t + 8)]
                + gpot[0:NC, tile(t)] * (1.0 + 3.0 * cubic_coef * v * v)
                + net[:, k * LZ : (k + 1) * LZ],
            )


def weight_grads(pres, rhs, grads, room, late):
    pres12, pre3 = pres
    rhs12, rhs3 = rhs
    room[...] = jnp.zeros((2 * HID, 2 * LZ), F32)
    room[:, 0:RHS] = dot(pres12[...], rhs12[...], 1, 1)
    lane = lanes((HID, LZ))
    upper, lower = room[HID:, 0:LZ], room[0:HID, 0:LZ]
    second = jnp.where(lane < HID, upper, lower)
    second = jnp.where(lane == HID + NC + 1, pltpu.roll(upper, 1, 1), second)
    room[0:RHS, 0:ROWS] = dot(rhs3[...], pre3[...], 1, 1)
    left, right = room[0:RHS, 0:LZ], room[0:RHS, LZ:]
    lane = lanes((RHS, LZ))
    third, rest = jnp.zeros((RHS, LZ), F32), jnp.zeros((RHS, LZ), F32)
    for g in range(NC):
        source, start = (left, GRP * g) if g < 8 else (right, GRP * g - LZ)
        goal = NC * g
        if goal < LZ:
            moved = pltpu.roll(source, (goal - start) % LZ, 1)
            third = jnp.where((lane >= goal) & (lane < goal + NC), moved, third)
        if goal + NC > LZ:
            moved = pltpu.roll(source, (goal - LZ - start) % LZ, 1)
            rest = jnp.where((lane >= max(goal - LZ, 0)) & (lane < goal + NC - LZ), moved, rest)
    second = second + jnp.where(lanes((HID, LZ)) >= 80, pltpu.roll(rest[0:HID, :], 80, 1), 0.0)
    row, lane = lax.broadcasted_iota(jnp.int32, (8, LZ), 0), lanes((8, LZ))
    bias = jnp.zeros((8, LZ), F32)
    for r in range(5):
        line = pltpu.roll(third[HID : HID + 8, :] if r < 4 else rest[HID : HID + 8, :], (96 - 32 * r) % LZ, 1)
        bias = jnp.where((row == r) & (lane >= 96), line, bias)
    blocks = ((0, third[0:HID, :]), (HID, second[0:8, :] + bias), (HID + 8, second[8:, :]))
    for at, block in blocks:
        where = slice(at, at + block.shape[0])
        grads[where, :] = block if late is None else block + late[where, :]


def late_kernel(*refs):
    faces, sent_z, prep, weights, slopes = refs[0:6], refs[6:8], refs[8:12], refs[12:15], refs[18:21]
    mob, flows, jumps = refs[15], refs[21:27], refs[27:29]
    back, outs, pres, values, adj = refs[29], refs[30:36], refs[36:38], refs[38], refs[39]
    pots, rim_mob, scratch = refs[40], refs[41], refs[42:]
    load_halo(faces, sent_z, 0, 0, values)
    load_halo(faces, sent_z, 1, 1, adj)
    pots[...] = potential(values[...])
    network(values, HALO, prep, False, rim_mob)
    clear(back)

    def emit(t, block):
        back[0:NC, tile(t + 8)] = block

    reverse_step(values, pots, adj, (mob, rim_mob), slopes, weights, flows, jumps, scratch, pres, emit, False)
    pack_tiles(back, outs, 0)


def late_grads_kernel(*refs):
    weight_grads(refs[0:2], refs[2:4], refs[4], refs[5], None)


def core_rows(half):
    core = lax.axis_index("gx") % 2
    mine = pl.multiple_of(core * half, 8)
    others = pl.multiple_of((1 - core) * half, 8)
    return pl.ds(mine, half), pl.ds(others, half)


def early_kernel(values, *refs):
    faces, sent_z, weights, mobs, rhs, slopes, late = refs[0:6], refs[6:8], refs[8:11], refs[11:13], refs[13:15], refs[15:18], refs[18]
    pots, jumps, flows = refs[20], refs[21:23], refs[23:29]
    final, keep, give, adj = refs[29:33]
    near, sem, pres, room, grads, scratch = refs[33], refs[34], refs[35:37], refs[37], refs[38], refs[39:]
    load_halo(faces, sent_z, 0, 0, adj)

    def emit(t, block):
        near[pl.ds(t, NC, stride=OWN), :] = block

    scratch = (*scratch, None, None)
    reverse_step(values, pots, adj, mobs, slopes, weights, flows, jumps, scratch, pres, emit, True)
    copy = pltpu.make_async_copy(near, final, sem)
    copy.start()
    weight_grads(pres, rhs, grads, room, late)
    half = GROWS // 2
    mine, others = core_rows(half)
    keep[...] = grads[mine, :]
    give[...] = grads[others, :]
    copy.wait()


def finish_kernel(factor, own, other, ow1t, ob1, ow2, ob2, ow3t, ob3, grads):
    mine, others = core_rows(GROWS // 2)
    grads[mine, :] = own[...]
    grads[others, :] = other[...]
    second = grads[HID:, :] * factor
    ow3t[:, 0:LZ] = grads[0:HID, :] * factor
    ow3t[:, LZ:] = pltpu.roll(second, LZ - 80, 1)[:, 0:16]
    ow2[...] = second[:, 0:HID]
    turned = pltpu.roll(second, 64, 1).T
    ow1t[...] = turned[0:NC, :]
    ob1[...] = turned[NC : NC + 1, :]
    ob2[...] = turned[NC + 1 : NC + 2, :]
    row, lane = lax.broadcasted_iota(jnp.int32, (8, LZ), 0), lanes((8, LZ))
    bias = jnp.zeros((8, LZ), F32)
    for r in range(4):
        line = pltpu.roll(second[0:8, :], (32 + 32 * r) % LZ, 1)
        bias = jnp.where((row == r) & (lane >= 32 * r) & (lane < 32 * r + 32), line, bias)
    ob3[:, 0:LZ] = jnp.sum(bias, axis=0, keepdims=True)
    ob3[:, LZ:] = pltpu.roll(second[0:8, :], 32, 1)[4:5, 0:16]


def shape(*dims):
    return jax.ShapeDtypeStruct(dims, F32)


def face_shapes(parts):
    x, y, z = shape(96 * parts, LZ), shape(24 * parts, LZ), shape(GRP * parts, LZ)
    return (x, y, y, z, z, x)


def call(kernel, outs, args, scratch=(), aliases=None, far=(), far_out=()):
    return pl.pallas_call(
        kernel,
        out_shape=outs,
        in_specs=[pl.BlockSpec(memory_space=pltpu.HBM) if i in far else VM for i in range(len(args))],
        out_specs=tuple(pl.BlockSpec(memory_space=pltpu.HBM) if i in far_out else VM for i in range(len(outs))),
        scratch_shapes=list(scratch),
        input_output_aliases=aliases or {},
        compiler_params=pltpu.CompilerParams(vmem_limit_bytes=12 << 20),
    )(*args)


def wide(tiles, rows=GRP, kind=F32):
    return pltpu.VMEM((rows, tiles * LZ), kind)


def array(tiles, rows=GRP, kind=F32):
    return jax.ShapeDtypeStruct((rows, tiles * LZ), kind)


FLOWS = (wide(OWN), wide(4))
EARLY = FLOWS + (wide(OWN),) * 3
BACK = FLOWS + (wide(OWN),) * 5
OWN_FLOWS = (array(8), array(14)) + (array(OWN),) * 4
KEPT = (array(OWN, RHS, BF16), array(OWN, RHS, BF16), array(OWN, HID), array(OWN, HID), array(OWN, ROWS))
PRES = (array(OWN, 2 * HID, BF16), array(OWN, ROWS, BF16))
ROOM = pltpu.VMEM((2 * HID, 2 * LZ), F32)


def group_sum(value, partners):
    received = [swap(value, partner) for partner in partners]
    for other in received:
        value = value + other
    return value


def along_z(goal):
    def partner(a, b, c):
        z = goal[(a // 2) * 4 + b // 4]
        return (z // 4) * 2 + a % 2, (z % 4) * 4 + b % 4, c

    return partner


def total_over_devices(keep, give):
    value = keep + swap(give, lambda a, b, c: (a ^ 1, b, c))
    value = group_sum(value, [lambda a, b, c, k=k: (a, b, c ^ k) for k in (2, 1, 3)])
    value = group_sum(value, [lambda a, b, c, k=k: (a, b ^ k, c) for k in (2, 1, 3)])
    value = value + swap(value, lambda a, b, c: (a, b ^ 4, c))
    value = group_sum(value, (along_z((5, 4, 7, 6, 1, 0, 3, 2)), along_z((6, 3, 0, 5, 2, 7, 4, 1)), along_z((7, 2, 1, 4, 3, 6, 5, 0))))
    return value, swap(value, lambda a, b, c: (a ^ 1, b, c))


def shards(composition, cotangent, w1, b1, w2, b2, w3, b3):
    block = composition.shape
    comp = composition.reshape(NC * OWN, LZ)
    cot = cotangent.reshape(NC * OWN, LZ)
    w1t, w3t = w1.T, w3.T
    mob_shape = array(OWN, ROWS)

    sent = call(pack_kernel, face_shapes(1), (comp,))
    comp_faces = exchange(sent)
    comp_z = sent[3:5]
    inputs = (cot, w1t, b1.reshape(1, HID), w2, b2.reshape(1, HID), w3t, b3.reshape(1, MM))
    inputs = tuple(pltpu.with_memory_space_constraint(a, pltpu.HBM) for a in inputs)
    w1p, w1c, w2c, w2t, w3c, w3r, w3rt, cols, mob, values, adj, *rest = call(
        prepare_kernel,
        (
            jax.ShapeDtypeStruct((HID, NC), BF16),
            jax.ShapeDtypeStruct((NC, HID), BF16),
            jax.ShapeDtypeStruct((HID, HID), BF16),
            jax.ShapeDtypeStruct((HID, HID), BF16),
            jax.ShapeDtypeStruct((ROWS, HID), BF16),
            jax.ShapeDtypeStruct((ROWS, HID), BF16),
            jax.ShapeDtypeStruct((HID, ROWS), BF16),
            shape(ROWS, LZ),
            mob_shape,
            array(TILES),
            array(TILES),
        )
        + face_shapes(1)
        + OWN_FLOWS[0:4],
        (comp, *inputs),
        tuple(pltpu.VMEM(a.shape, a.dtype) for a in inputs) + (pltpu.SemaphoreType.DMA((len(inputs),)), wide(TILES), wide(OWN), wide(OWN)),
        far=range(1, 1 + len(inputs)),
    )
    cot_faces, flows = rest[:6], rest[6:]
    forward, reverse, back_weights = (w1p, w2c, w3c, cols), (w1p, w2c, w3r, cols), (w1c, w2t, w3rt)
    state, *sent, values = call(
        forward_kernel,
        (array(TILES),) + face_shapes(2) + (array(TILES),),
        (*comp_faces, *comp_z, *cot_faces, *forward, mob, values, *flows),
        (wide(TILES), wide(RIM, ROWS)) + FLOWS,
        {19: 7},
    )
    got = exchange(sent)
    mob, *kept = call(
        own_networks_kernel,
        ((mob_shape,) + KEPT) * 2 + OWN_FLOWS + (array(OWN),) * 2,
        (state, values, adj, *reverse),
        (wide(TILES),),
    )
    kept, comp_mob, comp_kept, flows = kept[:5], kept[5], kept[6:11], kept[11:]
    back, *rest = call(
        late_kernel,
        (array(TILES),) + face_shapes(1) + PRES + (array(TILES), array(TILES)),
        (*got, *sent[3:5], *reverse, *back_weights, mob, state, adj, *kept[2:], *flows),
        (wide(TILES), wide(RIM, ROWS)) + BACK,
        {16: 9, 17: 10},
    )
    sent, pres = rest[:6], rest[6:8]
    got = exchange(sent)
    (late,) = call(late_grads_kernel, (shape(GROWS, LZ),), (*pres, *kept[:2]), (ROOM,))
    comp_rim, *jumps = call(
        rim_network_kernel,
        (array(RIM, ROWS), array(TILES), array(OWN), array(OWN)) + OWN_FLOWS,
        (values, back, comp_mob, *reverse),
    )
    final, keep, give, _ = call(
        early_kernel,
        (shape(NC * OWN, LZ), shape(GROWS // 2, LZ), shape(GROWS // 2, LZ), array(TILES)),
        (values, *got, *sent[3:5], *back_weights, comp_mob, comp_rim, *comp_kept, late, back, *jumps),
        (
            pltpu.VMEM((NC * OWN, LZ), F32),
            pltpu.SemaphoreType.DMA,
            wide(OWN, 2 * HID, BF16),
            wide(OWN, ROWS, BF16),
            ROOM,
            pltpu.VMEM((GROWS, LZ), F32),
        )
        + EARLY,
        {20: 3},
        far_out=(0,),
    )
    totals = total_over_devices(keep, give)
    cells = OWN * LZ * GX * GY * GZ
    factor = 1.0 / (step_size * math.sqrt(cells))
    ow1t, ob1, ow2, ob2, ow3t, ob3 = call(
        functools.partial(finish_kernel, factor),
        (shape(NC, HID), shape(1, HID), shape(HID, HID), shape(1, HID), shape(HID, MM), shape(1, MM)),
        totals,
        (pltpu.VMEM((GROWS, LZ), F32),),
    )
    return (final.reshape(block), ow1t.T, ob1.reshape(HID), ow2, ob2.reshape(HID), ow3t.T, ob3.reshape(MM))


def solution(mesh):
    in_specs = (P(None, "gx", "gy", "gz"), P(None, "gx", "gy", "gz"), P(), P(), P(), P(), P(), P())
    out_specs = (P(None, "gx", "gy", "gz"), P(), P(), P(), P(), P(), P())
    return jax.shard_map(shards, mesh=mesh, in_specs=in_specs, out_specs=out_specs, check_vma=False)
```

```python
import functools
import math

import jax
import jax.numpy as jnp
from jax import lax
from jax.experimental import pallas as pl
from jax.experimental.pallas import tpu as pltpu
from jax.sharding import PartitionSpec as P


AXES = ("gx", "gy", "gz")
GX, GY, GZ = 4, 16, 4
step_size = 0.08
cubic_coef = 0.1
diag_scale = 0.5
off_scale = 0.04

NC, HID, MM = 12, 64, 144
LX, LY, LZ = 2, 8, 128
OWN = LX * LY
GRP = 16
ROWS = NC * GRP
YM, YP, ZT = 32, 34, 36
TILES = 37
CHUNK = 1024
RIM = 21
HALO = ((0, 8, 0), (24, 32, 8), (32, 37, 16))
RHS = HID + GRP
GROWS = 128
UNROLL = 4
F32, BF16 = jnp.float32, jnp.bfloat16
VM = pl.BlockSpec(memory_space=pltpu.VMEM)


def swap(value, partner):
    pairs = []
    for a in range(GX):
        for b in range(GY):
            for c in range(GZ):
                a2, b2, c2 = partner(a, b, c)
                pairs.append(((a * GY + b) * GZ + c, (a2 * GY + b2) * GZ + c2))
    return lax.ppermute(value, AXES, pairs)


def odd_up(i, n):
    return (i + 1) % n if i % 2 else (i - 1) % n


FACE_PARTNERS = (
    lambda a, b, c: (odd_up(a, GX), b, c),
    lambda a, b, c: (a, odd_up(b, GY), c),
    lambda a, b, c: (a, b ^ 1, c),
    lambda a, b, c: (a, b, odd_up(c, GZ)),
    lambda a, b, c: (a, b, c ^ 1),
    lambda a, b, c: (a ^ 1, b, c),
)


def exchange(faces):
    return [swap(face, partner) for face, partner in zip(faces, FACE_PARTNERS)]


def parities():
    return lax.axis_index("gx") % 2, lax.axis_index("gy") % 2, lax.axis_index("gz") % 2


def lanes(shape):
    return lax.broadcasted_iota(jnp.int32, shape, len(shape) - 1)


def tile(index):
    start = index * LZ
    return pl.ds(start if isinstance(start, int) else pl.multiple_of(start, LZ), LZ)


def pack_faces(native, outs, part):
    px, py, pz = parities()
    xf, yb, ya, zb, za, xn = outs
    for ch in range(NC):
        xf[pl.ds(part * 96 + ch * 8, 8), :] = native[pl.ds(pl.multiple_of(ch * OWN + px * LY, 8), 8), :]
        xn[pl.ds(part * 96 + ch * 8, 8), :] = native[pl.ds(pl.multiple_of(ch * OWN + (1 - px) * LY, 8), 8), :]
    first = native[pl.ds(0, 24, stride=8), :]
    last = native[pl.ds(7, 24, stride=8), :]
    ya[pl.ds(part * 24, 24), :] = jnp.where(py == 0, last, first)
    yb[pl.ds(part * 24, 24), :] = jnp.where(py == 0, first, last)
    lane = lanes((NC, LZ))
    low = jnp.zeros((NC, LZ), F32)
    high = jnp.zeros((NC, LZ), F32)
    for t in range(OWN):
        block = native[pl.ds(t, NC, stride=OWN), :]
        low = jnp.where(lane == 2 * t, pltpu.roll(block, 2 * t, 1), low)
        high = jnp.where(lane == 2 * t, pltpu.roll(block, 2 * t + 1, 1), high)
    zero = jnp.zeros((GRP - NC, LZ), F32)
    za[pl.ds(part * GRP, NC), :] = jnp.where(pz == 0, high, low)
    zb[pl.ds(part * GRP, NC), :] = jnp.where(pz == 0, low, high)
    za[pl.ds(part * GRP + NC, GRP - NC), :] = zero
    zb[pl.ds(part * GRP + NC, GRP - NC), :] = zero


def load_own(native, dest):
    dest[...] = jnp.zeros((GRP, TILES * LZ), F32)
    for t in range(OWN):
        dest[0:NC, tile(8 + t)] = native[pl.ds(t, NC, stride=OWN), :]


def load_halo(faces, sent_z, part, sent_part, dest):
    px, py, pz = parities()
    xf, yb, ya, zb, za, xn = faces
    for y in range(LY):
        dest[0:NC, tile(24 * px + y)] = xf[pl.ds(part * 96 + y, NC, stride=LY), :]
        dest[0:NC, tile(24 - 24 * px + y)] = xn[pl.ds(part * 96 + y, NC, stride=LY), :]
    for x in range(LX):
        dest[0:NC, tile(YP - 2 * py + x)] = ya[pl.ds(part * 24 + x, NC, stride=LX), :]
        dest[0:NC, tile(YM + 2 * py + x)] = yb[pl.ds(part * 24 + x, NC, stride=LX), :]
    got = slice(part * GRP, part * GRP + GRP)
    own = slice(sent_part * GRP, sent_part * GRP + GRP)
    got_a, got_b = za[got, :], zb[got, :]
    own_b, own_a = sent_z[0][own, :], sent_z[1][own, :]
    even = pz == 0
    minus, plus = jnp.where(even, got_b, got_a), jnp.where(even, got_a, got_b)
    first, last = jnp.where(even, own_b, own_a), jnp.where(even, own_a, own_b)
    rim = (pltpu.roll(minus, 1, 1) + last) + (pltpu.roll(first, 33, 1) + pltpu.roll(plus, 32, 1))
    dest[:, tile(ZT)] = rim


def pack_tiles(source, outs, part):
    px, py, pz = parities()
    xf, yb, ya, zb, za, xn = outs
    for y in range(LY):
        xf[pl.ds(part * 96 + y, NC, stride=LY), :] = source[0:NC, tile(8 + 8 * px + y)]
        xn[pl.ds(part * 96 + y, NC, stride=LY), :] = source[0:NC, tile(16 - 8 * px + y)]
    for x in range(LX):
        ya[pl.ds(part * 24 + x, NC, stride=LX), :] = source[0:NC, tile(8 + x * 8 + 7 - 7 * py)]
        yb[pl.ds(part * 24 + x, NC, stride=LX), :] = source[0:NC, tile(8 + x * 8 + 7 * py)]
    lane = lanes((GRP, LZ))
    low = jnp.zeros((GRP, LZ), F32)
    high = jnp.zeros((GRP, LZ), F32)
    for t in range(OWN):
        block = source[:, tile(8 + t)]
        low = jnp.where(lane == 2 * t, pltpu.roll(block, 2 * t, 1), low)
        high = jnp.where(lane == 2 * t, pltpu.roll(block, 2 * t + 1, 1), high)
    za[pl.ds(part * GRP, GRP), :] = jnp.where(pz == 0, high, low)
    zb[pl.ds(part * GRP, GRP), :] = jnp.where(pz == 0, low, high)


def clear(dest):
    dest[...] = jnp.zeros(dest.shape, dest.dtype)


def row_tables(by_column):
    row = lax.broadcasted_iota(jnp.int32, (ROWS, MM), 0)
    entry = lax.broadcasted_iota(jnp.int32, (ROWS, MM), 1)
    g, j = row // GRP, row % GRP
    want = j * NC + g if by_column else g * NC + j
    pick = jnp.where((entry == want) & (j < NC), 1.0, 0.0).astype(F32)
    row1 = lax.broadcasted_iota(jnp.int32, (ROWS, 1), 0)
    g1, j1 = row1 // GRP, row1 % GRP
    identity = jnp.where(g1 == j1, 1.0, 0.0).astype(F32)
    scales = jnp.where(g1 == j1, diag_scale, jnp.where(j1 < NC, off_scale, 0.0)).astype(F32)
    return pick, identity, scales


def eye(size, kind=F32):
    same = lax.broadcasted_iota(jnp.int32, (size, size), 0) == lax.broadcasted_iota(jnp.int32, (size, size), 1)
    return jnp.where(same, 1.0, 0.0).astype(kind)


def dot(a, b, ca=1, cb=0, precision=None):
    return lax.dot_general(a, b, (((ca,), (cb,)), ((), ())), preferred_element_type=F32, precision=precision)


def prepare(w1t, b1, w2, b2, w3t, b3, outs):
    w1p, w1c, w2c, w2t, w3c, w3r, w3rt, cols = outs
    w1c[...] = w1t[...]
    w2c[...] = w2[...]
    w1p[...] = dot(w1t[...], eye(NC, BF16), 0, 0).astype(BF16)
    w2t[...] = dot(w2[...], eye(HID, BF16), 0, 0).astype(BF16)
    pick_c, _, _ = row_tables(True)
    pick_r, _, _ = row_tables(False)
    w3c[...] = dot(pick_c.astype(BF16), w3t[...], 1, 1).astype(BF16)
    w3r[...] = dot(pick_r.astype(BF16), w3t[...], 1, 1).astype(BF16)
    w3rt[...] = dot(w3t[...], pick_r.astype(BF16), 1, 1).astype(BF16)
    cols[:, 0:1] = jnp.sum(pick_c * b3[...], axis=1, keepdims=True)
    cols[:, 1:2] = jnp.sum(pick_r * b3[...], axis=1, keepdims=True)
    cols[0:HID, 2:3] = jnp.sum(eye(HID) * b1[...], axis=1, keepdims=True)
    cols[0:HID, 3:4] = jnp.sum(eye(HID) * b2[...], axis=1, keepdims=True)


def network(values, spans, prep, by_column, mob, keep=None):
    w1p, w2, w3p, cols = prep
    row1 = lax.broadcasted_iota(jnp.int32, (ROWS, 1), 0)
    g1, j1 = row1 // GRP, row1 % GRP
    identity = jnp.where(g1 == j1, 1.0, 0.0).astype(F32)
    scales = jnp.where(g1 == j1, diag_scale, jnp.where(j1 < NC, off_scale, 0.0)).astype(F32)
    bias1, bias2 = cols[0:HID, 2:3], cols[0:HID, 3:4]
    bias3 = cols[:, 0:1] if by_column else cols[:, 1:2]
    places = [slice(start * LZ, stop * LZ) for start, stop, _ in spans]
    ones = [jnp.tanh(dot(w1p[...], values[0:NC, at].astype(BF16)) + bias1).astype(BF16) for at in places]
    twos = [jnp.tanh(dot(w2[...], one) + bias2).astype(BF16) for one in ones]
    for (start, stop, goal), cols_at, one, two in zip(spans, places, ones, twos):
        active = jnp.tanh(dot(w3p[...], two) + bias3)
        mob[:, goal * LZ : (goal + stop - start) * LZ] = identity + scales * active
        if keep is not None:
            own = slice(goal * LZ, (goal + stop - start) * LZ)
            rhs12, rhs3, slope1, slope2, slope = keep
            width = (stop - start) * LZ
            row = lax.broadcasted_iota(jnp.int32, (GRP, width), 0)
            rhs12[0:HID, own] = one
            rhs12[HID:, own] = jnp.where(row == NC, 1.0, values[:, cols_at]).astype(BF16)
            rhs3[0:HID, own] = two
            rhs3[HID:, own] = jnp.ones((GRP, width), BF16)
            one32, two32 = one.astype(F32), two.astype(F32)
            slope1[:, own] = 1.0 - one32 * one32
            slope2[:, own] = 1.0 - two32 * two32
            slope[:, own] = (0.5 * scales) * (1.0 - active * active)


OWN_SPANS = ((8, 16, 0), (16, 24, 8))


def potential(v):
    return v + cubic_coef * v * v * v


def flow_of(lower, upper, weight):
    total = None
    for k in range(NC):
        term = (lower(k) + upper(k)) * weight[k : k + 1, :]
        total = term if total is None else total + term
    return total


def mob_rows(mob, index):
    return lambda k: mob[GRP * k : GRP * k + GRP, tile(index)]


def product(mob, index, weight):
    total = None
    for k in range(NC):
        term = mob[GRP * k : GRP * k + GRP, tile(index)] * weight[k : k + 1, :]
        total = term if total is None else total + term
    return total


def y_face(j):
    x, k = j // 9, j % 9
    low = jnp.where(k == 0, YM + x, (x + 1) * 8 + k - 1)
    high = jnp.where(k == 8, YP + x, (x + 1) * 8 + k)
    return low, high


def step_between(source, factor):
    return lambda low, high: factor * (source[:, tile(high)] - source[:, tile(low)])


def own_flows(mob, source, factor, outs):
    fx, fy, flow_up, flow_low, step_up, step_low = outs
    weight_of = step_between(source, factor)
    for k in range(8):
        fx[:, tile(k)] = flow_of(mob_rows(mob, k), mob_rows(mob, k + 8), weight_of(k + 8, k + 16))
    for x in range(LX):
        for k in range(LY - 1):
            at = x * 8 + k
            fy[:, tile(x * 7 + k)] = flow_of(mob_rows(mob, at), mob_rows(mob, at + 1), weight_of(at + 8, at + 9))

    def z_body(i, carry):
        for k in range(8):
            t = i * 8 + k
            here = source[:, tile(t + 8)]
            up = pltpu.roll(here, LZ - 1, 1) - here
            low = pltpu.roll(up, 1, 1)
            flow = product(mob, t, factor * up) + pltpu.roll(product(mob, t, factor * low), LZ - 1, 1)
            flow_up[:, tile(t)], flow_low[:, tile(t)] = flow, pltpu.roll(flow, 1, 1)
            step_up[:, tile(t)], step_low[:, tile(t)] = up, low
        return carry

    lax.fori_loop(0, 2, z_body, 0)


def halo_flows(mobs, source, factor, fx, fy):
    own, halo = mobs
    weight_of = step_between(source, factor)
    for y in range(LY):
        fx[:, tile(y)] = flow_of(mob_rows(halo, y), mob_rows(own, y), weight_of(y, y + 8))
        fx[:, tile(y + 8)] = flow_of(mob_rows(own, y + 8), mob_rows(halo, y + 8), weight_of(y + 16, y + 24))
    for x in range(LX):
        first, last = x * 8, x * 8 + 7
        fy[:, tile(2 * x)] = flow_of(mob_rows(halo, 16 + x), mob_rows(own, first), weight_of(YM + x, first + 8))
        fy[:, tile(2 * x + 1)] = flow_of(mob_rows(own, last), mob_rows(halo, 18 + x), weight_of(last + 8, YP + x))


def rim_flow_of(mob, rim, factor, lane):
    weight = factor * rim
    share = product(mob, RIM - 1, jnp.where(lane < 32, weight, pltpu.roll(weight, 32, 1)))
    return share + pltpu.roll(share, 96, 1)


def balance(t, own, halo, rim_flow, lane):
    fx, fy, flow_up, flow_low = own
    hx, hy = halo
    x, y = t // LY, t % LY
    x_low, x_up = (hx[:, tile(y)], fx[:, tile(y)]) if x == 0 else (fx[:, tile(y)], hx[:, tile(8 + y)])
    y_low = hy[:, tile(2 * x)] if y == 0 else fy[:, tile(x * 7 + y - 1)]
    y_up = hy[:, tile(2 * x + 1)] if y == LY - 1 else fy[:, tile(x * 7 + y)]
    ends = rim_ends(rim_flow, t)
    z_up = jnp.where(lane == LZ - 1, ends, flow_up[:, tile(t)])
    z_low = jnp.where(lane == 0, ends, flow_low[:, tile(t)])
    return (x_up - x_low) + (y_up - y_low) + (z_up - z_low)


def rim_step(source):
    here = source[:, tile(ZT)]
    return pltpu.roll(here, 96, 1) - here


def rim_ends(rim, t):
    return pltpu.roll(rim, LZ - 1 - 2 * t, 1)


def z_steps(source, rim, t, lane):
    here = source[:, tile(t + 8)]
    step = pltpu.roll(here, LZ - 1, 1) - here
    ends = rim_ends(rim, t)
    up = jnp.where(lane == LZ - 1, ends, step)
    low = jnp.where(lane == 0, ends, pltpu.roll(step, 1, 1))
    return up, low


def pack_kernel(comp, *outs):
    pack_faces(comp, outs, 0)


def prepare_kernel(comp, *refs):
    far, outs = refs[0:7], refs[7:15]
    mob, values, adj, faces, flows = refs[15], refs[16], refs[17], refs[18:24], refs[24:28]
    near, sems, pots, steps = refs[28:35], refs[35], refs[36], refs[37:39]
    copies = [pltpu.make_async_copy(a, b, sems.at[i]) for i, (a, b) in enumerate(zip(far, near))]
    for copy in copies:
        copy.start()
    clear(values)
    clear(adj)
    for t in range(OWN):
        values[0:NC, tile(8 + t)] = comp[pl.ds(t, NC, stride=OWN), :]
    for copy in copies:
        copy.wait()
    cot, w1t, b1, w2, b2, w3t, b3 = near
    prepare(w1t, b1, w2, b2, w3t, b3, outs)
    network(values, OWN_SPANS, (outs[0], w2, outs[4], outs[7]), True, mob)
    for t in range(OWN):
        adj[0:NC, tile(8 + t)] = cot[pl.ds(t, NC, stride=OWN), :]
    pack_tiles(adj, faces, 0)
    own = slice(8 * LZ, 24 * LZ)
    pots[:, own] = potential(values[:, own])
    own_flows(mob, pots, 0.5, (*flows, *steps))


def forward_kernel(*refs):
    faces, sent_z, cot_faces, prep = refs[0:6], refs[6:8], refs[8:14], refs[14:18]
    mob, flows, state, outs, values = refs[18], refs[20:24], refs[24], refs[25:31], refs[31]
    pots, rim_mob, hx, hy = refs[32:]
    load_halo(faces, sent_z, 0, 0, values)
    pots[...] = potential(values[...])
    network(values, HALO, prep, True, rim_mob)
    halo_flows((mob, rim_mob), pots, 0.5, hx, hy)
    lane = lanes((GRP, LZ))
    rim_flow = rim_flow_of(rim_mob, rim_step(pots), 0.5, lane)
    clear(state)
    for t in range(OWN):
        at = t + 8
        state[:, tile(at)] = values[:, tile(at)] + step_size * balance(t, flows, (hx, hy), rim_flow, lane)
    pack_tiles(state, outs, 0)
    for out, face in zip(outs, cot_faces):
        out[pl.ds(face.shape[0], face.shape[0]), :] = face[...]


def own_network_kernel(state, adj, w1p, w2, w3r, cols, *refs):
    outs, flows, jumps = refs[0:6], refs[6:12], refs[12:14]
    network(state, OWN_SPANS, (w1p, w2, w3r, cols), False, outs[0], outs[1:6])
    own_flows(outs[0], adj, -0.5 * step_size, flows)
    for t in range(OWN):
        here = potential(state[:, tile(t + 8)])
        step = pltpu.roll(here, LZ - 1, 1) - here
        jumps[0][:, tile(t)], jumps[1][:, tile(t)] = step, pltpu.roll(step, 1, 1)


def comp_network_kernel(values, back, w1p, w2, w3r, cols, *refs):
    outs, pots, jumps, steps = refs[0:6], refs[6], refs[7:9], refs[9:11]
    network(values, OWN_SPANS, (w1p, w2, w3r, cols), False, outs[0], outs[1:6])
    pots[...] = potential(values[...])
    lane = lanes((GRP, LZ))
    rim = rim_step(pots)
    for t in range(OWN):
        jumps[0][:, tile(t)], jumps[1][:, tile(t)] = z_steps(pots, rim, t, lane)
        here = back[:, tile(t + 8)]
        step = pltpu.roll(here, LZ - 1, 1) - here
        steps[0][:, tile(t)], steps[1][:, tile(t)] = step, pltpu.roll(step, 1, 1)


def outgoing(t, values, adj, gpot, net):
    v = values[0:NC, tile(t + 8)]
    return adj[0:NC, tile(t + 8)] + gpot[0:NC] * (1.0 + 3.0 * cubic_coef * v * v) + net


def reverse_layers(pots, adj, slopes, weights, steps, jumps, scratch, pres, take, jumps_ready):
    w1t, w2t, w3rt = weights
    slope1, slope2, slope = slopes
    pres12, pre3 = pres
    zau, zal, zju, zjl = scratch

    def jump_of(low, high):
        return pots[:, tile(high)] - pots[:, tile(low)]

    def adj_of(low, high):
        return step_size * (adj[:, tile(low)] - adj[:, tile(high)])

    lane = lanes((GRP, LZ))
    rim_jump, rim_adj = None if jumps_ready else rim_step(pots), rim_step(adj)
    if jumps_ready:
        zju, zjl = jumps
    for t in range(OWN):
        at = tile(t)
        ends = rim_ends(rim_adj, t)
        zau[:, at] = -step_size * jnp.where(lane == LZ - 1, ends, steps[0][:, at])
        zal[:, at] = -step_size * jnp.where(lane == 0, ends, steps[1][:, at])
        if not jumps_ready:
            ends = rim_ends(rim_jump, t)
            zju[:, at] = jnp.where(lane == LZ - 1, ends, jumps[0][:, at])
            zjl[:, at] = jnp.where(lane == 0, ends, jumps[1][:, at])

    def cell_body(i, carry):
        for t in (2 * i, 2 * i + 1):
            at = t + 8
            x, y = t // LY, t % LY
            y_low = jnp.where(y == 0, YM + x, at - 1)
            y_high = jnp.where(y == LY - 1, YP + x, at + 1)
            z = tile(t)
            pairs = (
                (adj_of(at - 8, at), jump_of(at - 8, at)),
                (adj_of(at, at + 8), jump_of(at, at + 8)),
                (adj_of(y_low, at), jump_of(y_low, at)),
                (adj_of(at, y_high), jump_of(at, y_high)),
                (zal[:, z], zjl[:, z]),
                (zau[:, z], zju[:, z]),
            )
            for k in range(NC):
                total = None
                for a, j in pairs:
                    term = a[k : k + 1, :] * j
                    total = term if total is None else total + term
                rows = slice(GRP * k, GRP * k + GRP)
                pre3[rows, z] = (total * slope[rows, z]).astype(BF16)
        return carry

    lax.fori_loop(0, OWN // 2, cell_body, 0)
    for at in range(0, OWN * LZ, CHUNK):
        own = slice(at, at + CHUNK)
        two = (dot(w3rt[...], pre3[:, own]) * slope2[:, own]).astype(BF16)
        one = (dot(w2t[...], two) * slope1[:, own]).astype(BF16)
        net = dot(w1t[...], one)
        pres12[0:HID, own] = one
        pres12[HID:, own] = two
        for k in range(CHUNK // LZ):
            t = at // LZ + k
            take(t, net[:, k * LZ : (k + 1) * LZ])


def weight_grads(pres, rhs, grads, room, late):
    pres12, pre3 = pres
    rhs12, rhs3 = rhs
    room[...] = jnp.zeros((2 * HID, 2 * LZ), F32)
    room[:, 0:RHS] = dot(pres12[...], rhs12[...], 1, 1)
    lane = lanes((HID, LZ))
    upper, lower = room[HID:, 0:LZ], room[0:HID, 0:LZ]
    second = jnp.where(lane < HID, upper, lower)
    second = jnp.where(lane == HID + NC + 1, pltpu.roll(upper, 1, 1), second)
    room[0:RHS, 0:ROWS] = dot(rhs3[...], pre3[...], 1, 1)
    left, right = room[0:RHS, 0:LZ], room[0:RHS, LZ:]
    lane = lanes((RHS, LZ))
    third, rest = jnp.zeros((RHS, LZ), F32), jnp.zeros((RHS, LZ), F32)
    for g in range(NC):
        source, start = (left, GRP * g) if g < 8 else (right, GRP * g - LZ)
        goal = NC * g
        if goal < LZ:
            moved = pltpu.roll(source, (goal - start) % LZ, 1)
            third = jnp.where((lane >= goal) & (lane < goal + NC), moved, third)
        if goal + NC > LZ:
            moved = pltpu.roll(source, (goal - LZ - start) % LZ, 1)
            rest = jnp.where((lane >= max(goal - LZ, 0)) & (lane < goal + NC - LZ), moved, rest)
    second = second + jnp.where(lanes((HID, LZ)) >= 80, pltpu.roll(rest[0:HID, :], 80, 1), 0.0)
    row, lane = lax.broadcasted_iota(jnp.int32, (8, LZ), 0), lanes((8, LZ))
    bias = jnp.zeros((8, LZ), F32)
    for r in range(5):
        line = pltpu.roll(third[HID : HID + 8, :] if r < 4 else rest[HID : HID + 8, :], (96 - 32 * r) % LZ, 1)
        bias = jnp.where((row == r) & (lane >= 96), line, bias)
    blocks = ((0, third[0:HID, :]), (HID, second[0:8, :] + bias), (HID + 8, second[8:, :]))
    for at, block in blocks:
        where = slice(at, at + block.shape[0])
        grads[where, :] = block if late is None else block + late[where, :]


def late_kernel(*refs):
    faces, sent_z, prep, weights, slopes = refs[0:6], refs[6:8], refs[8:12], refs[12:15], refs[18:21]
    mob, flows, jumps = refs[15], refs[21:27], refs[27:29]
    back, outs, pres, values, adj = refs[29], refs[30:36], refs[36:38], refs[38], refs[39]
    pots, rim_mob, scratch = refs[40], refs[41], refs[42:]
    load_halo(faces, sent_z, 0, 0, values)
    load_halo(faces, sent_z, 1, 1, adj)
    pots[...] = potential(values[...])
    network(values, HALO, prep, False, rim_mob)
    clear(back)

    hx, hy, gpot = scratch[0:3]
    halo_flows((mob, rim_mob), adj, -0.5 * step_size, hx, hy)
    lane = lanes((GRP, LZ))
    rim_flow = rim_flow_of(rim_mob, rim_step(adj), -0.5 * step_size, lane)
    for t in range(OWN):
        gpot[:, tile(t)] = -balance(t, flows[0:4], (hx, hy), rim_flow, lane)

    def take(t, net):
        back[0:NC, tile(t + 8)] = outgoing(t, values, adj, gpot[:, tile(t)], net)

    reverse_layers(pots, adj, slopes, weights, flows[4:6], jumps, scratch[3:], pres, take, False)
    pack_tiles(back, outs, 0)


def late_grads_kernel(*refs):
    weight_grads(refs[0:2], refs[2:4], refs[4], refs[5], None)


def core_rows(half):
    core = lax.axis_index("gx") % 2
    mine = pl.multiple_of(core * half, 8)
    others = pl.multiple_of((1 - core) * half, 8)
    return pl.ds(mine, half), pl.ds(others, half)


def early_kernel(*refs):
    faces, sent_z, weights, rhs, slopes, late = refs[0:6], refs[6:8], refs[8:11], refs[11:13], refs[13:16], refs[16]
    pots, jumps, steps = refs[18], refs[19:21], refs[21:23]
    net_out, keep, give, adj = refs[23:27]
    pres, room, grads, zau, zal = refs[27:29], refs[29], refs[30], refs[31], refs[32]
    load_halo(faces, sent_z, 0, 0, adj)

    def take(t, net):
        net_out[0:NC, tile(t)] = net

    reverse_layers(pots, adj, slopes, weights, steps, jumps, (zau, zal, None, None), pres, take, True)
    weight_grads(pres, rhs, grads, room, late)
    half = GROWS // 2
    mine, others = core_rows(half)
    keep[...] = grads[mine, :]
    give[...] = grads[others, :]


def final_kernel(values, adj, own_mob, net, w1p, w2, w3r, cols, after, final, *scratch):
    rim_mob, flows, hx, hy = scratch[0], scratch[1:7], scratch[7], scratch[8]
    network(values, HALO, (w1p, w2, w3r, cols), False, rim_mob)
    own_flows(own_mob, adj, -0.5 * step_size, flows)
    halo_flows((own_mob, rim_mob), adj, -0.5 * step_size, hx, hy)
    lane = lanes((GRP, LZ))
    rim_flow = rim_flow_of(rim_mob, rim_step(adj), -0.5 * step_size, lane)
    for t in range(OWN):
        gpot = -balance(t, flows[0:4], (hx, hy), rim_flow, lane)
        final[pl.ds(t, NC, stride=OWN), :] = outgoing(t, values, adj, gpot, net[0:NC, tile(t)])


def finish_kernel(factor, own, other, ow1t, ob1, ow2, ob2, ow3t, ob3, grads):
    mine, others = core_rows(GROWS // 2)
    grads[mine, :] = own[...]
    grads[others, :] = other[...]
    second = grads[HID:, :] * factor
    ow3t[:, 0:LZ] = grads[0:HID, :] * factor
    ow3t[:, LZ:] = pltpu.roll(second, LZ - 80, 1)[:, 0:16]
    ow2[...] = second[:, 0:HID]
    turned = pltpu.roll(second, 64, 1).T
    ow1t[...] = turned[0:NC, :]
    ob1[...] = turned[NC : NC + 1, :]
    ob2[...] = turned[NC + 1 : NC + 2, :]
    row, lane = lax.broadcasted_iota(jnp.int32, (8, LZ), 0), lanes((8, LZ))
    bias = jnp.zeros((8, LZ), F32)
    for r in range(4):
        line = pltpu.roll(second[0:8, :], (32 + 32 * r) % LZ, 1)
        bias = jnp.where((row == r) & (lane >= 32 * r) & (lane < 32 * r + 32), line, bias)
    ob3[:, 0:LZ] = jnp.sum(bias, axis=0, keepdims=True)
    ob3[:, LZ:] = pltpu.roll(second[0:8, :], 32, 1)[4:5, 0:16]


def shape(*dims):
    return jax.ShapeDtypeStruct(dims, F32)


def face_shapes(parts):
    x, y, z = shape(96 * parts, LZ), shape(24 * parts, LZ), shape(GRP * parts, LZ)
    return (x, y, y, z, z, x)


def call(kernel, outs, args, scratch=(), aliases=None, far=(), far_out=()):
    return pl.pallas_call(
        kernel,
        out_shape=outs,
        in_specs=[pl.BlockSpec(memory_space=pltpu.HBM) if i in far else VM for i in range(len(args))],
        out_specs=tuple(pl.BlockSpec(memory_space=pltpu.HBM) if i in far_out else VM for i in range(len(outs))),
        scratch_shapes=list(scratch),
        input_output_aliases=aliases or {},
        compiler_params=pltpu.CompilerParams(vmem_limit_bytes=12 << 20),
    )(*args)


def wide(tiles, rows=GRP, kind=F32):
    return pltpu.VMEM((rows, tiles * LZ), kind)


def array(tiles, rows=GRP, kind=F32):
    return jax.ShapeDtypeStruct((rows, tiles * LZ), kind)


FLOWS = (wide(OWN), wide(4))
BACK = FLOWS + (wide(OWN),) * 5
OWN_FLOWS = (array(8), array(14)) + (array(OWN),) * 4
KEPT = (array(OWN, RHS, BF16), array(OWN, RHS, BF16), array(OWN, HID), array(OWN, HID), array(OWN, ROWS))
PRES = (array(OWN, 2 * HID, BF16), array(OWN, ROWS, BF16))
ROOM = pltpu.VMEM((2 * HID, 2 * LZ), F32)


def group_sum(value, partners):
    received = [swap(value, partner) for partner in partners]
    for other in received:
        value = value + other
    return value


def along_z(goal):
    def partner(a, b, c):
        z = goal[(a // 2) * 4 + b // 4]
        return (z // 4) * 2 + a % 2, (z % 4) * 4 + b % 4, c

    return partner


def total_over_devices(keep, give, beside):
    value = keep + swap(give, lambda a, b, c: (a ^ 1, b, c))
    value = group_sum(value, [lambda a, b, c, k=k: (a, b, c ^ k) for k in (2, 1, 3)])
    value = group_sum(value, [lambda a, b, c, k=k: (a, b ^ k, c) for k in (2, 1, 3)])
    other = swap(value, lambda a, b, c: (a, b ^ 4, c))
    value, made = lax.optimization_barrier((value + other, beside(value)))
    value = group_sum(value, (along_z((5, 4, 7, 6, 1, 0, 3, 2)), along_z((6, 3, 0, 5, 2, 7, 4, 1)), along_z((7, 2, 1, 4, 3, 6, 5, 0))))
    return value, swap(value, lambda a, b, c: (a ^ 1, b, c)), made


def shards(composition, cotangent, w1, b1, w2, b2, w3, b3):
    block = composition.shape
    comp = composition.reshape(NC * OWN, LZ)
    cot = cotangent.reshape(NC * OWN, LZ)
    w1t, w3t = w1.T, w3.T
    mob_shape = array(OWN, ROWS)

    sent = call(pack_kernel, face_shapes(1), (comp,))
    comp_faces = exchange(sent)
    comp_z = sent[3:5]
    inputs = (cot, w1t, b1.reshape(1, HID), w2, b2.reshape(1, HID), w3t, b3.reshape(1, MM))
    inputs = tuple(pltpu.with_memory_space_constraint(a, pltpu.HBM) for a in inputs)
    w1p, w1c, w2c, w2t, w3c, w3r, w3rt, cols, mob, values, adj, *rest = call(
        prepare_kernel,
        (
            jax.ShapeDtypeStruct((HID, NC), BF16),
            jax.ShapeDtypeStruct((NC, HID), BF16),
            jax.ShapeDtypeStruct((HID, HID), BF16),
            jax.ShapeDtypeStruct((HID, HID), BF16),
            jax.ShapeDtypeStruct((ROWS, HID), BF16),
            jax.ShapeDtypeStruct((ROWS, HID), BF16),
            jax.ShapeDtypeStruct((HID, ROWS), BF16),
            shape(ROWS, LZ),
            mob_shape,
            array(TILES),
            array(TILES),
        )
        + face_shapes(1)
        + OWN_FLOWS[0:4],
        (comp, *inputs),
        tuple(pltpu.VMEM(a.shape, a.dtype) for a in inputs) + (pltpu.SemaphoreType.DMA((len(inputs),)), wide(TILES), wide(OWN), wide(OWN)),
        far=range(1, 1 + len(inputs)),
    )
    cot_faces, flows = rest[:6], rest[6:]
    forward, reverse, back_weights = (w1p, w2c, w3c, cols), (w1p, w2c, w3r, cols), (w1c, w2t, w3rt)
    state, *sent, values = call(
        forward_kernel,
        (array(TILES),) + face_shapes(2) + (array(TILES),),
        (*comp_faces, *comp_z, *cot_faces, *forward, mob, values, *flows),
        (wide(TILES), wide(RIM, ROWS)) + FLOWS,
        {19: 7},
    )
    got = exchange(sent)
    mob, *kept = call(
        own_network_kernel,
        (mob_shape,) + KEPT + OWN_FLOWS + (array(OWN),) * 2,
        (state, adj, *reverse),
    )
    kept, flows = kept[:5], kept[5:]
    back, *rest = call(
        late_kernel,
        (array(TILES),) + face_shapes(1) + PRES + (array(TILES), array(TILES)),
        (*got, *sent[3:5], *reverse, *back_weights, mob, state, adj, *kept[2:], *flows),
        (wide(TILES), wide(RIM, ROWS)) + BACK,
        {16: 9, 17: 10},
    )
    sent, pres = rest[:6], rest[6:8]
    got = exchange(sent)
    (late,) = call(late_grads_kernel, (shape(GROWS, LZ),), (*pres, *kept[:2]), (ROOM,))
    comp_mob, *rest = call(
        comp_network_kernel,
        (mob_shape,) + KEPT + (array(TILES),) + (array(OWN),) * 4,
        (values, back, *reverse),
    )
    comp_kept, steps = rest[:5], rest[5:]
    net, keep, give, adj = call(
        early_kernel,
        (array(OWN), shape(GROWS // 2, LZ), shape(GROWS // 2, LZ), array(TILES)),
        (*got, *sent[3:5], *back_weights, *comp_kept, late, back, *steps),
        (
            wide(OWN, 2 * HID, BF16),
            wide(OWN, ROWS, BF16),
            ROOM,
            pltpu.VMEM((GROWS, LZ), F32),
            wide(OWN),
            wide(OWN),
        ),
        {17: 3},
    )
    def final_gradient(after):
        return call(
            final_kernel,
            (shape(NC * OWN, LZ),),
            (values, adj, comp_mob, net, *reverse, after),
            (wide(RIM, ROWS), wide(8), wide(14)) + (wide(OWN),) * 4 + FLOWS,
        )[0]

    *totals, final = total_over_devices(keep, give, final_gradient)
    cells = OWN * LZ * GX * GY * GZ
    factor = 1.0 / (step_size * math.sqrt(cells))
    ow1t, ob1, ow2, ob2, ow3t, ob3 = call(
        functools.partial(finish_kernel, factor),
        (shape(NC, HID), shape(1, HID), shape(HID, HID), shape(1, HID), shape(HID, MM), shape(1, MM)),
        totals,
        (pltpu.VMEM((GROWS, LZ), F32),),
    )
    return (final.reshape(block), ow1t.T, ob1.reshape(HID), ow2, ob2.reshape(HID), ow3t.T, ob3.reshape(MM))


def solution(mesh):
    in_specs = (P(None, "gx", "gy", "gz"), P(None, "gx", "gy", "gz"), P(), P(), P(), P(), P(), P())
    out_specs = (P(None, "gx", "gy", "gz"), P(), P(), P(), P(), P(), P())
    return jax.shard_map(shards, mesh=mesh, in_specs=in_specs, out_specs=out_specs, check_vma=False)
```

```python
import functools
import math

import jax
import jax.numpy as jnp
from jax import lax
from jax.experimental import pallas as pl
from jax.experimental.pallas import tpu as pltpu
from jax.sharding import PartitionSpec as P


AXES = ("gx", "gy", "gz")
GX, GY, GZ = 4, 16, 4
step_size = 0.08
cubic_coef = 0.1
diag_scale = 0.5
off_scale = 0.04

NC, HID, MM = 12, 64, 144
LX, LY, LZ = 2, 8, 128
OWN = LX * LY
GRP = 16
ROWS = NC * GRP
YM, YP, ZT = 32, 34, 36
TILES = 37
CHUNK = 1024
RIM = 21
HALO = ((0, 8, 0), (24, 32, 8), (32, 37, 16))
RHS = HID + GRP
GROWS = 128
UNROLL = 4
F32, BF16 = jnp.float32, jnp.bfloat16
VM = pl.BlockSpec(memory_space=pltpu.VMEM)


def swap(value, partner):
    pairs = []
    for a in range(GX):
        for b in range(GY):
            for c in range(GZ):
                a2, b2, c2 = partner(a, b, c)
                pairs.append(((a * GY + b) * GZ + c, (a2 * GY + b2) * GZ + c2))
    return lax.ppermute(value, AXES, pairs)


def odd_up(i, n):
    return (i + 1) % n if i % 2 else (i - 1) % n


FACE_PARTNERS = (
    lambda a, b, c: (odd_up(a, GX), b, c),
    lambda a, b, c: (a, odd_up(b, GY), c),
    lambda a, b, c: (a, b ^ 1, c),
    lambda a, b, c: (a, b, odd_up(c, GZ)),
    lambda a, b, c: (a, b, c ^ 1),
    lambda a, b, c: (a ^ 1, b, c),
)


def exchange(faces):
    return [swap(face, partner) for face, partner in zip(faces, FACE_PARTNERS)]


def parities():
    return lax.axis_index("gx") % 2, lax.axis_index("gy") % 2, lax.axis_index("gz") % 2


def lanes(shape):
    return lax.broadcasted_iota(jnp.int32, shape, len(shape) - 1)


def tile(index):
    start = index * LZ
    return pl.ds(start if isinstance(start, int) else pl.multiple_of(start, LZ), LZ)


def pack_faces(native, outs, part):
    px, py, pz = parities()
    xf, yb, ya, zb, za, xn = outs
    for ch in range(NC):
        xf[pl.ds(part * 96 + ch * 8, 8), :] = native[pl.ds(pl.multiple_of(ch * OWN + px * LY, 8), 8), :]
        xn[pl.ds(part * 96 + ch * 8, 8), :] = native[pl.ds(pl.multiple_of(ch * OWN + (1 - px) * LY, 8), 8), :]
    first = native[pl.ds(0, 24, stride=8), :]
    last = native[pl.ds(7, 24, stride=8), :]
    ya[pl.ds(part * 24, 24), :] = jnp.where(py == 0, last, first)
    yb[pl.ds(part * 24, 24), :] = jnp.where(py == 0, first, last)
    lane = lanes((NC, LZ))
    low = jnp.zeros((NC, LZ), F32)
    high = jnp.zeros((NC, LZ), F32)
    for t in range(OWN):
        block = native[pl.ds(t, NC, stride=OWN), :]
        low = jnp.where(lane == 2 * t, pltpu.roll(block, 2 * t, 1), low)
        high = jnp.where(lane == 2 * t, pltpu.roll(block, 2 * t + 1, 1), high)
    zero = jnp.zeros((GRP - NC, LZ), F32)
    za[pl.ds(part * GRP, NC), :] = jnp.where(pz == 0, high, low)
    zb[pl.ds(part * GRP, NC), :] = jnp.where(pz == 0, low, high)
    za[pl.ds(part * GRP + NC, GRP - NC), :] = zero
    zb[pl.ds(part * GRP + NC, GRP - NC), :] = zero


def load_own(native, dest):
    dest[...] = jnp.zeros((GRP, TILES * LZ), F32)
    for t in range(OWN):
        dest[0:NC, tile(8 + t)] = native[pl.ds(t, NC, stride=OWN), :]


def load_halo(faces, sent_z, part, sent_part, dest):
    px, py, pz = parities()
    xf, yb, ya, zb, za, xn = faces
    for y in range(LY):
        dest[0:NC, tile(24 * px + y)] = xf[pl.ds(part * 96 + y, NC, stride=LY), :]
        dest[0:NC, tile(24 - 24 * px + y)] = xn[pl.ds(part * 96 + y, NC, stride=LY), :]
    for x in range(LX):
        dest[0:NC, tile(YP - 2 * py + x)] = ya[pl.ds(part * 24 + x, NC, stride=LX), :]
        dest[0:NC, tile(YM + 2 * py + x)] = yb[pl.ds(part * 24 + x, NC, stride=LX), :]
    got = slice(part * GRP, part * GRP + GRP)
    own = slice(sent_part * GRP, sent_part * GRP + GRP)
    got_a, got_b = za[got, :], zb[got, :]
    own_b, own_a = sent_z[0][own, :], sent_z[1][own, :]
    even = pz == 0
    minus, plus = jnp.where(even, got_b, got_a), jnp.where(even, got_a, got_b)
    first, last = jnp.where(even, own_b, own_a), jnp.where(even, own_a, own_b)
    rim = (pltpu.roll(minus, 1, 1) + last) + (pltpu.roll(first, 33, 1) + pltpu.roll(plus, 32, 1))
    dest[:, tile(ZT)] = rim


def pack_tiles(source, outs, part):
    px, py, pz = parities()
    xf, yb, ya, zb, za, xn = outs
    for y in range(LY):
        xf[pl.ds(part * 96 + y, NC, stride=LY), :] = source[0:NC, tile(8 + 8 * px + y)]
        xn[pl.ds(part * 96 + y, NC, stride=LY), :] = source[0:NC, tile(16 - 8 * px + y)]
    for x in range(LX):
        ya[pl.ds(part * 24 + x, NC, stride=LX), :] = source[0:NC, tile(8 + x * 8 + 7 - 7 * py)]
        yb[pl.ds(part * 24 + x, NC, stride=LX), :] = source[0:NC, tile(8 + x * 8 + 7 * py)]
    lane = lanes((GRP, LZ))
    low = jnp.zeros((GRP, LZ), F32)
    high = jnp.zeros((GRP, LZ), F32)
    for t in range(OWN):
        block = source[:, tile(8 + t)]
        low = jnp.where(lane == 2 * t, pltpu.roll(block, 2 * t, 1), low)
        high = jnp.where(lane == 2 * t, pltpu.roll(block, 2 * t + 1, 1), high)
    za[pl.ds(part * GRP, GRP), :] = jnp.where(pz == 0, high, low)
    zb[pl.ds(part * GRP, GRP), :] = jnp.where(pz == 0, low, high)


def clear(dest):
    dest[...] = jnp.zeros(dest.shape, dest.dtype)


def row_tables(by_column):
    row = lax.broadcasted_iota(jnp.int32, (ROWS, MM), 0)
    entry = lax.broadcasted_iota(jnp.int32, (ROWS, MM), 1)
    g, j = row // GRP, row % GRP
    want = j * NC + g if by_column else g * NC + j
    pick = jnp.where((entry == want) & (j < NC), 1.0, 0.0).astype(F32)
    row1 = lax.broadcasted_iota(jnp.int32, (ROWS, 1), 0)
    g1, j1 = row1 // GRP, row1 % GRP
    identity = jnp.where(g1 == j1, 1.0, 0.0).astype(F32)
    scales = jnp.where(g1 == j1, diag_scale, jnp.where(j1 < NC, off_scale, 0.0)).astype(F32)
    return pick, identity, scales


def eye(size, kind=F32):
    same = lax.broadcasted_iota(jnp.int32, (size, size), 0) == lax.broadcasted_iota(jnp.int32, (size, size), 1)
    return jnp.where(same, 1.0, 0.0).astype(kind)


def dot(a, b, ca=1, cb=0, precision=None):
    return lax.dot_general(a, b, (((ca,), (cb,)), ((), ())), preferred_element_type=F32, precision=precision)


def prepare(w1t, b1, w2, b2, w3t, b3, outs):
    w1p, w1c, w2c, w2t, w3c, w3r, w3rt, cols = outs
    w1c[...] = w1t[...]
    w2c[...] = w2[...]
    w1p[...] = dot(w1t[...], eye(NC, BF16), 0, 0).astype(BF16)
    w2t[...] = dot(w2[...], eye(HID, BF16), 0, 0).astype(BF16)
    pick_c, _, _ = row_tables(True)
    pick_r, _, _ = row_tables(False)
    w3c[...] = dot(pick_c.astype(BF16), w3t[...], 1, 1).astype(BF16)
    w3r[...] = dot(pick_r.astype(BF16), w3t[...], 1, 1).astype(BF16)
    w3rt[...] = dot(w3t[...], pick_r.astype(BF16), 1, 1).astype(BF16)
    cols[:, 0:1] = jnp.sum(pick_c * b3[...], axis=1, keepdims=True)
    cols[:, 1:2] = jnp.sum(pick_r * b3[...], axis=1, keepdims=True)
    cols[0:HID, 2:3] = jnp.sum(eye(HID) * b1[...], axis=1, keepdims=True)
    cols[0:HID, 3:4] = jnp.sum(eye(HID) * b2[...], axis=1, keepdims=True)


def network(values, spans, prep, by_column, mob, keep=None):
    w1p, w2, w3p, cols = prep
    row1 = lax.broadcasted_iota(jnp.int32, (ROWS, 1), 0)
    g1, j1 = row1 // GRP, row1 % GRP
    identity = jnp.where(g1 == j1, 1.0, 0.0).astype(F32)
    scales = jnp.where(g1 == j1, diag_scale, jnp.where(j1 < NC, off_scale, 0.0)).astype(F32)
    bias1, bias2 = cols[0:HID, 2:3], cols[0:HID, 3:4]
    bias3 = cols[:, 0:1] if by_column else cols[:, 1:2]
    places = [slice(start * LZ, stop * LZ) for start, stop, _ in spans]
    ones = [jnp.tanh(dot(w1p[...], values[0:NC, at].astype(BF16)) + bias1).astype(BF16) for at in places]
    twos = [jnp.tanh(dot(w2[...], one) + bias2).astype(BF16) for one in ones]
    for (start, stop, goal), cols_at, one, two in zip(spans, places, ones, twos):
        active = jnp.tanh(dot(w3p[...], two) + bias3)
        mob[:, goal * LZ : (goal + stop - start) * LZ] = identity + scales * active
        if keep is not None:
            own = slice(goal * LZ, (goal + stop - start) * LZ)
            rhs12, rhs3, slope1, slope2, slope = keep
            width = (stop - start) * LZ
            row = lax.broadcasted_iota(jnp.int32, (GRP, width), 0)
            rhs12[0:HID, own] = one
            rhs12[HID:, own] = jnp.where(row == NC, 1.0, values[:, cols_at]).astype(BF16)
            rhs3[0:HID, own] = two
            rhs3[HID:, own] = jnp.ones((GRP, width), BF16)
            one32, two32 = one.astype(F32), two.astype(F32)
            slope1[:, own] = 1.0 - one32 * one32
            slope2[:, own] = 1.0 - two32 * two32
            slope[:, own] = (0.5 * scales) * (1.0 - active * active)


OWN_SPANS = ((8, 16, 0), (16, 24, 8))


def potential(v):
    return v + cubic_coef * v * v * v


def flow_of(lower, upper, weight):
    total = None
    for k in range(NC):
        term = (lower(k) + upper(k)) * weight[k : k + 1, :]
        total = term if total is None else total + term
    return total


def mob_rows(mob, index):
    return lambda k: mob[GRP * k : GRP * k + GRP, tile(index)]


def product(mob, index, weight):
    total = None
    for k in range(NC):
        term = mob[GRP * k : GRP * k + GRP, tile(index)] * weight[k : k + 1, :]
        total = term if total is None else total + term
    return total


def y_face(j):
    x, k = j // 9, j % 9
    low = jnp.where(k == 0, YM + x, (x + 1) * 8 + k - 1)
    high = jnp.where(k == 8, YP + x, (x + 1) * 8 + k)
    return low, high


def step_between(source, factor):
    return lambda low, high: factor * (source[:, tile(high)] - source[:, tile(low)])


def own_flows(mob, source, factor, outs):
    fx, fy, flow_up, flow_low, step_up, step_low = outs
    weight_of = step_between(source, factor)
    for k in range(8):
        fx[:, tile(k)] = flow_of(mob_rows(mob, k), mob_rows(mob, k + 8), weight_of(k + 8, k + 16))
    for x in range(LX):
        for k in range(LY - 1):
            at = x * 8 + k
            fy[:, tile(x * 7 + k)] = flow_of(mob_rows(mob, at), mob_rows(mob, at + 1), weight_of(at + 8, at + 9))

    def z_body(i, carry):
        for k in range(8):
            t = i * 8 + k
            here = source[:, tile(t + 8)]
            up = pltpu.roll(here, LZ - 1, 1) - here
            low = pltpu.roll(up, 1, 1)
            flow = product(mob, t, factor * up) + pltpu.roll(product(mob, t, factor * low), LZ - 1, 1)
            flow_up[:, tile(t)], flow_low[:, tile(t)] = flow, pltpu.roll(flow, 1, 1)
            step_up[:, tile(t)], step_low[:, tile(t)] = up, low
        return carry

    lax.fori_loop(0, 2, z_body, 0)


def halo_flows(mobs, source, factor, fx, fy):
    own, halo = mobs
    weight_of = step_between(source, factor)
    for y in range(LY):
        fx[:, tile(y)] = flow_of(mob_rows(halo, y), mob_rows(own, y), weight_of(y, y + 8))
        fx[:, tile(y + 8)] = flow_of(mob_rows(own, y + 8), mob_rows(halo, y + 8), weight_of(y + 16, y + 24))
    for x in range(LX):
        first, last = x * 8, x * 8 + 7
        fy[:, tile(2 * x)] = flow_of(mob_rows(halo, 16 + x), mob_rows(own, first), weight_of(YM + x, first + 8))
        fy[:, tile(2 * x + 1)] = flow_of(mob_rows(own, last), mob_rows(halo, 18 + x), weight_of(last + 8, YP + x))


def rim_flow_of(mob, rim, factor, lane):
    weight = factor * rim
    share = product(mob, RIM - 1, jnp.where(lane < 32, weight, pltpu.roll(weight, 32, 1)))
    return share + pltpu.roll(share, 96, 1)


def balance(t, own, halo, rim_flow, lane):
    fx, fy, flow_up, flow_low = own
    hx, hy = halo
    x, y = t // LY, t % LY
    x_low, x_up = (hx[:, tile(y)], fx[:, tile(y)]) if x == 0 else (fx[:, tile(y)], hx[:, tile(8 + y)])
    y_low = hy[:, tile(2 * x)] if y == 0 else fy[:, tile(x * 7 + y - 1)]
    y_up = hy[:, tile(2 * x + 1)] if y == LY - 1 else fy[:, tile(x * 7 + y)]
    ends = rim_ends(rim_flow, t)
    z_up = jnp.where(lane == LZ - 1, ends, flow_up[:, tile(t)])
    z_low = jnp.where(lane == 0, ends, flow_low[:, tile(t)])
    return (x_up - x_low) + (y_up - y_low) + (z_up - z_low)


def rim_step(source):
    here = source[:, tile(ZT)]
    return pltpu.roll(here, 96, 1) - here


def rim_ends(rim, t):
    return pltpu.roll(rim, LZ - 1 - 2 * t, 1)


def z_steps(source, rim, t, lane):
    here = source[:, tile(t + 8)]
    step = pltpu.roll(here, LZ - 1, 1) - here
    ends = rim_ends(rim, t)
    up = jnp.where(lane == LZ - 1, ends, step)
    low = jnp.where(lane == 0, ends, pltpu.roll(step, 1, 1))
    return up, low


def pack_kernel(comp, *outs):
    pack_faces(comp, outs, 0)


def prepare_kernel(comp, *refs):
    far, outs = refs[0:7], refs[7:15]
    mob, values, adj, faces, flows = refs[15], refs[16], refs[17], refs[18:24], refs[24:28]
    near, sems, pots, steps = refs[28:35], refs[35], refs[36], refs[37:39]
    copies = [pltpu.make_async_copy(a, b, sems.at[i]) for i, (a, b) in enumerate(zip(far, near))]
    for copy in copies:
        copy.start()
    clear(values)
    clear(adj)
    for t in range(OWN):
        values[0:NC, tile(8 + t)] = comp[pl.ds(t, NC, stride=OWN), :]
    for copy in copies:
        copy.wait()
    cot, w1t, b1, w2, b2, w3t, b3 = near
    prepare(w1t, b1, w2, b2, w3t, b3, outs)
    network(values, OWN_SPANS, (outs[0], w2, outs[4], outs[7]), True, mob)
    for t in range(OWN):
        adj[0:NC, tile(8 + t)] = cot[pl.ds(t, NC, stride=OWN), :]
    pack_tiles(adj, faces, 0)
    own = slice(8 * LZ, 24 * LZ)
    pots[:, own] = potential(values[:, own])
    own_flows(mob, pots, 0.5, (*flows, *steps))


def forward_kernel(*refs):
    faces, sent_z, cot_faces, prep = refs[0:6], refs[6:8], refs[8:14], refs[14:18]
    mob, flows, state, outs, values = refs[18], refs[20:24], refs[24], refs[25:31], refs[31]
    pots, rim_mob, hx, hy = refs[32:]
    load_halo(faces, sent_z, 0, 0, values)
    pots[...] = potential(values[...])
    network(values, HALO, prep, True, rim_mob)
    halo_flows((mob, rim_mob), pots, 0.5, hx, hy)
    lane = lanes((GRP, LZ))
    rim_flow = rim_flow_of(rim_mob, rim_step(pots), 0.5, lane)
    clear(state)
    for t in range(OWN):
        at = t + 8
        state[:, tile(at)] = values[:, tile(at)] + step_size * balance(t, flows, (hx, hy), rim_flow, lane)
    pack_tiles(state, outs, 0)
    for out, face in zip(outs, cot_faces):
        out[pl.ds(face.shape[0], face.shape[0]), :] = face[...]


def own_network_kernel(state, adj, w1p, w2, w3r, cols, *refs):
    outs, flows, jumps = refs[0:6], refs[6:12], refs[12:14]
    network(state, OWN_SPANS, (w1p, w2, w3r, cols), False, outs[0], outs[1:6])
    own_flows(outs[0], adj, -0.5 * step_size, flows)
    for t in range(OWN):
        here = potential(state[:, tile(t + 8)])
        step = pltpu.roll(here, LZ - 1, 1) - here
        jumps[0][:, tile(t)], jumps[1][:, tile(t)] = step, pltpu.roll(step, 1, 1)


def comp_network_kernel(values, back, w1p, w2, w3r, cols, *refs):
    outs, pots, jumps, steps = refs[0:6], refs[6], refs[7:9], refs[9:11]
    network(values, OWN_SPANS, (w1p, w2, w3r, cols), False, outs[0], outs[1:6])
    pots[...] = potential(values[...])
    lane = lanes((GRP, LZ))
    rim = rim_step(pots)
    for t in range(OWN):
        jumps[0][:, tile(t)], jumps[1][:, tile(t)] = z_steps(pots, rim, t, lane)
        here = back[:, tile(t + 8)]
        step = pltpu.roll(here, LZ - 1, 1) - here
        steps[0][:, tile(t)], steps[1][:, tile(t)] = step, pltpu.roll(step, 1, 1)


def outgoing(t, values, adj, gpot, net):
    v = values[0:NC, tile(t + 8)]
    return adj[0:NC, tile(t + 8)] + gpot[0:NC] * (1.0 + 3.0 * cubic_coef * v * v) + net


def reverse_layers(pots, adj, slopes, weights, steps, jumps, scratch, pres, take, jumps_ready):
    w1t, w2t, w3rt = weights
    slope1, slope2, slope = slopes
    pres12, pre3 = pres
    zau, zal, zju, zjl = scratch

    def jump_of(low, high):
        return pots[:, tile(high)] - pots[:, tile(low)]

    def adj_of(low, high):
        return step_size * (adj[:, tile(low)] - adj[:, tile(high)])

    lane = lanes((GRP, LZ))
    rim_jump, rim_adj = None if jumps_ready else rim_step(pots), rim_step(adj)
    if jumps_ready:
        zju, zjl = jumps
    for t in range(OWN):
        at = tile(t)
        ends = rim_ends(rim_adj, t)
        zau[:, at] = -step_size * jnp.where(lane == LZ - 1, ends, steps[0][:, at])
        zal[:, at] = -step_size * jnp.where(lane == 0, ends, steps[1][:, at])
        if not jumps_ready:
            ends = rim_ends(rim_jump, t)
            zju[:, at] = jnp.where(lane == LZ - 1, ends, jumps[0][:, at])
            zjl[:, at] = jnp.where(lane == 0, ends, jumps[1][:, at])

    def cell_body(i, carry):
        for t in (2 * i, 2 * i + 1):
            at = t + 8
            x, y = t // LY, t % LY
            y_low = jnp.where(y == 0, YM + x, at - 1)
            y_high = jnp.where(y == LY - 1, YP + x, at + 1)
            z = tile(t)
            pairs = (
                (adj_of(at - 8, at), jump_of(at - 8, at)),
                (adj_of(at, at + 8), jump_of(at, at + 8)),
                (adj_of(y_low, at), jump_of(y_low, at)),
                (adj_of(at, y_high), jump_of(at, y_high)),
                (zal[:, z], zjl[:, z]),
                (zau[:, z], zju[:, z]),
            )
            for k in range(NC):
                total = None
                for a, j in pairs:
                    term = a[k : k + 1, :] * j
                    total = term if total is None else total + term
                rows = slice(GRP * k, GRP * k + GRP)
                pre3[rows, z] = (total * slope[rows, z]).astype(BF16)
        return carry

    lax.fori_loop(0, OWN // 2, cell_body, 0)
    for at in range(0, OWN * LZ, CHUNK):
        own = slice(at, at + CHUNK)
        two = (dot(w3rt[...], pre3[:, own]) * slope2[:, own]).astype(BF16)
        one = (dot(w2t[...], two) * slope1[:, own]).astype(BF16)
        net = dot(w1t[...], one)
        pres12[0:HID, own] = one
        pres12[HID:, own] = two
        for k in range(CHUNK // LZ):
            t = at // LZ + k
            take(t, net[:, k * LZ : (k + 1) * LZ])


def weight_grads(pres, rhs, grads, room, late):
    pres12, pre3 = pres
    rhs12, rhs3 = rhs
    room[...] = jnp.zeros((2 * HID, 2 * LZ), F32)
    room[:, 0:RHS] = dot(pres12[...], rhs12[...], 1, 1)
    lane = lanes((HID, LZ))
    upper, lower = room[HID:, 0:LZ], room[0:HID, 0:LZ]
    second = jnp.where(lane < HID, upper, lower)
    second = jnp.where(lane == HID + NC + 1, pltpu.roll(upper, 1, 1), second)
    room[0:RHS, 0:ROWS] = dot(rhs3[...], pre3[...], 1, 1)
    left, right = room[0:RHS, 0:LZ], room[0:RHS, LZ:]
    lane = lanes((RHS, LZ))
    third, rest = jnp.zeros((RHS, LZ), F32), jnp.zeros((RHS, LZ), F32)
    for g in range(NC):
        source, start = (left, GRP * g) if g < 8 else (right, GRP * g - LZ)
        goal = NC * g
        if goal < LZ:
            moved = pltpu.roll(source, (goal - start) % LZ, 1)
            third = jnp.where((lane >= goal) & (lane < goal + NC), moved, third)
        if goal + NC > LZ:
            moved = pltpu.roll(source, (goal - LZ - start) % LZ, 1)
            rest = jnp.where((lane >= max(goal - LZ, 0)) & (lane < goal + NC - LZ), moved, rest)
    second = second + jnp.where(lanes((HID, LZ)) >= 80, pltpu.roll(rest[0:HID, :], 80, 1), 0.0)
    row, lane = lax.broadcasted_iota(jnp.int32, (8, LZ), 0), lanes((8, LZ))
    bias = jnp.zeros((8, LZ), F32)
    for r in range(5):
        line = pltpu.roll(third[HID : HID + 8, :] if r < 4 else rest[HID : HID + 8, :], (96 - 32 * r) % LZ, 1)
        bias = jnp.where((row == r) & (lane >= 96), line, bias)
    blocks = ((0, third[0:HID, :]), (HID, second[0:8, :] + bias), (HID + 8, second[8:, :]))
    for at, block in blocks:
        where = slice(at, at + block.shape[0])
        grads[where, :] = block if late is None else block + late[where, :]


def late_kernel(*refs):
    faces, sent_z, prep, weights, slopes = refs[0:6], refs[6:8], refs[8:12], refs[12:15], refs[18:21]
    mob, flows, jumps = refs[15], refs[21:27], refs[27:29]
    back, outs, pres, values, adj = refs[29], refs[30:36], refs[36:38], refs[38], refs[39]
    pots, rim_mob, scratch = refs[40], refs[41], refs[42:]
    load_halo(faces, sent_z, 0, 0, values)
    load_halo(faces, sent_z, 1, 1, adj)
    pots[...] = potential(values[...])
    network(values, HALO, prep, False, rim_mob)
    clear(back)

    hx, hy, gpot = scratch[0:3]
    halo_flows((mob, rim_mob), adj, -0.5 * step_size, hx, hy)
    lane = lanes((GRP, LZ))
    rim_flow = rim_flow_of(rim_mob, rim_step(adj), -0.5 * step_size, lane)
    for t in range(OWN):
        gpot[:, tile(t)] = -balance(t, flows[0:4], (hx, hy), rim_flow, lane)

    def take(t, net):
        back[0:NC, tile(t + 8)] = outgoing(t, values, adj, gpot[:, tile(t)], net)

    reverse_layers(pots, adj, slopes, weights, flows[4:6], jumps, scratch[3:], pres, take, False)
    pack_tiles(back, outs, 0)


def late_grads_kernel(*refs):
    weight_grads(refs[0:2], refs[2:4], refs[4], refs[5], None)


def core_rows(half):
    core = lax.axis_index("gx") % 2
    mine = pl.multiple_of(core * half, 8)
    others = pl.multiple_of((1 - core) * half, 8)
    return pl.ds(mine, half), pl.ds(others, half)


def early_kernel(*refs):
    faces, sent_z, weights, rhs, slopes, late = refs[0:6], refs[6:8], refs[8:11], refs[11:13], refs[13:16], refs[16]
    pots, jumps, steps = refs[18], refs[19:21], refs[21:23]
    net_out, keep, give, adj = refs[23:27]
    pres, room, grads, zau, zal = refs[27:29], refs[29], refs[30], refs[31], refs[32]
    load_halo(faces, sent_z, 0, 0, adj)

    def take(t, net):
        net_out[0:NC, tile(t)] = net

    reverse_layers(pots, adj, slopes, weights, steps, jumps, (zau, zal, None, None), pres, take, True)
    weight_grads(pres, rhs, grads, room, late)
    half = GROWS // 2
    mine, others = core_rows(half)
    keep[...] = grads[mine, :]
    give[...] = grads[others, :]


def flows_kernel(values, adj, own_mob, w1p, w2, w3r, cols, after, rim_mob, *refs):
    network(values, HALO, (w1p, w2, w3r, cols), False, rim_mob)
    own_flows(own_mob, adj, -0.5 * step_size, refs)


def final_kernel(values, adj, own_mob, net, rim_mob, fx, fy, flow_up, flow_low, after, final, hx, hy):
    halo_flows((own_mob, rim_mob), adj, -0.5 * step_size, hx, hy)
    lane = lanes((GRP, LZ))
    rim_flow = rim_flow_of(rim_mob, rim_step(adj), -0.5 * step_size, lane)
    for t in range(OWN):
        gpot = -balance(t, (fx, fy, flow_up, flow_low), (hx, hy), rim_flow, lane)
        final[pl.ds(t, NC, stride=OWN), :] = outgoing(t, values, adj, gpot, net[0:NC, tile(t)])


def finish_kernel(factor, own, other, ow1t, ob1, ow2, ob2, ow3t, ob3, grads):
    mine, others = core_rows(GROWS // 2)
    grads[mine, :] = own[...]
    grads[others, :] = other[...]
    second = grads[HID:, :] * factor
    ow3t[:, 0:LZ] = grads[0:HID, :] * factor
    ow3t[:, LZ:] = pltpu.roll(second, LZ - 80, 1)[:, 0:16]
    ow2[...] = second[:, 0:HID]
    turned = pltpu.roll(second, 64, 1).T
    ow1t[...] = turned[0:NC, :]
    ob1[...] = turned[NC : NC + 1, :]
    ob2[...] = turned[NC + 1 : NC + 2, :]
    row, lane = lax.broadcasted_iota(jnp.int32, (8, LZ), 0), lanes((8, LZ))
    bias = jnp.zeros((8, LZ), F32)
    for r in range(4):
        line = pltpu.roll(second[0:8, :], (32 + 32 * r) % LZ, 1)
        bias = jnp.where((row == r) & (lane >= 32 * r) & (lane < 32 * r + 32), line, bias)
    ob3[:, 0:LZ] = jnp.sum(bias, axis=0, keepdims=True)
    ob3[:, LZ:] = pltpu.roll(second[0:8, :], 32, 1)[4:5, 0:16]


def shape(*dims):
    return jax.ShapeDtypeStruct(dims, F32)


def face_shapes(parts):
    x, y, z = shape(96 * parts, LZ), shape(24 * parts, LZ), shape(GRP * parts, LZ)
    return (x, y, y, z, z, x)


def call(kernel, outs, args, scratch=(), aliases=None, far=(), far_out=()):
    return pl.pallas_call(
        kernel,
        out_shape=outs,
        in_specs=[pl.BlockSpec(memory_space=pltpu.HBM) if i in far else VM for i in range(len(args))],
        out_specs=tuple(pl.BlockSpec(memory_space=pltpu.HBM) if i in far_out else VM for i in range(len(outs))),
        scratch_shapes=list(scratch),
        input_output_aliases=aliases or {},
        compiler_params=pltpu.CompilerParams(vmem_limit_bytes=12 << 20),
    )(*args)


def wide(tiles, rows=GRP, kind=F32):
    return pltpu.VMEM((rows, tiles * LZ), kind)


def array(tiles, rows=GRP, kind=F32):
    return jax.ShapeDtypeStruct((rows, tiles * LZ), kind)


FLOWS = (wide(OWN), wide(4))
BACK = FLOWS + (wide(OWN),) * 5
OWN_FLOWS = (array(8), array(14)) + (array(OWN),) * 4
KEPT = (array(OWN, RHS, BF16), array(OWN, RHS, BF16), array(OWN, HID), array(OWN, HID), array(OWN, ROWS))
PRES = (array(OWN, 2 * HID, BF16), array(OWN, ROWS, BF16))
ROOM = pltpu.VMEM((2 * HID, 2 * LZ), F32)


def group_sum(value, partners):
    received = [swap(value, partner) for partner in partners]
    for other in received:
        value = value + other
    return value


def along_z(goal):
    def partner(a, b, c):
        z = goal[(a // 2) * 4 + b // 4]
        return (z // 4) * 2 + a % 2, (z % 4) * 4 + b % 4, c

    return partner


def total_over_devices(keep, give, beside_y, beside_z):
    value = keep + swap(give, lambda a, b, c: (a ^ 1, b, c))
    value = group_sum(value, [lambda a, b, c, k=k: (a, b, c ^ k) for k in (2, 1, 3)])
    summed = group_sum(value, [lambda a, b, c, k=k: (a, b ^ k, c) for k in (2, 1, 3)])
    value, flows = lax.optimization_barrier((summed, beside_y(value)))
    other = swap(value, lambda a, b, c: (a, b ^ 4, c))
    value, made = lax.optimization_barrier((value + other, beside_z(value, flows)))
    value = group_sum(value, (along_z((5, 4, 7, 6, 1, 0, 3, 2)), along_z((6, 3, 0, 5, 2, 7, 4, 1)), along_z((7, 2, 1, 4, 3, 6, 5, 0))))
    return value, swap(value, lambda a, b, c: (a ^ 1, b, c)), made


def shards(composition, cotangent, w1, b1, w2, b2, w3, b3):
    block = composition.shape
    comp = composition.reshape(NC * OWN, LZ)
    cot = cotangent.reshape(NC * OWN, LZ)
    w1t, w3t = w1.T, w3.T
    mob_shape = array(OWN, ROWS)

    sent = call(pack_kernel, face_shapes(1), (comp,))
    comp_faces = exchange(sent)
    comp_z = sent[3:5]
    inputs = (cot, w1t, b1.reshape(1, HID), w2, b2.reshape(1, HID), w3t, b3.reshape(1, MM))
    inputs = tuple(pltpu.with_memory_space_constraint(a, pltpu.HBM) for a in inputs)
    w1p, w1c, w2c, w2t, w3c, w3r, w3rt, cols, mob, values, adj, *rest = call(
        prepare_kernel,
        (
            jax.ShapeDtypeStruct((HID, NC), BF16),
            jax.ShapeDtypeStruct((NC, HID), BF16),
            jax.ShapeDtypeStruct((HID, HID), BF16),
            jax.ShapeDtypeStruct((HID, HID), BF16),
            jax.ShapeDtypeStruct((ROWS, HID), BF16),
            jax.ShapeDtypeStruct((ROWS, HID), BF16),
            jax.ShapeDtypeStruct((HID, ROWS), BF16),
            shape(ROWS, LZ),
            mob_shape,
            array(TILES),
            array(TILES),
        )
        + face_shapes(1)
        + OWN_FLOWS[0:4],
        (comp, *inputs),
        tuple(pltpu.VMEM(a.shape, a.dtype) for a in inputs) + (pltpu.SemaphoreType.DMA((len(inputs),)), wide(TILES), wide(OWN), wide(OWN)),
        far=range(1, 1 + len(inputs)),
    )
    cot_faces, flows = rest[:6], rest[6:]
    forward, reverse, back_weights = (w1p, w2c, w3c, cols), (w1p, w2c, w3r, cols), (w1c, w2t, w3rt)
    state, *sent, values = call(
        forward_kernel,
        (array(TILES),) + face_shapes(2) + (array(TILES),),
        (*comp_faces, *comp_z, *cot_faces, *forward, mob, values, *flows),
        (wide(TILES), wide(RIM, ROWS)) + FLOWS,
        {19: 7},
    )
    got = exchange(sent)
    mob, *kept = call(
        own_network_kernel,
        (mob_shape,) + KEPT + OWN_FLOWS + (array(OWN),) * 2,
        (state, adj, *reverse),
    )
    kept, flows = kept[:5], kept[5:]
    back, *rest = call(
        late_kernel,
        (array(TILES),) + face_shapes(1) + PRES + (array(TILES), array(TILES)),
        (*got, *sent[3:5], *reverse, *back_weights, mob, state, adj, *kept[2:], *flows),
        (wide(TILES), wide(RIM, ROWS)) + BACK,
        {16: 9, 17: 10},
    )
    sent, pres = rest[:6], rest[6:8]
    got = exchange(sent)
    (late,) = call(late_grads_kernel, (shape(GROWS, LZ),), (*pres, *kept[:2]), (ROOM,))
    comp_mob, *rest = call(
        comp_network_kernel,
        (mob_shape,) + KEPT + (array(TILES),) + (array(OWN),) * 4,
        (values, back, *reverse),
    )
    comp_kept, steps = rest[:5], rest[5:]
    net, keep, give, adj = call(
        early_kernel,
        (array(OWN), shape(GROWS // 2, LZ), shape(GROWS // 2, LZ), array(TILES)),
        (*got, *sent[3:5], *back_weights, *comp_kept, late, back, *steps),
        (
            wide(OWN, 2 * HID, BF16),
            wide(OWN, ROWS, BF16),
            ROOM,
            pltpu.VMEM((GROWS, LZ), F32),
            wide(OWN),
            wide(OWN),
        ),
        {17: 3},
    )
    def own_part(after):
        outs = (array(RIM, ROWS),) + OWN_FLOWS[0:4]
        return call(flows_kernel, outs, (values, adj, comp_mob, *reverse, after), (wide(OWN), wide(OWN)))

    def final_gradient(after, flows):
        return call(final_kernel, (shape(NC * OWN, LZ),), (values, adj, comp_mob, net, *flows, after), FLOWS)[0]

    *totals, final = total_over_devices(keep, give, own_part, final_gradient)
    cells = OWN * LZ * GX * GY * GZ
    factor = 1.0 / (step_size * math.sqrt(cells))
    ow1t, ob1, ow2, ob2, ow3t, ob3 = call(
        functools.partial(finish_kernel, factor),
        (shape(NC, HID), shape(1, HID), shape(HID, HID), shape(1, HID), shape(HID, MM), shape(1, MM)),
        totals,
        (pltpu.VMEM((GROWS, LZ), F32),),
    )
    return (final.reshape(block), ow1t.T, ob1.reshape(HID), ow2, ob2.reshape(HID), ow3t.T, ob3.reshape(MM))


def solution(mesh):
    in_specs = (P(None, "gx", "gy", "gz"), P(None, "gx", "gy", "gz"), P(), P(), P(), P(), P(), P())
    out_specs = (P(None, "gx", "gy", "gz"), P(), P(), P(), P(), P(), P())
    return jax.shard_map(shards, mesh=mesh, in_specs=in_specs, out_specs=out_specs, check_vma=False)
```
